32 devices in a mesh: dp: 8 (over z, x), tensor: 4 (over y, core).
Axes of the slice: x: 2, y: 2, z: 4, core: 2. Of those that a mesh axis runs over, the one named last changes fastest.
Arguments:
- images: bfloat16 [64, 576, 768], P(('dp', 'tensor')), may hold values from -6 to 6
- keep_mask: int32 [64, 576], P(('dp', 'tensor')), may hold values from 0 to 1, as said below
- ln1_gain: float32 [768], replicated, may hold values from 0.25 to 1.75
- ln1_bias: float32 [768], replicated, may hold values from -1.75 to 1.75
- qkv_weight: bfloat16 [768, 2304], replicated, may hold values from -0.3125 to 0.3125
- qkv_bias: float32 [2304], replicated, may hold values from -1.75 to 1.75
- frequencies: float32 [2, 12, 32], replicated, may hold values from -1 to 1
- proj_weight: bfloat16 [768, 768], replicated, may hold values from -1.75 to 1.75
- proj_bias: float32 [768], replicated, may hold values from -1.75 to 1.75
- ln2_gain: float32 [768], replicated, may hold values from 0.25 to 1.75
- ln2_bias: float32 [768], replicated, may hold values from -1.75 to 1.75
- fc1_weight: bfloat16 [768, 3072], P(None, 'tensor'), may hold values from -0.21875 to 0.21875
- fc1_bias: bfloat16 [3072], P('tensor'), may hold values from -1.75 to 1.75
- fc2_weight: bfloat16 [3072, 768], P('tensor'), may hold values from -0.109375 to 0.109375
- fc2_bias: float32 [768], replicated, may hold values from -1.75 to 1.75
- out_grad: bfloat16 [64, 576, 768], P(('dp', 'tensor')), may hold values from -6 to 6
Outputs:
- block_out: bfloat16 [64, 576, 768], P(('dp', 'tensor'))
- input_grad: bfloat16 [64, 576, 768], P(('dp', 'tensor'))
- ln1_gain_grad: float32 [768], replicated
- ln1_bias_grad: float32 [768], replicated
- qkv_weight_grad: float32 [768, 2304], replicated
- qkv_bias_grad: float32 [2304], replicated
- freq_grad: float32 [2, 12, 32], replicated
- proj_weight_grad: float32 [768, 768], replicated
- proj_bias_grad: float32 [768], replicated
- ln2_gain_grad: float32 [768], replicated
- ln2_bias_grad: float32 [768], replicated
- fc1_weight_grad: float32 [768, 3072], P(None, 'tensor')
- fc1_bias_grad: float32 [3072], P('tensor')
- fc2_weight_grad: float32 [3072, 768], P('tensor')
- fc2_bias_grad: float32 [768], replicated
- freq_norm: float32 [], replicated
- rest_norm: float32 [], replicated
The draws below stay inside these ranges and needn't reach their ends.
Inputs may be any that keep to these rules, and one draw needn't show every extreme that they name: `keep_mask`: every image keeps at least 96 of its 576 slots; the number kept varies widely from image to image.
All inputs are finite; a program needn't handle non-finite values.
Results may differ from the reference program's by a relative error of at most 0.015.
The reference program's roundings to bfloat16 on the way count: a program that leaves them out, or rounds other values in their place, can miss the bound.
Values may be sent and summed in bfloat16 or wider, within the bound.
No kernel may reach another device: no remote copies, remote signals or barrier semaphores. Data moves between devices by JAX's collectives and lax.ppermute only.
A program may use at most 192 MiB of HBM per device.

```python
import math
import jax
import jax.numpy as jnp
from jax import lax

D = 768
HEADS = 12
HEAD = 64
FF = 3072
GRID = 24
HALF = 32
SLOTS = 576
IMAGES = 64


def draw_keep_mask(key, part):
    key_count, key_order = jax.random.split(jax.random.fold_in(key, 17))
    divisor = jax.random.randint(key_count, (IMAGES, 1), 1, 7)
    kept_count = SLOTS // divisor
    order_scores = jax.random.randint(key_order, (IMAGES, SLOTS), 0, 4096) * SLOTS + jnp.arange(SLOTS)[None, :]
    ranks = jnp.argsort(jnp.argsort(order_scores, axis=1), axis=1)
    return (ranks < kept_count).astype(jnp.int32)


def block_scale(key, dims, cuts, smallest, largest):
    factor_of, own = 1.0, jax.random.fold_in(key, 6)
    for axis_at, parts in cuts:
        heights = jnp.exp(jax.random.uniform(jax.random.fold_in(own, axis_at), (parts,), jnp.float32, smallest / len(cuts), largest / len(cuts)))
        factor_of = factor_of * jnp.repeat(heights, dims[axis_at] // parts).reshape([-1 if axis == axis_at else 1 for axis in range(len(dims))])
    return factor_of


def scatter_about(own_key, extent, deviation, reach, shards=(), dtype=jnp.bfloat16):
    level = block_scale(own_key, extent, shards, -0.22, 0.18) if shards else 1.0
    entries = jax.random.normal(own_key, extent, jnp.float32) * deviation * level
    return jnp.minimum(jnp.maximum(entries, -reach), reach).astype(dtype)


def setup_inputs(seed: int = 0) -> dict:
    streams_of = jax.random.split(jax.random.key(seed), 17)
    images = scatter_about(streams_of[0], (IMAGES, SLOTS, D), 1.0, 6.0, ((0, 32),))
    keep_mask = draw_keep_mask(jax.random.fold_in(streams_of[16], 71), 0)
    ln1_gain = jnp.clip(1.0 + 0.15 * jax.random.normal(streams_of[2], (D,), jnp.float32), 0.25, 1.75)
    ln1_bias = scatter_about(streams_of[3], (D,), 0.3, 1.75, (), jnp.float32)
    qkv_weight = scatter_about(streams_of[4], (D, 3 * D), (D // 2) ** -0.5, 0.3125)
    qkv_bias = scatter_about(streams_of[5], (3 * D,), 0.3, 1.75, (), jnp.float32)
    frequencies = jnp.clip(jax.random.uniform(streams_of[6], (2, HEADS, HALF), jnp.float32, -1.0, 1.0), -1.0, 1.0)
    proj_weight = scatter_about(streams_of[7], (D, D), (D // 64) ** -0.5, 1.75)
    proj_bias = scatter_about(streams_of[8], (D,), 0.3, 1.75, (), jnp.float32)
    ln2_gain = jnp.clip(1.0 + 0.15 * jax.random.normal(streams_of[9], (D,), jnp.float32), 0.25, 1.75)
    ln2_bias = scatter_about(streams_of[10], (D,), 0.3, 1.75, (), jnp.float32)
    fc1_weight = scatter_about(streams_of[11], (D, FF), D ** -0.5, 0.21875, ((1, 4),))
    fc1_bias = scatter_about(streams_of[12], (FF,), 0.3, 1.75, ((0, 4),))
    fc2_weight = scatter_about(streams_of[13], (FF, D), FF ** -0.5, 0.109375, ((0, 4),))
    fc2_bias = scatter_about(streams_of[14], (D,), 0.3, 1.75, (), jnp.float32)
    out_grad = scatter_about(streams_of[15], (IMAGES, SLOTS, D), 1.0, 6.0, ((0, 32),))
    return dict(images=images, keep_mask=keep_mask, ln1_gain=ln1_gain, ln1_bias=ln1_bias, qkv_weight=qkv_weight, qkv_bias=qkv_bias, frequencies=frequencies, proj_weight=proj_weight, proj_bias=proj_bias, ln2_gain=ln2_gain, ln2_bias=ln2_bias, fc1_weight=fc1_weight, fc1_bias=fc1_bias, fc2_weight=fc2_weight, fc2_bias=fc2_bias, out_grad=out_grad)


@jax.custom_vjp
def low(v):
    return lax.optimization_barrier(v.astype(jnp.bfloat16)).astype(jnp.float32)

@jax.custom_vjp
def low_back(v):
    return v

def low_keep(v):
    return (low(v), None)

def low_pass(kept, grad):
    return (grad,)

def back_keep(v):
    return (v, None)

def back_low(kept, grad):
    return (low(grad),)
low.defvjp(low_keep, low_pass)
low_back.defvjp(back_keep, back_low)
HIGHEST = lax.Precision.HIGHEST
EPSILON = 1e-06

def matmul(left, right):
    return jnp.dot(left, right, precision=HIGHEST, preferred_element_type=jnp.float32)

def layer_norm(values, gain, shift):
    row_mean = lax.optimization_barrier(jnp.mean(values, axis=-1, keepdims=True))
    centred = values - row_mean
    variance = lax.optimization_barrier(jnp.mean(centred * centred, axis=-1, keepdims=True))
    return centred * lax.rsqrt(variance + EPSILON) * gain + shift

def rotate(tensor, cosine, sine):
    first_half = tensor[..., :HALF]
    second_half = tensor[..., HALF:]
    return jnp.concatenate([first_half * cosine - second_half * sine, first_half * sine + second_half * cosine], axis=-1)

def forward(params, images, kept):
    ln1_gain, ln1_bias, qkv_weight, qkv_bias, frequencies, proj_weight, proj_bias, ln2_gain, ln2_bias, fc1_weight, fc1_bias, fc2_weight, fc2_bias = params
    image_count = images.shape[0]
    row_data = images.reshape(image_count * SLOTS, D)
    normed = low(layer_norm(row_data, ln1_gain, ln1_bias))
    packed = low_back(matmul(normed, qkv_weight) + qkv_bias).reshape(image_count, SLOTS, 3, HEADS, HEAD)
    place = jnp.arange(SLOTS)
    across = (place // GRID).astype(jnp.float32)
    downward = (place % GRID).astype(jnp.float32)
    angle = across[:, None, None] * frequencies[0][None] + downward[:, None, None] * frequencies[1][None]
    cosine = jnp.cos(angle)
    sine = jnp.sin(angle)
    queries = low(rotate(packed[:, :, 0], cosine, sine))
    key_rows = low(rotate(packed[:, :, 1], cosine, sine))
    values = low(packed[:, :, 2])
    score_scale = 1.0 / math.sqrt(HEAD)
    scores = jnp.einsum('nqhd,nkhd->nhqk', queries, key_rows, precision=HIGHEST) * score_scale
    scores = low_back(jnp.where(kept[:, None, None, :] > 0, scores, -1e+30))
    weights = low(jax.nn.softmax(scores, axis=-1))
    mixed = low_back(low(jnp.einsum('nhqk,nkhd->nqhd', weights, values, precision=HIGHEST)))
    mixed = mixed.reshape(image_count * SLOTS, D)
    branch = low_back(matmul(mixed, proj_weight) + proj_bias)
    resid = row_data + branch
    second = low(layer_norm(resid, ln2_gain, ln2_bias))
    hidden = low_back(matmul(second, fc1_weight) + fc1_bias)
    active = low(jax.nn.gelu(hidden, approximate=False))
    mlp_out = low_back(matmul(active, fc2_weight))
    result = kept.reshape(-1, 1) * (resid + mlp_out + fc2_bias)
    return result.reshape(image_count, SLOTS, D)

def reference(images, keep_mask, ln1_gain, ln1_bias, qkv_weight, qkv_bias, frequencies, proj_weight, proj_bias, ln2_gain, ln2_bias, fc1_weight, fc1_bias, fc2_weight, fc2_bias, out_grad):
    params = tuple((p.astype(jnp.float32) for p in (ln1_gain, ln1_bias, qkv_weight, qkv_bias, frequencies, proj_weight, proj_bias, ln2_gain, ln2_bias, fc1_weight, fc1_bias, fc2_weight, fc2_bias)))
    group_inputs = images.astype(jnp.float32).reshape(-1, 4, SLOTS, D)
    group_kept = keep_mask.astype(jnp.float32).reshape(-1, 4, SLOTS)
    group_cot = out_grad.astype(jnp.float32).reshape(-1, 4, SLOTS, D)

    def step_group(totals, block_item):
        inputs, kept, cotangent = block_item
        result, pullback = jax.vjp(lambda p, v: forward(p, v, kept), params, inputs)
        param_grads, input_grads = pullback(cotangent)
        totals = jax.tree.map(jnp.add, totals, param_grads)
        return (totals, (result, input_grads))
    zeros = jax.tree.map(jnp.zeros_like, params)
    grads, (results, input_grads) = lax.scan(step_group, zeros, (group_inputs, group_kept, group_cot))
    block_out = results.reshape(IMAGES, SLOTS, D).astype(jnp.bfloat16)
    input_grad = input_grads.reshape(IMAGES, SLOTS, D).astype(jnp.bfloat16)
    freq_grad = grads[4]
    freq_norm = jnp.sqrt(jnp.sum(freq_grad * freq_grad))
    rest_square = jnp.float32(0.0)
    for position in (0, 1, 2, 3, 5, 6, 7, 8, 12):
        rest_square = rest_square + jnp.sum(grads[position] * grads[position])
    rest_norm = jnp.sqrt(rest_square)
    return (block_out, input_grad, grads[0], grads[1], grads[2], grads[3], grads[4], grads[5], grads[6], grads[7], grads[8], grads[9], grads[10], grads[11], grads[12], freq_norm, rest_norm)
```

```python
import functools

import jax
import jax.numpy as jnp
from jax import lax
from jax.experimental import pallas as pl
from jax.experimental.pallas import tpu as pltpu
from jax.sharding import PartitionSpec as P

GRID = 24
EPSILON = 1e-06
MASKED_SCORE = -1e30
ROOT_HALF = 0.7071067811865476
DENSITY_SCALE = 0.3989422804014327
F32 = jnp.float32
BF16 = jnp.bfloat16
LANES = 128
HEAD = 64
GROUPS = 3
VMEM_LIMIT = 56 << 20


def dot(left, right, left_dim=1, right_dim=0):
    return lax.dot_general(
        left, right, (((left_dim,), (right_dim,)), ((), ())), preferred_element_type=F32
    )


def normalize(row_data):
    row_mean = jnp.mean(row_data, axis=-1, keepdims=True)
    centred = row_data - row_mean
    inverse = lax.rsqrt(jnp.mean(centred * centred, axis=-1, keepdims=True) + EPSILON)
    return (centred * inverse, inverse)


def norm_back(grad_unit, unit_rows, inverse):
    return inverse * (
        grad_unit
        - jnp.mean(grad_unit, axis=-1, keepdims=True)
        - unit_rows * jnp.mean(grad_unit * unit_rows, axis=-1, keepdims=True)
    )


def gelu_exact(values):
    return 0.5 * values * (1.0 + lax.erf(values * ROOT_HALF))


def gelu_slope(values):
    return (
        0.5 * (1.0 + lax.erf(values * ROOT_HALF))
        + values * jnp.exp(-0.5 * values * values) * DENSITY_SCALE
    )


def swap_halves(tile):
    lane = lax.broadcasted_iota(jnp.int32, (1, LANES), 1)
    first = (lane % HEAD) < HEAD // 2
    return jnp.where(
        first, pltpu.roll(tile, LANES - HEAD // 2, 1), pltpu.roll(tile, HEAD // 2, 1)
    )


def qkv_kernel(
    x_ref, gain_ref, shift_ref, weight_ref, bias_ref, cos_ref, sin_ref, normed_ref, qkv_ref
):
    width = x_ref.shape[1]
    unit, _ = normalize(x_ref[...].astype(F32))
    normed = (unit * gain_ref[...] + shift_ref[...]).astype(BF16)
    normed_ref[...] = normed
    for part in range(3):
        packed = (
            dot(normed, weight_ref[:, part * width : (part + 1) * width])
            + bias_ref[:, part * width : (part + 1) * width]
        )
        for tile in range(width // LANES):
            cols = slice(tile * LANES, (tile + 1) * LANES)
            piece = packed[:, cols]
            if part < 2:
                piece = piece * cos_ref[:, cols] + swap_halves(piece) * sin_ref[:, cols]
            if part == 0:
                piece = piece * (HEAD**-0.5)
            qkv_ref[:, part * width + tile * LANES : part * width + (tile + 1) * LANES] = (
                piece.astype(BF16)
            )


def project_qkv(rows, gain, shift, weight, bias, cosine, sine, slots):
    row_count, width = rows.shape
    tile = slots // 2
    whole = lambda shape: pl.BlockSpec(shape, lambda i: (0, 0))
    return pl.pallas_call(
        qkv_kernel,
        grid=(row_count // tile,),
        in_specs=[
            pl.BlockSpec((tile, width), lambda i: (i, 0)),
            whole((1, width)),
            whole((1, width)),
            whole((width, 3 * width)),
            whole((1, 3 * width)),
            pl.BlockSpec((tile, width), lambda i: (i % 2, 0)),
            pl.BlockSpec((tile, width), lambda i: (i % 2, 0)),
        ],
        out_specs=[
            pl.BlockSpec((tile, width), lambda i: (i, 0)),
            pl.BlockSpec((tile, 3 * width), lambda i: (i, 0)),
        ],
        out_shape=[
            jax.ShapeDtypeStruct((row_count, width), BF16),
            jax.ShapeDtypeStruct((row_count, 3 * width), BF16),
        ],
        cost_estimate=pl.CostEstimate(
            flops=6 * row_count * width * width,
            bytes_accessed=row_count * width * 16 + 6 * width * width,
            transcendentals=0,
        ),
        compiler_params=pltpu.CompilerParams(vmem_limit_bytes=VMEM_LIMIT),
    )(rows, gain, shift, weight, bias, cosine, sine)


def attend_kernel(q_ref, k_ref, v_ref, mask_ref, mixed_ref, total_ref):
    low = lax.broadcasted_iota(jnp.int32, (1, LANES), 1) < HEAD
    queries, keys, values = q_ref[...], k_ref[...], v_ref[...]
    zero = jnp.zeros_like(queries)
    mask = mask_ref[0]
    mixed, totals = None, []
    for head in range(2):
        keep = low if head == 0 else ~low
        scores = dot(jnp.where(keep, queries, zero), keys, 1, 1) + mask
        row_max = jnp.max(scores, axis=1, keepdims=True)
        weights = jnp.exp(scores - row_max)
        row_total = jnp.sum(weights, axis=1, keepdims=True)
        low_weights = (weights * (1.0 / row_total)).astype(BF16)
        part = dot(low_weights, jnp.where(keep, values, zero))
        mixed = part if mixed is None else mixed + part
        totals.append(row_max + jnp.log(row_total))
    mixed_ref[...] = mixed.astype(BF16)
    total_ref[...] = jnp.where(low, totals[0], totals[1])


def attend(qkv, mask_row, slots):
    row_count, width = qkv.shape[0], qkv.shape[1] // 3
    images, pairs = row_count // slots, width // LANES
    block = lambda part: pl.BlockSpec((slots, LANES), lambda i, p: (i, p + part * pairs))
    return pl.pallas_call(
        attend_kernel,
        grid=(images, pairs),
        in_specs=[
            block(0),
            block(1),
            block(2),
            pl.BlockSpec((1, 1, slots), lambda i, p: (i, 0, 0)),
        ],
        out_specs=[block(0), block(0)],
        out_shape=[
            jax.ShapeDtypeStruct((row_count, width), BF16),
            jax.ShapeDtypeStruct((row_count, width), F32),
        ],
        cost_estimate=pl.CostEstimate(
            flops=16 * row_count * slots * width,
            bytes_accessed=row_count * width * 12,
            transcendentals=row_count * slots * 2 * pairs,
        ),
        compiler_params=pltpu.CompilerParams(vmem_limit_bytes=VMEM_LIMIT),
    )(qkv, qkv, qkv, mask_row)


def attend_back_pair(q, k, v, mixed, grad_mixed, totals, mask, cosine, sine, place):
    low = lax.broadcasted_iota(jnp.int32, (1, LANES), 1) < HEAD
    zero = jnp.zeros_like(q)
    product = jnp.transpose(grad_mixed.astype(F32) * mixed.astype(F32))
    totals = jnp.transpose(totals)
    grad_q = grad_k = grad_v = None
    for head in range(2):
        keep = low if head == 0 else ~low
        q_head = jnp.where(keep, q, zero)
        grad_head = jnp.where(keep, grad_mixed, zero)
        k_head = jnp.where(keep, k, zero)
        total = totals[head * HEAD : head * HEAD + 1]
        inner = jnp.sum(product[head * HEAD : (head + 1) * HEAD], axis=0, keepdims=True)
        weights = jnp.exp((dot(k, q_head, 1, 1) + mask) - total)
        grad_weights = dot(v, grad_head, 1, 1)
        grad_scores = (weights * (grad_weights - inner)).astype(BF16)
        part_v = dot(weights.astype(BF16), grad_head)
        part_k = dot(grad_scores, q_head)
        part_q = dot(grad_scores, k_head, 0, 0)
        grad_v = part_v if grad_v is None else grad_v + part_v
        grad_k = part_k if grad_k is None else grad_k + part_k
        grad_q = part_q if grad_q is None else grad_q + part_q
    turn = grad_q * swap_halves(q.astype(F32)) + grad_k * swap_halves(k.astype(F32))
    freq_across = jnp.sum(turn * place[:, 0:1], axis=0, keepdims=True)
    freq_down = jnp.sum(turn * place[:, 1:2], axis=0, keepdims=True)
    grad_q = grad_q * (HEAD**-0.5)
    grad_q = (grad_q * cosine - swap_halves(grad_q) * sine).astype(BF16)
    grad_k = (grad_k * cosine - swap_halves(grad_k) * sine).astype(BF16)
    return (grad_q, grad_k, grad_v.astype(BF16), freq_across, freq_down)


def attend_back_kernel(
    q_ref, k_ref, v_ref, mixed_ref, grad_ref, total_ref, mask_ref, cos_ref, sin_ref, place_ref,
    packed_ref, sums_ref,
):
    span = q_ref.shape[1]
    row = lax.broadcasted_iota(jnp.int32, (8, LANES), 0)
    for pair in range(span // LANES):
        cols = slice(pair * LANES, (pair + 1) * LANES)
        grad_q, grad_k, grad_v, across, down = attend_back_pair(
            q_ref[:, cols], k_ref[:, cols], v_ref[:, cols], mixed_ref[:, cols], grad_ref[:, cols],
            total_ref[:, cols], mask_ref[...], cos_ref[:, cols], sin_ref[:, cols], place_ref[...],
        )
        sums = jnp.where(row == 0, across, jnp.where(row == 1, down, 0.0))
        for part, member in enumerate((grad_q, grad_k, grad_v)):
            packed_ref[:, part * span + pair * LANES : part * span + (pair + 1) * LANES] = member
            column_sum = jnp.sum(member.astype(F32), axis=0, keepdims=True)
            sums = jnp.where(row == 2 + part, column_sum, sums)
        sums_ref[0, :, cols] = sums


def attend_back(qkv, mixed, grad_mixed, totals, mask_col, cosine, sine, place, slots, group):
    row_count, width = mixed.shape
    images, span = row_count // slots, width // GROUPS
    block = lambda part: pl.BlockSpec((slots, span), lambda i: (i, group + part * GROUPS))
    table = pl.BlockSpec((slots, span), lambda i: (0, group))
    pairs = span // LANES
    return pl.pallas_call(
        attend_back_kernel,
        grid=(images,),
        in_specs=[
            block(0), block(1), block(2), block(0), block(0), block(0),
            pl.BlockSpec((slots, 1), lambda i: (i, 0)),
            table,
            table,
            pl.BlockSpec((slots, LANES), lambda i: (0, 0)),
        ],
        out_specs=[
            pl.BlockSpec((slots, 3 * span), lambda i: (i, 0)),
            pl.BlockSpec((1, 8, span), lambda i: (i, 0, 0)),
        ],
        out_shape=[
            jax.ShapeDtypeStruct((row_count, 3 * span), BF16),
            jax.ShapeDtypeStruct((images, 8, span), F32),
        ],
        cost_estimate=pl.CostEstimate(
            flops=40 * row_count * slots * span,
            bytes_accessed=row_count * span * 20,
            transcendentals=row_count * slots * 2 * pairs,
        ),
        compiler_params=pltpu.CompilerParams(vmem_limit_bytes=VMEM_LIMIT),
    )(qkv, qkv, qkv, mixed, grad_mixed, totals, mask_col, cosine, sine, place)


class Exchange:
    def __init__(self, mesh):
        self.sizes = dict(mesh.shape)

    def bits(self, axis):
        return [(axis, 1 << b) for b in range(self.sizes[axis].bit_length() - 1)]

    def swap(self, value, step):
        axis, bit = step
        pairs = [(i, i ^ bit) for i in range(self.sizes[axis])]
        return lax.ppermute(value, axis, pairs)

    def side(self, step):
        axis, bit = step
        return (lax.axis_index(axis) // bit) % 2

    def halve(self, value, step):
        size = value.shape[0] // 2
        mine = self.side(step)
        keep = lax.dynamic_slice_in_dim(value, mine * size, size, 0)
        send = lax.dynamic_slice_in_dim(value, (1 - mine) * size, size, 0)
        got = self.swap(send, step)
        return (keep.astype(F32) + got.astype(F32)).astype(BF16)

    def double(self, value, step):
        other = self.swap(value, step)
        first = self.side(step) == 0
        return jnp.concatenate(
            [jnp.where(first, value, other), jnp.where(first, other, value)], axis=0
        )

    def sum_over(self, value, steps):
        for step in steps:
            value = self.halve(value, step)
        for step in reversed(steps):
            value = self.double(value, step)
        return value

    def sum_small(self, value, steps):
        for step in steps:
            value = value + self.swap(value, step)
        return value


def body(
    net,
    images,
    keep_mask,
    ln1_gain,
    ln1_bias,
    qkv_weight,
    qkv_bias,
    frequencies,
    proj_weight,
    proj_bias,
    ln2_gain,
    ln2_bias,
    fc1_weight,
    fc1_bias,
    fc2_weight,
    fc2_bias,
    out_grad,
):
    image_count, slots, width = images.shape
    row_count = image_count * slots
    span = width // GROUPS
    inner_step, outer_step = net.bits("tensor")
    tensor_steps, dp_steps = net.bits("tensor"), net.bits("dp")

    shards = {0: (fc1_weight, fc1_bias, fc2_weight)}
    shards[2] = tuple(net.swap(member, outer_step) for member in shards[0])
    shards[1] = tuple(net.swap(member, inner_step) for member in shards[0])
    shards[3] = tuple(net.swap(member, inner_step) for member in shards[2])

    kept = keep_mask.astype(F32)
    kept_col = kept.reshape(row_count, 1)
    mask_add = jnp.where(kept > 0, 0.0, MASKED_SCORE)
    mask_row = mask_add.reshape(image_count, 1, slots)
    mask_col = mask_add.reshape(row_count, 1)
    place = jnp.arange(slots)
    across = (place // GRID).astype(F32)
    downward = (place % GRID).astype(F32)
    lane_freq = jnp.concatenate([frequencies, frequencies], axis=-1).reshape(2, 1, width)
    steps = jnp.arange(slots // GRID).astype(F32)[:, None]
    angle_a = steps * lane_freq[0]
    angle_d = jnp.arange(GRID).astype(F32)[:, None] * lane_freq[1]
    sign = jnp.where(jnp.arange(width) % HEAD < HEAD // 2, -1.0, 1.0)
    cos_a, sin_a = jnp.cos(angle_a)[:, None], jnp.sin(angle_a)[:, None]
    cos_d, sin_d = jnp.cos(angle_d)[None], jnp.sin(angle_d)[None]
    cosine = (cos_a * cos_d - sin_a * sin_d).reshape(slots, width)
    sine = ((sin_a * cos_d + cos_a * sin_d) * sign).reshape(slots, width)
    lane = jnp.arange(LANES)[None]
    places = jnp.where(lane == 0, across[:, None], jnp.where(lane == 1, downward[:, None], 0.0))

    rows = images.reshape(row_count, width)
    row_of = lambda vector: vector.reshape(1, -1)
    normed_one, qkv = project_qkv(
        rows, row_of(ln1_gain), row_of(ln1_bias), qkv_weight, row_of(qkv_bias), cosine, sine, slots
    )
    mixed, totals = attend(qkv, mask_row, slots)

    inputs = rows.astype(F32)
    resid = inputs + dot(mixed, proj_weight) + proj_bias
    unit_two, inverse_two = normalize(resid)
    normed_two = (unit_two * ln2_gain + ln2_bias).astype(BF16)
    grad_low = (kept_col * out_grad.astype(F32).reshape(row_count, width)).astype(BF16)

    mlp_out = jnp.zeros((), F32)
    grad_normed_two = jnp.zeros((), F32)
    fc1_grads, fc2_grads, hidden_sums = {}, {}, {}
    for r in (0, 2, 3, 1):
        weight_in, bias_in, weight_out = shards[r]
        hidden = dot(normed_two, weight_in) + bias_in.astype(F32)
        active = gelu_exact(hidden).astype(BF16)
        mlp_out = mlp_out + dot(active, weight_out)
        fc2_grads[r] = dot(active, grad_low, 0, 0).astype(BF16)
        grad_hidden = (dot(grad_low, weight_out, 1, 1) * gelu_slope(hidden)).astype(BF16)
        fc1_grads[r] = dot(normed_two, grad_hidden, 0, 0).astype(BF16)
        hidden_sums[r] = jnp.sum(grad_hidden.astype(F32), axis=0)
        grad_normed_two = grad_normed_two + dot(grad_hidden, weight_in, 1, 1)

    def to_owner(grads, order):
        far = grads[2].astype(F32) + net.swap(grads[3], inner_step).astype(F32)
        far = net.swap(far.astype(BF16), outer_step)
        near = grads[0].astype(F32) + net.swap(grads[1], inner_step).astype(F32)
        return net.sum_over((near + far.astype(F32)).astype(BF16), order)

    rotated = dp_steps[1:] + dp_steps[:1]
    fc2_weight_grad = to_owner(fc2_grads, dp_steps).astype(F32)
    fc1_weight_grad = to_owner(fc1_grads, rotated).astype(F32)

    grad_rows = grad_low.astype(F32)
    block_out = (kept_col * (resid + mlp_out + fc2_bias)).astype(BF16).reshape(images.shape)
    grad_resid = grad_rows + norm_back(grad_normed_two * ln2_gain, unit_two, inverse_two)
    low_grad_branch = grad_resid.astype(BF16)
    proj_weight_grad = dot(mixed, low_grad_branch, 0, 0).astype(BF16)
    low_grad_mixed = dot(low_grad_branch, proj_weight, 1, 1).astype(BF16)
    proj_weight_grad = net.sum_over(proj_weight_grad, tensor_steps + dp_steps).astype(F32)

    own = lax.axis_index("tensor")
    parts = jnp.arange(4)[:, None]
    hidden_rows = sum(jnp.where(parts == (own ^ r), hidden_sums[r][None], 0.0) for r in range(4))
    early = jnp.concatenate(
        [
            hidden_rows,
            jnp.stack(
                [
                    jnp.sum(low_grad_branch.astype(F32), axis=0),
                    jnp.sum(grad_normed_two * unit_two, axis=0),
                    jnp.sum(grad_normed_two, axis=0),
                    jnp.sum(grad_rows, axis=0),
                ]
            ),
        ],
        axis=0,
    )
    early = net.sum_small(early, tensor_steps + dp_steps)
    fc1_bias_grad = lax.dynamic_slice_in_dim(early, own, 1, 0)[0]
    proj_bias_grad, ln2_gain_grad, ln2_bias_grad, fc2_bias_grad = early[4:]

    grad_normed_one = jnp.zeros((), F32)
    group_grads, group_sums = [], []
    orders = [tensor_steps + dp_steps, dp_steps + tensor_steps, tensor_steps + rotated]
    for group in range(GROUPS):
        packed, sums = attend_back(
            qkv, mixed, low_grad_mixed, totals, mask_col, cosine, sine, places, slots, group
        )
        group_sums.append(jnp.sum(sums, axis=0))
        weight_grad = dot(normed_one, packed, 0, 0).astype(BF16)
        group_grads.append(net.sum_over(weight_grad, orders[group]).astype(F32))
        weight = jnp.concatenate(
            [
                qkv_weight[:, part * width + group * span : part * width + (group + 1) * span]
                for part in range(3)
            ],
            axis=1,
        )
        grad_normed_one = grad_normed_one + dot(packed, weight, 1, 1)
    qkv_weight_grad = jnp.concatenate(
        [g[:, part * span : (part + 1) * span] for part in range(3) for g in group_grads], axis=1
    )

    unit_one, inverse_one = normalize(inputs)
    input_grad = grad_resid + norm_back(grad_normed_one * ln1_gain, unit_one, inverse_one)
    input_grad = input_grad.astype(BF16).reshape(images.shape)
    late = jnp.concatenate(
        [
            jnp.concatenate(group_sums, axis=1)[:5],
            jnp.stack(
                [jnp.sum(grad_normed_one * unit_one, axis=0), jnp.sum(grad_normed_one, axis=0)]
            ),
            jnp.zeros((1, width), F32),
        ],
        axis=0,
    )
    late = net.sum_small(late, tensor_steps + dp_steps)
    turned = late[:2].reshape(2, width // HEAD, 2, HEAD // 2)
    freq_grad = turned[:, :, 1] - turned[:, :, 0]
    qkv_bias_grad = late[2:5].reshape(-1)
    ln1_gain_grad, ln1_bias_grad = late[5], late[6]

    freq_norm = jnp.sqrt(jnp.sum(freq_grad * freq_grad))
    square = jnp.float32(0.0)
    for member in (
        ln1_gain_grad,
        ln1_bias_grad,
        qkv_weight_grad,
        qkv_bias_grad,
        proj_weight_grad,
        proj_bias_grad,
        ln2_gain_grad,
        ln2_bias_grad,
        fc2_bias_grad,
    ):
        square = square + jnp.sum(member * member)
    return (
        block_out,
        input_grad,
        ln1_gain_grad,
        ln1_bias_grad,
        qkv_weight_grad,
        qkv_bias_grad,
        freq_grad,
        proj_weight_grad,
        proj_bias_grad,
        ln2_gain_grad,
        ln2_bias_grad,
        fc1_weight_grad,
        fc1_bias_grad,
        fc2_weight_grad,
        fc2_bias_grad,
        freq_norm,
        jnp.sqrt(square),
    )


def solution(mesh):
    rows = P(("dp", "tensor"), None, None)
    whole = P()
    hidden_in, hidden_out = P(None, "tensor"), P("tensor", None)
    return jax.shard_map(
        functools.partial(body, Exchange(mesh)),
        mesh=mesh,
        in_specs=(
            (rows, P(("dp", "tensor"), None))
            + (whole,) * 9
            + (hidden_in, P("tensor"), hidden_out, whole, rows)
        ),
        out_specs=(
            (rows, rows) + (whole,) * 9 + (hidden_in, P("tensor"), hidden_out) + (whole,) * 3
        ),
        check_vma=False,
    )
```

```python
import functools

import jax
import jax.numpy as jnp
from jax import lax
from jax.experimental import pallas as pl
from jax.experimental.pallas import tpu as pltpu
from jax.sharding import PartitionSpec as P

GRID = 24
EPSILON = 1e-06
MASKED_SCORE = 1e30
ROOT_HALF = 0.7071067811865476
DENSITY_SCALE = 0.3989422804014327
F32 = jnp.float32
BF16 = jnp.bfloat16
LANES = 128
HEAD = 64
HIDDEN_TILE = 256
PARAMS = pltpu.CompilerParams(vmem_limit_bytes=56 << 20)


def dot(left, right, left_dim=1, right_dim=0):
    return lax.dot_general(
        left, right, (((left_dim,), (right_dim,)), ((), ())), preferred_element_type=F32
    )


def normalize(row_data):
    row_mean = jnp.mean(row_data, axis=-1, keepdims=True)
    centred = row_data - row_mean
    inverse = lax.rsqrt(jnp.mean(centred * centred, axis=-1, keepdims=True) + EPSILON)
    return (centred * inverse, inverse)


def norm_back(grad_unit, unit_rows, inverse):
    return inverse * (
        grad_unit
        - jnp.mean(grad_unit, axis=-1, keepdims=True)
        - unit_rows * jnp.mean(grad_unit * unit_rows, axis=-1, keepdims=True)
    )


def swap_halves(tile):
    lane = lax.broadcasted_iota(jnp.int32, (1, LANES), 1)
    first = (lane % HEAD) < HEAD // 2
    return jnp.where(
        first, pltpu.roll(tile, LANES - HEAD // 2, 1), pltpu.roll(tile, HEAD // 2, 1)
    )


def column_sum(values):
    return jnp.sum(values, axis=0, keepdims=True)


def stack_rows(members):
    width = members[0].shape[1]
    row = lax.broadcasted_iota(jnp.int32, (8, width), 0)
    total = jnp.zeros((8, width), F32)
    for at, member in enumerate(members):
        total = jnp.where(row == at, member, total)
    return total


def shape(dims, dtype=BF16):
    return jax.ShapeDtypeStruct(dims, dtype)


def fixed(*dims):
    return pl.BlockSpec(dims, lambda *_: (0,) * len(dims))


def cost(flops, moved, steep=0):
    return pl.CostEstimate(flops=flops, bytes_accessed=moved, transcendentals=steep)


def qkv_kernel(x_ref, vector_ref, weight_ref, normed_ref, qkv_ref, cos_ref, sin_ref):
    tile, width = x_ref.shape
    across_count = tile // GRID

    @pl.when(pl.program_id(1) == 0)
    def _():
        first = (pl.program_id(0) * across_count).astype(F32)
        padded = -(-across_count // 8) * 8
        across = first + lax.broadcasted_iota(jnp.int32, (padded, width), 0).astype(F32)
        down = lax.broadcasted_iota(jnp.int32, (GRID, width), 0).astype(F32)
        across = across * vector_ref[5:6]
        down = down * vector_ref[6:7]
        cos_a, sin_a, cos_d, sin_d = jnp.cos(across), jnp.sin(across), jnp.cos(down), jnp.sin(down)
        lane = lax.broadcasted_iota(jnp.int32, (1, width), 1)
        sign = jnp.where((lane % HEAD) < HEAD // 2, -1.0, 1.0)
        for at in range(across_count):
            rows = slice(at * GRID, (at + 1) * GRID)
            one_cos, one_sin = cos_a[at : at + 1], sin_a[at : at + 1]
            cos_ref[rows, :] = one_cos * cos_d - one_sin * sin_d
            sin_ref[rows, :] = (one_sin * cos_d + one_cos * sin_d) * sign

    unit, _ = normalize(x_ref[...].astype(F32))
    normed = (unit * vector_ref[0:1] + vector_ref[1:2]).astype(BF16)
    normed_ref[...] = normed
    for part in range(3):
        cols = slice(part * width, (part + 1) * width)
        packed = dot(normed, weight_ref[:, cols]) + vector_ref[2 + part : 3 + part]
        for at in range(0, width, LANES):
            piece = packed[:, at : at + LANES]
            if part < 2:
                cosine, sine = cos_ref[:, at : at + LANES], sin_ref[:, at : at + LANES]
                piece = piece * cosine + swap_halves(piece) * sine
            if part == 0:
                piece = piece * (HEAD**-0.5)
            qkv_ref[:, part * width + at : part * width + at + LANES] = piece.astype(BF16)


def project_qkv(rows, vectors, weight, slots):
    row_count, width = rows.shape
    halves = 2
    tile = slots // halves
    row_block = lambda cols: pl.BlockSpec((tile, cols), lambda h, n: (n * halves + h, 0))
    table = pl.BlockSpec((tile, width), lambda h, n: (h, 0))
    return pl.pallas_call(
        qkv_kernel,
        grid=(halves, row_count // slots),
        in_specs=[row_block(width), fixed(*vectors.shape), fixed(*weight.shape)],
        out_specs=[row_block(width), row_block(3 * width), table, table],
        out_shape=[
            shape((row_count, width)),
            shape((row_count, 3 * width)),
            shape((slots, width), F32),
            shape((slots, width), F32),
        ],
        cost_estimate=cost(6 * row_count * width * width, row_count * width * 14),
        compiler_params=PARAMS,
    )(rows, vectors, weight)


def attend_kernel(q_ref, k_ref, v_ref, kept_ref, mixed_ref, total_ref):
    low = lax.broadcasted_iota(jnp.int32, (1, LANES), 1) < HEAD
    queries, keys, values = q_ref[...], k_ref[...], v_ref[...]
    zero = jnp.zeros_like(queries)
    mask = (kept_ref[0] - 1.0) * MASKED_SCORE
    mixed, totals = None, []
    for head in range(2):
        keep = low if head == 0 else ~low
        scores = dot(jnp.where(keep, queries, zero), keys, 1, 1) + mask
        row_max = jnp.max(scores, axis=1, keepdims=True)
        weights = jnp.exp(scores - row_max)
        row_total = jnp.sum(weights, axis=1, keepdims=True)
        low_weights = (weights * (1.0 / row_total)).astype(BF16)
        part = dot(low_weights, jnp.where(keep, values, zero))
        mixed = part if mixed is None else mixed + part
        totals.append(row_max + jnp.log(row_total))
    mixed_ref[...] = mixed.astype(BF16)
    total_ref[...] = jnp.where(low, totals[0], totals[1])


def attend(qkv, kept_row, slots):
    row_count, width = qkv.shape[0], qkv.shape[1] // 3
    images, pairs = row_count // slots, width // LANES
    block = lambda part: pl.BlockSpec((slots, LANES), lambda i, p: (i, p + part * pairs))
    return pl.pallas_call(
        attend_kernel,
        grid=(images, pairs),
        in_specs=[
            block(0),
            block(1),
            block(2),
            pl.BlockSpec((1, 1, slots), lambda i, p: (i, 0, 0)),
        ],
        out_specs=[block(0), block(0)],
        out_shape=[shape((row_count, width)), shape((row_count, width), F32)],
        cost_estimate=cost(
            16 * row_count * slots * width, row_count * width * 12, row_count * slots * 2 * pairs
        ),
        compiler_params=PARAMS,
    )(qkv, qkv, qkv, kept_row)


def project_kernel(
    mixed_ref, x_ref, grad_ref, kept_ref, vector_ref, weight_ref, resid_ref, normed_ref, low_ref
):
    resid = x_ref[...].astype(F32) + dot(mixed_ref[...], weight_ref[...]) + vector_ref[0:1]
    unit, _ = normalize(resid)
    resid_ref[...] = resid
    normed_ref[...] = (unit * vector_ref[1:2] + vector_ref[2:3]).astype(BF16)
    low_ref[...] = (kept_ref[...] * grad_ref[...].astype(F32)).astype(BF16)


def project_out(mixed, rows, out_grad, kept_col, vectors, weight):
    row_count, width = rows.shape
    tile = row_count // 4
    block = pl.BlockSpec((tile, width), lambda i: (i, 0))
    return pl.pallas_call(
        project_kernel,
        grid=(4,),
        in_specs=[
            block,
            block,
            block,
            pl.BlockSpec((tile, 1), lambda i: (i, 0)),
            fixed(*vectors.shape),
            fixed(*weight.shape),
        ],
        out_specs=[block, block, block],
        out_shape=[
            shape((row_count, width), F32),
            shape((row_count, width)),
            shape((row_count, width)),
        ],
        cost_estimate=cost(2 * row_count * width * width, row_count * width * 14),
        compiler_params=PARAMS,
    )(mixed, rows, out_grad, kept_col, vectors, weight)


def hidden_kernel(
    normed_ref, grad_ref, in_ref, bias_ref, out_ref,
    active_ref, hidden_ref, in_grad_ref, out_grad_ref, bias_grad_ref,
):
    normed, grad = normed_ref[...], grad_ref[...]
    hidden = dot(normed, in_ref[...]) + bias_ref[...]
    grad_active = dot(grad, out_ref[...], 1, 1)
    half = 0.5 * (1.0 + lax.erf(hidden * ROOT_HALF))
    active = (hidden * half).astype(BF16)
    slope = half + hidden * jnp.exp(-0.5 * hidden * hidden) * DENSITY_SCALE
    grad_hidden = (grad_active * slope).astype(BF16)
    active_ref[...] = active
    hidden_ref[...] = grad_hidden
    in_grad_ref[...] = dot(normed, grad_hidden, 0, 0).astype(BF16)
    out_grad_ref[...] = dot(active, grad, 0, 0).astype(BF16)
    bias_grad_ref[...] = column_sum(grad_hidden.astype(F32))


def hidden_units(normed, grad, weight_in, bias_in, weight_out):
    row_count, width = normed.shape
    units = weight_in.shape[1]
    tile = HIDDEN_TILE
    cols = lambda rows: pl.BlockSpec((rows, tile), lambda i: (0, i))
    rows = pl.BlockSpec((tile, width), lambda i: (i, 0))
    return pl.pallas_call(
        hidden_kernel,
        grid=(units // tile,),
        in_specs=[
            fixed(row_count, width), fixed(row_count, width), cols(width), cols(1), rows
        ],
        out_specs=[cols(row_count), cols(row_count), cols(width), rows, cols(1)],
        out_shape=[
            shape((row_count, units)),
            shape((row_count, units)),
            shape((width, units)),
            shape((units, width)),
            shape((1, units), F32),
        ],
        cost_estimate=cost(
            8 * row_count * width * units, row_count * width * 8 + width * units * 8,
            2 * row_count * units,
        ),
        compiler_params=PARAMS,
    )(normed, grad, weight_in, bias_in, weight_out)


def mlp_out_kernel(*refs):
    actives, outs = refs[0:4], refs[4:8]
    resid_ref, kept_ref, vector_ref, block_ref = refs[8:]
    mlp_out = sum(dot(a[...], w[...]) for a, w in zip(actives, outs))
    block_ref[...] = (kept_ref[...] * (resid_ref[...] + mlp_out + vector_ref[3:4])).astype(BF16)


def mlp_back_kernel(*refs):
    hiddens, ins = refs[0:4], refs[4:8]
    proj_ref, resid_ref, low_ref, vector_ref = refs[8:12]
    grad_ref, branch_ref, mixed_ref, sums_ref = refs[12:]
    grad_normed = sum(dot(h[...], w[...], 1, 1) for h, w in zip(hiddens, ins))
    unit, inverse = normalize(resid_ref[...])
    grad_rows = low_ref[...].astype(F32)
    grad = grad_rows + norm_back(grad_normed * vector_ref[1:2], unit, inverse)
    branch = grad.astype(BF16)
    grad_ref[...] = grad
    branch_ref[...] = branch
    mixed_ref[...] = dot(branch, proj_ref[...], 1, 1).astype(BF16)
    sums = stack_rows(
        [
            column_sum(branch.astype(F32)),
            column_sum(grad_normed * unit),
            column_sum(grad_normed),
            column_sum(grad_rows),
        ]
    )

    @pl.when(pl.program_id(0) == 0)
    def _():
        sums_ref[...] = sums

    @pl.when(pl.program_id(0) > 0)
    def _():
        sums_ref[...] += sums


def mlp_result(actives, outs, resid, kept_col, vectors):
    row_count, width = resid.shape
    tile = row_count // 4
    block = pl.BlockSpec((tile, width), lambda i: (i, 0))
    return pl.pallas_call(
        mlp_out_kernel,
        grid=(4,),
        in_specs=[block] * 4
        + [fixed(width, width)] * 4
        + [block, pl.BlockSpec((tile, 1), lambda i: (i, 0)), fixed(*vectors.shape)],
        out_specs=block,
        out_shape=shape((row_count, width)),
        cost_estimate=cost(8 * row_count * width * width, row_count * width * 14),
        compiler_params=PARAMS,
    )(*actives, *outs, resid, kept_col, vectors)


def mlp_back(hiddens, ins, proj_weight, resid, grad_low, vectors):
    row_count, width = resid.shape
    tile = row_count // 4
    block = pl.BlockSpec((tile, width), lambda i: (i, 0))
    return pl.pallas_call(
        mlp_back_kernel,
        grid=(4,),
        in_specs=[block] * 4
        + [fixed(width, width)] * 5
        + [block, block, fixed(*vectors.shape)],
        out_specs=[block, block, block, fixed(8, width)],
        out_shape=[
            shape((row_count, width), F32),
            shape((row_count, width)),
            shape((row_count, width)),
            shape((8, width), F32),
        ],
        cost_estimate=cost(10 * row_count * width * width, row_count * width * 22),
        compiler_params=PARAMS,
    )(*hiddens, *ins, proj_weight, resid, grad_low, vectors)


def attend_back_kernel(
    q_ref, k_ref, v_ref, mixed_ref, grad_ref, total_ref, kept_ref, cos_ref, sin_ref, normed_ref,
    packed_ref, weight_ref, sums_ref, total_weight,
):
    slots = q_ref.shape[0]
    low = lax.broadcasted_iota(jnp.int32, (1, LANES), 1) < HEAD
    q, k, v, grad_mixed = q_ref[...], k_ref[...], v_ref[...], grad_ref[...]
    zero = jnp.zeros_like(q)
    mask = (kept_ref[...] - 1.0) * MASKED_SCORE
    product = jnp.transpose(grad_mixed.astype(F32) * mixed_ref[...].astype(F32))
    totals = jnp.transpose(total_ref[...])
    grad_q = grad_k = grad_v = None
    for head in range(2):
        keep = low if head == 0 else ~low
        q_head = jnp.where(keep, q, zero)
        grad_head = jnp.where(keep, grad_mixed, zero)
        k_head = jnp.where(keep, k, zero)
        total = totals[head * HEAD : head * HEAD + 1]
        inner = column_sum(product[head * HEAD : (head + 1) * HEAD])
        weights = jnp.exp((dot(k, q_head, 1, 1) + mask) - total)
        grad_weights = dot(v, grad_head, 1, 1)
        grad_scores = (weights * (grad_weights - inner)).astype(BF16)
        part_v = dot(weights.astype(BF16), grad_head)
        part_k = dot(grad_scores, q_head)
        part_q = dot(grad_scores, k_head, 0, 0)
        grad_v = part_v if grad_v is None else grad_v + part_v
        grad_k = part_k if grad_k is None else grad_k + part_k
        grad_q = part_q if grad_q is None else grad_q + part_q
    turn = grad_q * swap_halves(q.astype(F32)) + grad_k * swap_halves(k.astype(F32))
    slot = lax.broadcasted_iota(jnp.int32, (slots, 1), 0)
    across = slot // GRID
    down = slot - across * GRID
    cosine, sine = cos_ref[...], sin_ref[...]
    grad_q = grad_q * (HEAD**-0.5)
    grad_q = (grad_q * cosine - swap_halves(grad_q) * sine).astype(BF16)
    grad_k = (grad_k * cosine - swap_halves(grad_k) * sine).astype(BF16)
    packed = jnp.concatenate([grad_q, grad_k, grad_v.astype(BF16)], axis=1)
    packed_ref[...] = packed
    parts = column_sum(packed.astype(F32))
    sums = stack_rows(
        [
            column_sum(turn * across.astype(F32)),
            column_sum(turn * down.astype(F32)),
            parts[:, :LANES],
            parts[:, LANES : 2 * LANES],
            parts[:, 2 * LANES :],
        ]
    )
    weight_grad = dot(normed_ref[...], packed, 0, 0)
    last = pl.num_programs(0) - 1

    @pl.when(pl.program_id(0) == 0)
    def _():
        sums_ref[...] = sums
        total_weight[...] = weight_grad

    @pl.when(pl.program_id(0) > 0)
    def _():
        sums_ref[...] += sums
        total_weight[...] += weight_grad

    @pl.when(pl.program_id(0) == last)
    def _():
        weight_ref[...] = total_weight[...].astype(BF16)


def attend_back(qkv, mixed, grad_mixed, totals, kept_col, cosine, sine, normed, slots, pair):
    row_count, width = mixed.shape
    images, pairs = row_count // slots, width // LANES
    block = lambda part: pl.BlockSpec((slots, LANES), lambda i: (i, pair + part * pairs))
    table = pl.BlockSpec((slots, LANES), lambda i: (0, pair))
    return pl.pallas_call(
        attend_back_kernel,
        grid=(images,),
        in_specs=[
            block(0), block(1), block(2), block(0), block(0), block(0),
            pl.BlockSpec((slots, 1), lambda i: (i, 0)),
            table,
            table,
            pl.BlockSpec((slots, width), lambda i: (i, 0)),
        ],
        out_specs=[
            pl.BlockSpec((slots, 3 * LANES), lambda i: (i, 0)),
            fixed(width, 3 * LANES),
            fixed(8, LANES),
        ],
        out_shape=[
            shape((row_count, 3 * LANES)),
            shape((width, 3 * LANES)),
            shape((8, LANES), F32),
        ],
        scratch_shapes=[pltpu.VMEM((width, 3 * LANES), F32)],
        cost_estimate=cost(
            40 * row_count * slots * LANES, row_count * LANES * 30, row_count * slots * 2
        ),
        compiler_params=PARAMS,
    )(qkv, qkv, qkv, mixed, grad_mixed, totals, kept_col, cosine, sine, normed)


def finish_kernel(*refs):
    packed, (weight_ref, x_ref, grad_ref, vector_ref) = refs[:-6], refs[-6:-2]
    input_ref, sums_ref = refs[-2:]
    full = jnp.concatenate(
        [p[:, part * LANES : (part + 1) * LANES] for part in range(3) for p in packed], axis=1
    )
    grad_normed = dot(full, weight_ref[...], 1, 1)
    unit, inverse = normalize(x_ref[...].astype(F32))
    input_ref[...] = (
        grad_ref[...] + norm_back(grad_normed * vector_ref[0:1], unit, inverse)
    ).astype(BF16)
    sums = stack_rows([column_sum(grad_normed * unit), column_sum(grad_normed)])

    @pl.when(pl.program_id(0) == 0)
    def _():
        sums_ref[...] = sums

    @pl.when(pl.program_id(0) > 0)
    def _():
        sums_ref[...] += sums


def finish(packed, weight, rows, grad_resid, vectors):
    row_count, width = rows.shape
    tile = row_count // 4
    block = lambda cols: pl.BlockSpec((tile, cols), lambda i: (i, 0))
    return pl.pallas_call(
        finish_kernel,
        grid=(4,),
        in_specs=[block(3 * LANES)] * len(packed)
        + [fixed(*weight.shape), block(width), block(width), fixed(*vectors.shape)],
        out_specs=[block(width), fixed(8, width)],
        out_shape=[shape((row_count, width)), shape((8, width), F32)],
        cost_estimate=cost(6 * row_count * width * width, row_count * width * 14),
        compiler_params=PARAMS,
    )(*packed, weight, rows, grad_resid, vectors)


class Exchange:
    def __init__(self, mesh):
        self.sizes = dict(mesh.shape)

    def bits(self, axis):
        return [(axis, 1 << b) for b in range(self.sizes[axis].bit_length() - 1)]

    def swap(self, value, step):
        axis, bit = step
        pairs = [(i, i ^ bit) for i in range(self.sizes[axis])]
        return lax.ppermute(value, axis, pairs)

    def side(self, step):
        axis, bit = step
        return (lax.axis_index(axis) // bit) % 2

    def half(self, value, step, mine):
        size = value.shape[0] // 2
        side = self.side(step)
        return lax.dynamic_slice_in_dim(value, (side if mine else 1 - side) * size, size, 0)

    def join(self, mine, other, step):
        first = self.side(step) == 0
        return jnp.concatenate(
            [jnp.where(first, mine, other), jnp.where(first, other, mine)], axis=0
        )


def add(*members):
    return sum(member.astype(F32) for member in members).astype(BF16)


def tie(*members):
    return lax.optimization_barrier(members)


class Chain:
    def __init__(self, net, value, halving, full=(), joins=None):
        joins = list(reversed(halving)) if joins is None else joins
        self.net, self.value = net, value
        self.todo = [("halve", s) for s in halving] + [("full", s) for s in full]
        self.todo += [("join", s) for s in joins]
        self.flight = None

    def start(self):
        if not self.todo or self.flight is not None:
            return
        kind, step = self.todo[0]
        sent = self.net.half(self.value, step, False) if kind == "halve" else self.value
        self.flight = self.net.swap(sent, step)

    def end(self):
        if self.flight is None:
            return
        kind, step = self.todo.pop(0)
        if kind == "halve":
            self.value = add(self.net.half(self.value, step, True), self.flight)
        elif kind == "full":
            total = self.value.astype(F32) + self.flight.astype(F32)
            self.value = total.astype(self.value.dtype)
        else:
            self.value = self.net.join(self.value, self.flight, step)
        self.flight = None


def meet(chains, *outputs):
    flights = [c.flight for c in chains if c.flight is not None]
    tied = tie(flights, outputs)
    landed = list(tied[0])
    for chain in chains:
        if chain.flight is not None:
            chain.flight = landed.pop(0)
            chain.end()
    return tied[1]


def body(
    net,
    images,
    keep_mask,
    ln1_gain,
    ln1_bias,
    qkv_weight,
    qkv_bias,
    frequencies,
    proj_weight,
    proj_bias,
    ln2_gain,
    ln2_bias,
    fc1_weight,
    fc1_bias,
    fc2_weight,
    fc2_bias,
    out_grad,
):
    image_count, slots, width = images.shape
    row_count = image_count * slots
    inner, outer = net.bits("tensor")
    dp_steps = net.bits("dp")
    near_dp, far_dp = dp_steps[:1], dp_steps[1:]
    everyone = ("dp", "tensor")

    ins, outs = {0: fc1_weight}, {0: fc2_weight}
    ins[2], outs[2] = net.swap(fc1_weight, outer), net.swap(fc2_weight, outer)
    ins[1], outs[1] = net.swap(fc1_weight, inner), net.swap(fc2_weight, inner)
    own = lax.axis_index("tensor")
    biases = {0: fc1_bias}
    biases[1], biases[2] = net.swap(fc1_bias, inner), net.swap(fc1_bias, outer)
    biases[3] = net.swap(biases[2], inner)

    kept = keep_mask.astype(F32)
    kept_col = kept.reshape(row_count, 1)
    kept_row = kept.reshape(image_count, 1, slots)
    lane_freq = jnp.concatenate([frequencies, frequencies], axis=-1).reshape(2, width)
    first_vectors = jnp.concatenate(
        [
            ln1_gain[None],
            ln1_bias[None],
            qkv_bias.reshape(3, width),
            lane_freq,
            jnp.zeros((1, width), F32),
        ],
        axis=0,
    )
    vectors = jnp.concatenate(
        [v[None] for v in (proj_bias, ln2_gain, ln2_bias, fc2_bias)], axis=0
    )
    rows = images.reshape(row_count, width)
    normed_one, qkv, cosine, sine = project_qkv(rows, first_vectors, qkv_weight, slots)
    mixed, totals = attend(qkv, kept_row, slots)
    resid, normed_two, grad_low = project_out(
        mixed, rows, out_grad.reshape(row_count, width), kept_col, vectors, proj_weight
    )

    actives, hiddens, in_grads, out_grads, bias_grads = {}, {}, {}, {}, {}

    def chunk(r, normed, grad):
        results = hidden_units(normed, grad, ins[r], biases[r].astype(F32)[None], outs[r])
        actives[r], hiddens[r], in_grads[r], out_grads[r], bias_grads[r] = results

    normed_two, grad_low, ins[1], outs[1] = tie(normed_two, grad_low, ins[1], outs[1])
    chunk(1, normed_two, grad_low)
    normed_two, in_grads[1], out_grads[1], ins[2], outs[2] = tie(
        normed_two, in_grads[1], out_grads[1], ins[2], outs[2]
    )
    near_in, near_out = net.swap(in_grads[1], inner), net.swap(out_grads[1], inner)
    ins[3], outs[3] = net.swap(ins[2], inner), net.swap(outs[2], inner)
    chunk(0, normed_two, grad_low)
    normed_two, in_grads[0], out_grads[0], near_in, near_out, ins[3], outs[3] = tie(
        normed_two, in_grads[0], out_grads[0], near_in, near_out, ins[3], outs[3]
    )
    near_in = Chain(net, add(in_grads[0], near_in), near_dp, joins=[])
    near_out = Chain(net, add(out_grads[0], near_out), near_dp, joins=[])
    near_out.start()
    chunk(3, normed_two, grad_low)
    normed_two, in_grads[3], out_grads[3] = meet(
        [near_out], normed_two, in_grads[3], out_grads[3]
    )
    far_in, far_out = net.swap(in_grads[3], inner), net.swap(out_grads[3], inner)
    near_in.start()
    chunk(2, normed_two, grad_low)
    far_in, far_out, in_grads[2], out_grads[2], actives[2] = meet(
        [near_in], far_in, far_out, in_grads[2], out_grads[2], actives[2]
    )
    far_in = Chain(net, add(in_grads[2], far_in), near_dp, joins=[])
    far_out = Chain(net, add(out_grads[2], far_out), near_dp, joins=[])
    far_out.start()
    ranks = range(4)
    grad_resid, grad_branch, grad_mixed, joined = mlp_back(
        [hiddens[r] for r in ranks], [ins[r] for r in ranks],
        proj_weight, resid, grad_low, vectors,
    )
    grad_branch, grad_mixed = meet([far_out], grad_branch, grad_mixed)
    far_in.start()
    cross_out = net.swap(far_out.value, outer)
    proj_weight_grad = dot(mixed, grad_branch, 0, 0).astype(BF16)

    packed, pair_grads, pair_sums = {}, {}, {}

    def back(pair, grad):
        packed[pair], pair_grads[pair], pair_sums[pair] = attend_back(
            qkv, mixed, grad, totals, kept_col, cosine, sine, normed_one, slots, pair
        )

    def group(*members):
        value = jnp.concatenate(members, axis=1) if len(members) > 1 else members[0]
        return Chain(net, value, [inner, outer] + near_dp, far_dp)

    def begin(*chains):
        for chain in chains:
            chain.start()

    back(0, grad_mixed)
    grad_mixed, proj_weight_grad, pair_grads[0] = tie(
        grad_mixed, proj_weight_grad, pair_grads[0]
    )
    group_a = group(proj_weight_grad, pair_grads[0])
    begin(group_a)
    back(1, grad_mixed)
    grad_mixed, cross_out, pair_grads[1] = meet(
        [far_in, group_a], grad_mixed, cross_out, pair_grads[1]
    )
    out_sum = Chain(
        net, add(near_out.value, cross_out), far_dp[:1], far_dp[1:], far_dp[:1] + near_dp
    )
    cross_in = net.swap(far_in.value, outer)
    begin(out_sum, group_a)
    back(2, grad_mixed)
    grad_mixed, pair_grads[2], pair_grads[1] = meet(
        [out_sum, group_a], grad_mixed, pair_grads[2], pair_grads[1]
    )
    group_b = group(pair_grads[1], pair_grads[2])
    begin(out_sum, group_a, group_b)
    back(3, grad_mixed)
    grad_mixed, cross_in, pair_grads[3] = meet(
        [group_a, group_b], grad_mixed, cross_in, pair_grads[3]
    )
    in_sum = Chain(
        net, add(near_in.value, cross_in), far_dp[:1], far_dp[1:], far_dp[:1] + near_dp
    )
    begin(in_sum, group_a, group_b)
    back(4, grad_mixed)
    grad_mixed, pair_grads[3], pair_grads[4] = meet(
        [out_sum, in_sum, group_a, group_b], grad_mixed, pair_grads[3], pair_grads[4]
    )
    group_c = group(pair_grads[3], pair_grads[4])
    begin(out_sum, in_sum, group_a, group_b, group_c)
    back(5, grad_mixed)
    pair_grads[5], packed[5] = meet(
        [out_sum, group_a, group_b, group_c], pair_grads[5], packed[5]
    )
    group_d = group(pair_grads[5])
    begin(out_sum, group_a, group_b, group_c, group_d)
    input_grad, last_sums = finish(
        [packed[p] for p in range(6)], qkv_weight, rows, grad_resid, first_vectors
    )
    last_sums, actives[0] = meet(
        [in_sum, group_a, group_b, group_c, group_d], last_sums, actives[0]
    )

    parts = jnp.arange(4)[:, None]
    hidden_rows = sum(jnp.where(parts == (own ^ r), bias_grads[r], 0.0) for r in ranks)
    small = jnp.concatenate(
        [
            hidden_rows,
            joined[:4],
            jnp.concatenate([pair_sums[p] for p in range(6)], axis=1)[:5],
            last_sums[:2],
            jnp.zeros((1, width), F32),
        ],
        axis=0,
    )
    small = Chain(net, small, [], [inner, outer] + dp_steps)
    begin(in_sum, group_a, group_b, group_c, group_d, small)
    block_out = mlp_result(
        [actives[r] for r in ranks], [outs[r] for r in ranks], resid, kept_col, vectors
    )
    chains = [in_sum, out_sum, group_a, group_b, group_c, group_d, small]
    (block_out,) = meet(chains, block_out)
    slow = [in_sum, out_sum]
    while any(chain.todo for chain in chains):
        begin(*chains)
        meet([c for c in chains if c not in slow or not any(d.todo for d in chains if d not in slow)])
    fc1_weight_grad, fc2_weight_grad = in_sum.value.astype(F32), out_sum.value.astype(F32)
    small = small.value
    early, late = small[:8], small[8:]
    proj_weight_grad = group_a.value[:, :width].astype(F32)
    blocks = [group_a.value[:, width:], group_b.value, group_c.value, group_d.value]
    per_pair = [
        block[:, at : at + 3 * LANES]
        for block in blocks
        for at in range(0, block.shape[1], 3 * LANES)
    ]
    qkv_weight_grad = jnp.concatenate(
        [pair[:, part * LANES : (part + 1) * LANES] for part in range(3) for pair in per_pair],
        axis=1,
    ).astype(F32)

    fc1_bias_grad = lax.dynamic_slice_in_dim(early, own, 1, 0)[0]
    proj_bias_grad, ln2_gain_grad, ln2_bias_grad, fc2_bias_grad = early[4:]
    turned = late[:2].reshape(2, width // HEAD, 2, HEAD // 2)
    freq_grad = turned[:, :, 1] - turned[:, :, 0]
    qkv_bias_grad = late[2:5].reshape(-1)
    ln1_gain_grad, ln1_bias_grad = late[5], late[6]

    freq_norm = jnp.sqrt(jnp.sum(freq_grad * freq_grad))
    square = jnp.float32(0.0)
    for member in (qkv_weight_grad, proj_weight_grad, late[2:7], early[4:]):
        square = square + jnp.sum(member * member)
    return (
        block_out.reshape(images.shape),
        input_grad.reshape(images.shape),
        ln1_gain_grad,
        ln1_bias_grad,
        qkv_weight_grad,
        qkv_bias_grad,
        freq_grad,
        proj_weight_grad,
        proj_bias_grad,
        ln2_gain_grad,
        ln2_bias_grad,
        fc1_weight_grad,
        fc1_bias_grad,
        fc2_weight_grad,
        fc2_bias_grad,
        freq_norm,
        jnp.sqrt(square),
    )


def solution(mesh):
    rows = P(("dp", "tensor"), None, None)
    whole = P()
    hidden_in, hidden_out = P(None, "tensor"), P("tensor", None)
    return jax.shard_map(
        functools.partial(body, Exchange(mesh)),
        mesh=mesh,
        in_specs=(
            (rows, P(("dp", "tensor"), None))
            + (whole,) * 9
            + (hidden_in, P("tensor"), hidden_out, whole, rows)
        ),
        out_specs=(
            (rows, rows) + (whole,) * 9 + (hidden_in, P("tensor"), hidden_out) + (whole,) * 3
        ),
        check_vma=False,
    )
```

```python
import functools

import jax
import jax.numpy as jnp
from jax import lax
from jax.experimental import pallas as pl
from jax.experimental.pallas import tpu as pltpu
from jax.sharding import PartitionSpec as P

GRID = 24
EPSILON = 1e-06
MASKED_SCORE = 1e30
ROOT_HALF = 0.7071067811865476
DENSITY_SCALE = 0.3989422804014327
F32 = jnp.float32
BF16 = jnp.bfloat16
LANES = 128
HEAD = 64
HIDDEN_TILE = 256
PARAMS = pltpu.CompilerParams(vmem_limit_bytes=56 << 20)


def dot(left, right, left_dim=1, right_dim=0):
    return lax.dot_general(
        left, right, (((left_dim,), (right_dim,)), ((), ())), preferred_element_type=F32
    )


def normalize(row_data):
    row_mean = jnp.mean(row_data, axis=-1, keepdims=True)
    centred = row_data - row_mean
    inverse = lax.rsqrt(jnp.mean(centred * centred, axis=-1, keepdims=True) + EPSILON)
    return (centred * inverse, inverse)


def norm_back(grad_unit, unit_rows, inverse):
    return inverse * (
        grad_unit
        - jnp.mean(grad_unit, axis=-1, keepdims=True)
        - unit_rows * jnp.mean(grad_unit * unit_rows, axis=-1, keepdims=True)
    )


def swap_halves(tile):
    lane = lax.broadcasted_iota(jnp.int32, (1, LANES), 1)
    first = (lane % HEAD) < HEAD // 2
    return jnp.where(
        first, pltpu.roll(tile, LANES - HEAD // 2, 1), pltpu.roll(tile, HEAD // 2, 1)
    )


def as_row(ref):
    return ref[...].astype(F32).reshape(1, -1)


def column_sum(values):
    return jnp.sum(values, axis=0, keepdims=True)


def stack_rows(members):
    width = members[0].shape[1]
    row = lax.broadcasted_iota(jnp.int32, (8, width), 0)
    total = jnp.zeros((8, width), F32)
    for at, member in enumerate(members):
        total = jnp.where(row == at, member, total)
    return total


def shape(dims, dtype=BF16):
    return jax.ShapeDtypeStruct(dims, dtype)


def fixed(*dims):
    return pl.BlockSpec(dims, lambda *_: (0,) * len(dims))


def cost(flops, moved, steep=0):
    return pl.CostEstimate(flops=flops, bytes_accessed=moved, transcendentals=steep)


def qkv_kernel(
    x_ref, gain_ref, shift_ref, bias_ref, freq_ref, weight_ref,
    normed_ref, qkv_ref, cos_ref, sin_ref, lanes_ref,
):
    tile, width = x_ref.shape
    across_count = tile // GRID

    @pl.when(pl.program_id(1) == 0)
    def _():
        half = HEAD // 2
        for head in range(width // HEAD):
            for at in (head * HEAD, head * HEAD + half):
                lanes_ref[0:1, at : at + half] = freq_ref[0, head : head + 1, :]
                lanes_ref[1:2, at : at + half] = freq_ref[1, head : head + 1, :]
        first = (pl.program_id(0) * across_count).astype(F32)
        padded = -(-across_count // 8) * 8
        across = first + lax.broadcasted_iota(jnp.int32, (padded, width), 0).astype(F32)
        down = lax.broadcasted_iota(jnp.int32, (GRID, width), 0).astype(F32)
        across = across * lanes_ref[0:1, :]
        down = down * lanes_ref[1:2, :]
        cos_a, sin_a, cos_d, sin_d = jnp.cos(across), jnp.sin(across), jnp.cos(down), jnp.sin(down)
        lane = lax.broadcasted_iota(jnp.int32, (1, width), 1)
        sign = jnp.where((lane % HEAD) < HEAD // 2, -1.0, 1.0)
        for at in range(across_count):
            rows = slice(at * GRID, (at + 1) * GRID)
            one_cos, one_sin = cos_a[at : at + 1], sin_a[at : at + 1]
            cos_ref[rows, :] = one_cos * cos_d - one_sin * sin_d
            sin_ref[rows, :] = (one_sin * cos_d + one_cos * sin_d) * sign

    unit, _ = normalize(x_ref[...].astype(F32))
    normed = (unit * as_row(gain_ref) + as_row(shift_ref)).astype(BF16)
    normed_ref[...] = normed
    bias = as_row(bias_ref)
    for part in range(3):
        cols = slice(part * width, (part + 1) * width)
        packed = dot(normed, weight_ref[:, cols]) + bias[:, cols]
        for at in range(0, width, LANES):
            piece = packed[:, at : at + LANES]
            if part < 2:
                cosine, sine = cos_ref[:, at : at + LANES], sin_ref[:, at : at + LANES]
                piece = piece * cosine + swap_halves(piece) * sine
            if part == 0:
                piece = piece * (HEAD**-0.5)
            qkv_ref[:, part * width + at : part * width + at + LANES] = piece.astype(BF16)


def project_qkv(rows, gain, shift, bias, frequencies, weight, slots):
    row_count, width = rows.shape
    halves = 2
    tile = slots // halves
    row_block = lambda cols: pl.BlockSpec((tile, cols), lambda h, n: (n * halves + h, 0))
    table = pl.BlockSpec((tile, width), lambda h, n: (h, 0))
    return pl.pallas_call(
        qkv_kernel,
        grid=(halves, row_count // slots),
        in_specs=[
            row_block(width),
            fixed(width),
            fixed(width),
            fixed(3 * width),
            fixed(*frequencies.shape),
            fixed(*weight.shape),
        ],
        out_specs=[row_block(width), row_block(3 * width), table, table],
        out_shape=[
            shape((row_count, width)),
            shape((row_count, 3 * width)),
            shape((slots, width), F32),
            shape((slots, width), F32),
        ],
        scratch_shapes=[pltpu.VMEM((8, width), F32)],
        cost_estimate=cost(6 * row_count * width * width, row_count * width * 14),
        compiler_params=PARAMS,
    )(rows, gain, shift, bias, frequencies, weight)


def attend_kernel(q_ref, k_ref, v_ref, mask_ref, mixed_ref, total_ref):
    low = lax.broadcasted_iota(jnp.int32, (1, LANES), 1) < HEAD
    queries, keys, values = q_ref[...], k_ref[...], v_ref[...]
    zero = jnp.zeros_like(queries)
    kept = mask_ref[pl.ds(pl.program_id(0), 1), :].astype(F32)
    mask = (kept - 1.0) * MASKED_SCORE
    mixed, totals = None, []
    for head in range(2):
        keep = low if head == 0 else ~low
        scores = dot(jnp.where(keep, queries, zero), keys, 1, 1) + mask
        row_max = jnp.max(scores, axis=1, keepdims=True)
        weights = jnp.exp(scores - row_max)
        row_total = jnp.sum(weights, axis=1, keepdims=True)
        low_weights = (weights * (1.0 / row_total)).astype(BF16)
        part = dot(low_weights, jnp.where(keep, values, zero))
        mixed = part if mixed is None else mixed + part
        totals.append(row_max + jnp.log(row_total))
    mixed_ref[...] = mixed.astype(BF16)
    total_ref[...] = jnp.where(low, totals[0], totals[1])


def attend(qkv, keep_mask, slots):
    row_count, width = qkv.shape[0], qkv.shape[1] // 3
    images, pairs = row_count // slots, width // LANES
    block = lambda part: pl.BlockSpec((slots, LANES), lambda i, p: (i, p + part * pairs))
    return pl.pallas_call(
        attend_kernel,
        grid=(images, pairs),
        in_specs=[
            block(0),
            block(1),
            block(2),
            fixed(*keep_mask.shape),
        ],
        out_specs=[block(0), block(0)],
        out_shape=[shape((row_count, width)), shape((row_count, width), F32)],
        cost_estimate=cost(
            16 * row_count * slots * width, row_count * width * 12, row_count * slots * 2 * pairs
        ),
        compiler_params=PARAMS,
    )(qkv, qkv, qkv, keep_mask)


def project_kernel(
    mixed_ref, x_ref, grad_ref, mask_ref, bias_ref, gain_ref, shift_ref, weight_ref,
    resid_ref, normed_ref, low_ref, kept_ref,
):
    row = mask_ref[pl.ds(pl.program_id(0), 1), :].astype(F32)
    kept = jnp.transpose(jnp.broadcast_to(row, (8, row.shape[1])))[:, 0:1]
    resid = x_ref[...].astype(F32) + dot(mixed_ref[...], weight_ref[...]) + as_row(bias_ref)
    unit, _ = normalize(resid)
    resid_ref[...] = resid
    normed_ref[...] = (unit * as_row(gain_ref) + as_row(shift_ref)).astype(BF16)
    low_ref[...] = (kept * grad_ref[...].astype(F32)).astype(BF16)
    kept_ref[...] = kept


def project_out(mixed, rows, out_grad, keep_mask, bias, gain, shift, weight):
    row_count, width = rows.shape
    images, slots = keep_mask.shape
    block = pl.BlockSpec((slots, width), lambda i: (i, 0))
    return pl.pallas_call(
        project_kernel,
        grid=(images,),
        in_specs=[block, block, block, fixed(images, slots)]
        + [fixed(width)] * 3
        + [fixed(*weight.shape)],
        out_specs=[block, block, block, pl.BlockSpec((slots, 1), lambda i: (i, 0))],
        out_shape=[
            shape((row_count, width), F32),
            shape((row_count, width)),
            shape((row_count, width)),
            shape((row_count, 1), F32),
        ],
        cost_estimate=cost(2 * row_count * width * width, row_count * width * 14),
        compiler_params=PARAMS,
    )(mixed, rows, out_grad, keep_mask, bias, gain, shift, weight)


def hidden_kernel(
    normed_ref, grad_ref, in_ref, bias_ref, out_ref,
    active_ref, hidden_ref, in_grad_ref, out_grad_ref, bias_grad_ref,
):
    normed, grad = normed_ref[...], grad_ref[...]
    hidden = dot(normed, in_ref[...]) + bias_ref[...]
    grad_active = dot(grad, out_ref[...], 1, 1)
    half = 0.5 * (1.0 + lax.erf(hidden * ROOT_HALF))
    active = (hidden * half).astype(BF16)
    slope = half + hidden * jnp.exp(-0.5 * hidden * hidden) * DENSITY_SCALE
    grad_hidden = (grad_active * slope).astype(BF16)
    active_ref[...] = active
    hidden_ref[...] = grad_hidden
    in_grad_ref[...] = dot(normed, grad_hidden, 0, 0).astype(BF16)
    out_grad_ref[...] = dot(active, grad, 0, 0).astype(BF16)
    bias_grad_ref[...] = column_sum(grad_hidden.astype(F32))


def hidden_units(normed, grad, weight_in, bias_in, weight_out):
    row_count, width = normed.shape
    units = weight_in.shape[1]
    tile = HIDDEN_TILE
    cols = lambda rows: pl.BlockSpec((rows, tile), lambda i: (0, i))
    rows = pl.BlockSpec((tile, width), lambda i: (i, 0))
    return pl.pallas_call(
        hidden_kernel,
        grid=(units // tile,),
        in_specs=[
            fixed(row_count, width), fixed(row_count, width), cols(width), cols(1), rows
        ],
        out_specs=[cols(row_count), cols(row_count), cols(width), rows, cols(1)],
        out_shape=[
            shape((row_count, units)),
            shape((row_count, units)),
            shape((width, units)),
            shape((units, width)),
            shape((1, units), F32),
        ],
        cost_estimate=cost(
            8 * row_count * width * units, row_count * width * 8 + width * units * 8,
            2 * row_count * units,
        ),
        compiler_params=PARAMS,
    )(normed, grad, weight_in, bias_in, weight_out)


def mlp_out_kernel(*refs):
    actives, outs = refs[0:4], refs[4:8]
    resid_ref, kept_ref, bias_ref = refs[8:11]
    block_ref = refs[-1]
    mlp_out = sum(dot(a[...], w[...]) for a, w in zip(actives, outs))
    block_ref[...] = (kept_ref[...] * (resid_ref[...] + mlp_out + as_row(bias_ref))).astype(BF16)


def mlp_back_kernel(*refs):
    hiddens, ins = refs[0:4], refs[4:8]
    proj_ref, resid_ref, low_ref, gain_ref = refs[8:12]
    grad_ref, branch_ref, mixed_ref, sums_ref = refs[12:]
    grad_normed = sum(dot(h[...], w[...], 1, 1) for h, w in zip(hiddens, ins))
    unit, inverse = normalize(resid_ref[...])
    grad_rows = low_ref[...].astype(F32)
    grad = grad_rows + norm_back(grad_normed * as_row(gain_ref), unit, inverse)
    branch = grad.astype(BF16)
    grad_ref[...] = grad
    branch_ref[...] = branch
    mixed_ref[...] = dot(branch, proj_ref[...], 1, 1).astype(BF16)
    sums = stack_rows(
        [
            column_sum(branch.astype(F32)),
            column_sum(grad_normed * unit),
            column_sum(grad_normed),
            column_sum(grad_rows),
        ]
    )

    @pl.when(pl.program_id(0) == 0)
    def _():
        sums_ref[...] = sums

    @pl.when(pl.program_id(0) > 0)
    def _():
        sums_ref[...] += sums


def mlp_result(actives, outs, resid, kept_col, bias, image, slots, earlier):
    row_count, width = resid.shape
    tile = slots // 2
    block = pl.BlockSpec((tile, width), lambda i: (2 * image + i, 0))
    return pl.pallas_call(
        mlp_out_kernel,
        grid=(2,),
        in_specs=[block] * 4
        + [fixed(width, width)] * 4
        + [block, pl.BlockSpec((tile, 1), lambda i: (2 * image + i, 0)), fixed(width)]
        + [pl.BlockSpec(memory_space=pl.ANY)] * len(earlier),
        out_specs=block,
        out_shape=shape((row_count, width)),
        input_output_aliases={11: 0} if earlier else {},
        cost_estimate=cost(8 * slots * width * width, slots * width * 14),
        compiler_params=PARAMS,
    )(*actives, *outs, resid, kept_col, bias, *earlier)


def mlp_back(hiddens, ins, proj_weight, resid, grad_low, gain):
    row_count, width = resid.shape
    tile = row_count // 4
    block = pl.BlockSpec((tile, width), lambda i: (i, 0))
    return pl.pallas_call(
        mlp_back_kernel,
        grid=(4,),
        in_specs=[block] * 4
        + [fixed(width, width)] * 5
        + [block, block, fixed(width)],
        out_specs=[block, block, block, fixed(8, width)],
        out_shape=[
            shape((row_count, width), F32),
            shape((row_count, width)),
            shape((row_count, width)),
            shape((8, width), F32),
        ],
        cost_estimate=cost(10 * row_count * width * width, row_count * width * 22),
        compiler_params=PARAMS,
    )(*hiddens, *ins, proj_weight, resid, grad_low, gain)


def attend_back_kernel(
    q_ref, k_ref, v_ref, mixed_ref, grad_ref, total_ref, kept_ref, cos_ref, sin_ref, *refs
):
    packed_ref, sums_ref = refs[-2:]
    slots = q_ref.shape[0]
    low = lax.broadcasted_iota(jnp.int32, (1, LANES), 1) < HEAD
    q, k, v, grad_mixed = q_ref[...], k_ref[...], v_ref[...], grad_ref[...]
    zero = jnp.zeros_like(q)
    mask = (kept_ref[...] - 1.0) * MASKED_SCORE
    product = jnp.transpose(grad_mixed.astype(F32) * mixed_ref[...].astype(F32))
    totals = jnp.transpose(total_ref[...])
    grad_q = grad_k = grad_v = None
    for head in range(2):
        keep = low if head == 0 else ~low
        q_head = jnp.where(keep, q, zero)
        grad_head = jnp.where(keep, grad_mixed, zero)
        k_head = jnp.where(keep, k, zero)
        total = totals[head * HEAD : head * HEAD + 1]
        inner = column_sum(product[head * HEAD : (head + 1) * HEAD])
        weights = jnp.exp((dot(k, q_head, 1, 1) + mask) - total)
        grad_weights = dot(v, grad_head, 1, 1)
        grad_scores = (weights * (grad_weights - inner)).astype(BF16)
        part_v = dot(weights.astype(BF16), grad_head)
        part_k = dot(grad_scores, q_head)
        part_q = dot(grad_scores, k_head, 0, 0)
        grad_v = part_v if grad_v is None else grad_v + part_v
        grad_k = part_k if grad_k is None else grad_k + part_k
        grad_q = part_q if grad_q is None else grad_q + part_q
    turn = grad_q * swap_halves(q.astype(F32)) + grad_k * swap_halves(k.astype(F32))
    slot = lax.broadcasted_iota(jnp.int32, (slots, 1), 0)
    across = slot // GRID
    down = slot - across * GRID
    cosine, sine = cos_ref[...], sin_ref[...]
    grad_q = grad_q * (HEAD**-0.5)
    grad_q = (grad_q * cosine - swap_halves(grad_q) * sine).astype(BF16)
    grad_k = (grad_k * cosine - swap_halves(grad_k) * sine).astype(BF16)
    packed = jnp.concatenate([grad_q, grad_k, grad_v.astype(BF16)], axis=1)
    packed_ref[...] = packed
    parts = column_sum(packed.astype(F32))
    sums = stack_rows(
        [
            column_sum(turn * across.astype(F32)),
            column_sum(turn * down.astype(F32)),
            parts[:, :LANES],
            parts[:, LANES : 2 * LANES],
            parts[:, 2 * LANES :],
        ]
    )

    @pl.when(pl.program_id(0) == 0)
    def _():
        sums_ref[...] = sums

    @pl.when(pl.program_id(0) > 0)
    def _():
        sums_ref[...] += sums


def attend_back(
    qkv, mixed, grad_mixed, totals, kept_col, cosine, sine, slots, pair, count, at, earlier
):
    row_count, width = mixed.shape
    images, pairs = row_count // slots, width // LANES
    block = lambda part: pl.BlockSpec((slots, LANES), lambda i: (i, pair + part * pairs))
    table = pl.BlockSpec((slots, LANES), lambda i: (0, pair))
    return pl.pallas_call(
        attend_back_kernel,
        grid=(images,),
        in_specs=[
            block(0), block(1), block(2), block(0), block(0), block(0),
            pl.BlockSpec((slots, 1), lambda i: (i, 0)),
            table,
            table,
        ] + [pl.BlockSpec(memory_space=pl.ANY)] * len(earlier),
        out_specs=[pl.BlockSpec((slots, 3 * LANES), lambda i: (i, at)), fixed(8, LANES)],
        out_shape=[shape((row_count, count * 3 * LANES)), shape((8, LANES), F32)],
        input_output_aliases={9: 0} if earlier else {},
        cost_estimate=cost(
            40 * row_count * slots * LANES, row_count * LANES * 30, row_count * slots * 2
        ),
        compiler_params=PARAMS,
    )(qkv, qkv, qkv, mixed, grad_mixed, totals, kept_col, cosine, sine, *earlier)


def finish_kernel(count, *refs):
    packed, (weight_ref, x_ref, grad_ref, gain_ref) = refs[:count], refs[count : count + 4]
    more, (input_ref, sums_ref) = refs[count + 4 : -2], refs[-2:]
    pieces = [p[:, at : at + 3 * LANES] for p in packed for at in range(0, p.shape[1], 3 * LANES)]
    full = jnp.concatenate(
        [p[:, part * LANES : (part + 1) * LANES] for part in range(3) for p in pieces], axis=1
    )
    grad_normed = dot(full, weight_ref[...], 1, 1)
    unit, inverse = normalize(x_ref[...].astype(F32))
    input_ref[...] = (
        grad_ref[...] + norm_back(grad_normed * as_row(gain_ref), unit, inverse)
    ).astype(BF16)
    members = [column_sum(grad_normed * unit), column_sum(grad_normed)]
    step = pl.program_id(0)
    if not more:

        @pl.when(step == 0)
        def _():
            sums_ref[...] = stack_rows(members)

        @pl.when(step > 0)
        def _():
            sums_ref[...] += stack_rows(members)

    else:
        own_ref, joined_ref, hidden_refs, pair_refs, before_ref = (
            more[0], more[1], more[2:6], more[6:-2], more[-2],
        )

        @pl.when(step == 0)
        def _():
            row = lax.broadcasted_iota(jnp.int32, (8, 1), 0)
            top = jnp.zeros((8, input_ref.shape[1]), F32)
            for r, hidden in enumerate(hidden_refs):
                top = jnp.where(row == (own_ref[0] ^ r), hidden[...], top)
            low = jnp.where(row < 4, 0.0, pltpu.roll(joined_ref[...], 4, 0))
            sums_ref[0:8, :] = top + low
            pairs = jnp.concatenate([p[...] for p in pair_refs], axis=1)
            ends = pltpu.roll(before_ref[...] + stack_rows(members), 5, 0)
            sums_ref[8:16, :] = jnp.where(row < 5, pairs, ends)

        @pl.when(step > 0)
        def _():
            sums_ref[8:16, :] += pltpu.roll(stack_rows(members), 5, 0)


def finish(packed, weight, rows, grad_resid, gain, image, slots, more):
    row_count, width = rows.shape
    tile = slots // 2
    block = lambda cols: pl.BlockSpec((tile, cols), lambda i: (2 * image + i, 0))
    more_specs = [fixed(*m.shape) for m in more]
    if more:
        more_specs[0] = pl.BlockSpec(memory_space=pltpu.SMEM)
        more_specs[-1] = pl.BlockSpec(memory_space=pl.ANY)
    count = len(packed)
    sums = 16 if more else 8
    return pl.pallas_call(
        functools.partial(finish_kernel, count),
        grid=(2,),
        in_specs=[block(p.shape[1]) for p in packed]
        + [fixed(*weight.shape), block(width), block(width), fixed(width)]
        + more_specs,
        out_specs=[block(width), fixed(sums, width)],
        out_shape=[shape((row_count, width)), shape((sums, width), F32)],
        input_output_aliases={count + 3 + len(more): 0} if more else {},
        cost_estimate=cost(6 * slots * width * width, slots * width * 14),
        compiler_params=PARAMS,
    )(*packed, weight, rows, grad_resid, gain, *more)


def final_kernel(own_ref, small_ref, proj_ref, *refs):
    blocks, outputs = refs[:-13], refs[-13:]
    (
        weight_out, proj_out, gain1_ref, shift1_ref, bias_ref, freq_ref, proj_bias_ref,
        gain2_ref, shift2_ref, hidden_ref, out_bias_ref, freq_norm_ref, rest_norm_ref,
    ) = outputs[:13]
    width = proj_ref.shape[1]
    step = pl.program_id(0)
    square = jnp.zeros((1, 1), F32)

    def total(values):
        return jnp.sum(jnp.sum(values * values, axis=0, keepdims=True), axis=1, keepdims=True)

    proj = proj_ref[...].astype(F32)
    proj_out[...] = proj
    square = square + total(proj)
    pair = 0
    for block in blocks:
        for at in range(0, block.shape[1], 3 * LANES):
            for part in range(3):
                piece = block[:, at + part * LANES : at + (part + 1) * LANES].astype(F32)
                first = part * width + pair * LANES
                weight_out[:, first : first + LANES] = piece
                square = square + total(piece)
            pair += 1

    @pl.when(step == 0)
    def _():
        small = small_ref[...]
        hidden_ref[...] = small_ref[pl.ds(own_ref[0], 1), :].reshape(width)
        for at, ref in enumerate((proj_bias_ref, gain2_ref, shift2_ref, out_bias_ref)):
            ref[...] = small[4 + at]
        bias_ref[...] = jnp.concatenate([small[10], small[11], small[12]], axis=0)
        gain1_ref[...] = small[13]
        shift1_ref[...] = small[14]
        freq_square = jnp.zeros((1, 1), F32)
        half = HEAD // 2
        for head in range(width // HEAD):
            at = head * HEAD
            for axis in range(2):
                row = slice(8 + axis, 9 + axis)
                turned = small_ref[row, at + half : at + HEAD] - small_ref[row, at : at + half]
                freq_ref[axis, head : head + 1, :] = turned
                freq_square = freq_square + total(turned)
        freq_norm_ref[...] = jnp.sqrt(freq_square)
        rest_norm_ref[...] = square + total(small[4:8]) + total(small[10:15])

    @pl.when(step > 0)
    def _():
        rest_norm_ref[...] += square

    @pl.when(step == pl.num_programs(0) - 1)
    def _():
        rest_norm_ref[...] = jnp.sqrt(rest_norm_ref[...])


def final(own, small, proj, blocks, freq_shape):
    depth, width = proj.shape
    tile = depth // 4
    row_block = lambda cols: pl.BlockSpec((tile, cols), lambda i: (i, 0))
    vector = (shape((width,), F32), fixed(width))
    outputs = [
        (shape((depth, 3 * width), F32), row_block(3 * width)),
        (shape((depth, width), F32), row_block(width)),
        vector,
        vector,
        (shape((3 * width,), F32), fixed(3 * width)),
        (shape(freq_shape, F32), fixed(*freq_shape)),
        vector,
        vector,
        vector,
        vector,
        vector,
        (shape((1, 1), F32), fixed(1, 1)),
        (shape((1, 1), F32), fixed(1, 1)),
    ]
    return pl.pallas_call(
        final_kernel,
        grid=(4,),
        in_specs=[
            pl.BlockSpec(memory_space=pltpu.SMEM),
            fixed(*small.shape),
            row_block(width),
        ]
        + [row_block(b.shape[1]) for b in blocks],
        out_specs=[spec for _, spec in outputs],
        out_shape=[dims for dims, _ in outputs],
        cost_estimate=cost(depth * width * 16, depth * width * 24),
        compiler_params=PARAMS,
    )(own, small, proj, *blocks)


class Exchange:
    def __init__(self, mesh):
        self.sizes = dict(mesh.shape)

    def bits(self, axis):
        return [(axis, 1 << b) for b in range(self.sizes[axis].bit_length() - 1)]

    def swap(self, value, step):
        axis, bit = step
        pairs = [(i, i ^ bit) for i in range(self.sizes[axis])]
        return lax.ppermute(value, axis, pairs)

    def side(self, step):
        axis, bit = step
        return (lax.axis_index(axis) // bit) % 2

    def half(self, value, step, mine):
        size = value.shape[0] // 2
        side = self.side(step)
        return lax.dynamic_slice_in_dim(value, (side if mine else 1 - side) * size, size, 0)

    def join(self, mine, other, step):
        first = self.side(step) == 0
        return jnp.concatenate(
            [jnp.where(first, mine, other), jnp.where(first, other, mine)], axis=0
        )


def add(*members):
    return sum(member.astype(F32) for member in members).astype(BF16)


def tie(*members):
    return lax.optimization_barrier(members)


class Chain:
    def __init__(self, net, value, halving, full=(), joins=None):
        joins = list(reversed(halving)) if joins is None else joins
        self.net, self.value = net, value
        self.todo = [("halve", s) for s in halving] + [("full", s) for s in full]
        self.todo += [("join", s) for s in joins]
        self.flight = None

    def start(self):
        if not self.todo or self.flight is not None:
            return
        kind, step = self.todo[0]
        sent = self.net.half(self.value, step, False) if kind == "halve" else self.value
        self.flight = self.net.swap(sent, step)

    def end(self):
        if self.flight is None:
            return
        kind, step = self.todo.pop(0)
        if kind == "halve":
            self.value = add(self.net.half(self.value, step, True), self.flight)
        elif kind == "full":
            total = self.value.astype(F32) + self.flight.astype(F32)
            self.value = total.astype(self.value.dtype)
        else:
            self.value = self.net.join(self.value, self.flight, step)
        self.flight = None


def meet(chains, *outputs):
    flights = [c.flight for c in chains if c.flight is not None]
    tied = tie(flights, outputs)
    landed = list(tied[0])
    for chain in chains:
        if chain.flight is not None:
            chain.flight = landed.pop(0)
            chain.end()
    return tied[1]


def body(
    net,
    images,
    keep_mask,
    ln1_gain,
    ln1_bias,
    qkv_weight,
    qkv_bias,
    frequencies,
    proj_weight,
    proj_bias,
    ln2_gain,
    ln2_bias,
    fc1_weight,
    fc1_bias,
    fc2_weight,
    fc2_bias,
    out_grad,
):
    image_count, slots, width = images.shape
    row_count = image_count * slots
    inner, outer = net.bits("tensor")
    dp_steps = net.bits("dp")
    near_dp, far_dp = dp_steps[:1], dp_steps[1:]

    ins, outs = {0: fc1_weight}, {0: fc2_weight}
    ins[2], outs[2] = net.swap(fc1_weight, outer), net.swap(fc2_weight, outer)
    ins[1], outs[1] = net.swap(fc1_weight, inner), net.swap(fc2_weight, inner)
    biases = {0: fc1_bias.astype(F32).reshape(1, -1)}
    biases[1], biases[2] = net.swap(biases[0], inner), net.swap(biases[0], outer)
    biases[3] = net.swap(biases[2], inner)

    rows = images.reshape(row_count, width)
    normed_one, qkv, cosine, sine = project_qkv(
        rows, ln1_gain, ln1_bias, qkv_bias, frequencies, qkv_weight, slots
    )
    mixed, totals = attend(qkv, keep_mask, slots)
    resid, normed_two, grad_low, kept_col = project_out(
        mixed, rows, out_grad.reshape(row_count, width), keep_mask,
        proj_bias, ln2_gain, ln2_bias, proj_weight,
    )

    actives, hiddens, in_grads, out_grads, bias_grads = {}, {}, {}, {}, {}

    def chunk(r, normed, grad):
        results = hidden_units(normed, grad, ins[r], biases[r], outs[r])
        actives[r], hiddens[r], in_grads[r], out_grads[r], bias_grads[r] = results

    normed_two, grad_low, ins[1], outs[1] = tie(normed_two, grad_low, ins[1], outs[1])
    chunk(1, normed_two, grad_low)
    normed_two, in_grads[1], out_grads[1], ins[2], outs[2] = tie(
        normed_two, in_grads[1], out_grads[1], ins[2], outs[2]
    )
    near_in, near_out = net.swap(in_grads[1], inner), net.swap(out_grads[1], inner)
    ins[3], outs[3] = net.swap(ins[2], inner), net.swap(outs[2], inner)
    chunk(0, normed_two, grad_low)
    normed_two, in_grads[0], out_grads[0], near_in, near_out, ins[3], outs[3] = tie(
        normed_two, in_grads[0], out_grads[0], near_in, near_out, ins[3], outs[3]
    )
    near_in = Chain(net, add(in_grads[0], near_in), near_dp, joins=[])
    near_out = Chain(net, add(out_grads[0], near_out), near_dp, joins=[])
    near_out.start()
    chunk(3, normed_two, grad_low)
    normed_two, in_grads[3], out_grads[3] = meet(
        [near_out], normed_two, in_grads[3], out_grads[3]
    )
    far_in, far_out = net.swap(in_grads[3], inner), net.swap(out_grads[3], inner)
    near_in.start()
    chunk(2, normed_two, grad_low)
    far_in, far_out, in_grads[2], out_grads[2], actives[2] = meet(
        [near_in], far_in, far_out, in_grads[2], out_grads[2], actives[2]
    )
    far_in = Chain(net, add(in_grads[2], far_in), near_dp, joins=[])
    far_out = Chain(net, add(out_grads[2], far_out), near_dp, joins=[])
    far_out.start()
    ranks = range(4)
    grad_resid, grad_branch, grad_mixed, joined = mlp_back(
        [hiddens[r] for r in ranks], [ins[r] for r in ranks],
        proj_weight, resid, grad_low, ln2_gain,
    )
    grad_branch, grad_mixed = meet([far_out], grad_branch, grad_mixed)
    far_in.start()
    cross_out = net.swap(far_out.value, outer)
    proj_grad = dot(mixed, grad_branch, 0, 0).astype(BF16)

    pair_sums = {}

    def back(pair, grad, count=1, at=0, earlier=()):
        packed, pair_sums[pair] = attend_back(
            qkv, mixed, grad, totals, kept_col, cosine, sine, slots, pair, count, at, earlier
        )
        return packed

    def weight_grad(packed):
        return dot(normed_one, packed, 0, 0).astype(BF16)

    def group(value):
        return Chain(net, value, [inner, outer] + near_dp, far_dp)

    def begin(*chains):
        for chain in chains:
            chain.start()

    def whole(value):
        return Chain(net, value, far_dp[:1], far_dp[1:], far_dp[:1] + near_dp)

    packed_a = back(0, grad_mixed)
    grad_mixed, *first_grads = tie(grad_mixed, proj_grad, weight_grad(packed_a))
    first_grads = lax.psum(first_grads, ("dp", "tensor"))
    packed_b = back(1, grad_mixed, 2, 0)
    grad_mixed, cross_out, packed_b = meet([far_in], grad_mixed, cross_out, packed_b)
    out_sum = whole(add(near_out.value, cross_out))
    cross_in = net.swap(far_in.value, outer)
    begin(out_sum)
    packed_b = back(2, grad_mixed, 2, 1, [packed_b])
    grad_b = weight_grad(packed_b)
    grad_mixed, grad_b = meet([out_sum], grad_mixed, grad_b)
    group_b = group(grad_b)
    begin(out_sum, group_b)
    packed_c = back(3, grad_mixed, 2, 0)
    grad_mixed, cross_in, packed_c = meet([group_b], grad_mixed, cross_in, packed_c)
    in_sum = whole(add(near_in.value, cross_in))
    begin(in_sum, group_b)
    packed_c = back(4, grad_mixed, 2, 1, [packed_c])
    grad_c = weight_grad(packed_c)
    grad_mixed, grad_c = meet([out_sum, in_sum, group_b], grad_mixed, grad_c)
    group_c = group(grad_c)
    begin(out_sum, in_sum, group_b, group_c)
    packed_d = back(5, grad_mixed)
    grad_d = weight_grad(packed_d)
    packed_d, grad_d = meet([out_sum, group_b, group_c], packed_d, grad_d)
    group_d = group(grad_d)
    begin(out_sum, group_b, group_c, group_d)

    packed = [packed_a, packed_b, packed_c, packed_d]
    own_list = lax.axis_index("tensor").astype(jnp.int32).reshape(1)
    input_grad, half_sums = finish(
        packed, qkv_weight, rows, grad_resid, ln1_gain, 0, slots, ()
    )
    input_grad, half_sums = meet([in_sum, group_b, group_c, group_d], input_grad, half_sums)
    begin(in_sum, group_b, group_c, group_d)
    input_grad, small = finish(
        packed, qkv_weight, rows, grad_resid, ln1_gain, 1, slots,
        [own_list, joined, *[bias_grads[r] for r in ranks], *[pair_sums[p] for p in range(6)],
         half_sums, input_grad],
    )
    small, actives[0] = meet([group_b, group_c, group_d], small, actives[0])
    small = Chain(net, small, [], [inner, outer] + dp_steps)
    begin(group_b, group_c, group_d, small)
    result = lambda image, earlier: mlp_result(
        [actives[r] for r in ranks], [outs[r] for r in ranks],
        resid, kept_col, fc2_bias, image, slots, earlier,
    )
    block_out = result(0, ())
    groups = [group_b, group_c, group_d, small]
    (block_out,) = meet([in_sum, out_sum, *groups], block_out)
    begin(in_sum, *groups)
    block_out = result(1, (block_out,))
    (block_out,) = meet(groups, block_out)
    while any(chain.todo for chain in groups):
        begin(*groups)
        meet(groups)
    meet([in_sum])
    while in_sum.todo or out_sum.todo:
        begin(in_sum, out_sum)
        meet([in_sum, out_sum])

    (
        qkv_weight_grad, proj_weight_grad, ln1_gain_grad, ln1_bias_grad, qkv_bias_grad,
        freq_grad, proj_bias_grad, ln2_gain_grad, ln2_bias_grad, fc1_bias_grad, fc2_bias_grad,
        freq_norm, rest_norm,
    ) = final(
        own_list, small.value, first_grads[0],
        [first_grads[1], group_b.value, group_c.value, group_d.value], frequencies.shape,
    )
    return (
        block_out.reshape(images.shape),
        input_grad.reshape(images.shape),
        ln1_gain_grad,
        ln1_bias_grad,
        qkv_weight_grad,
        qkv_bias_grad,
        freq_grad,
        proj_weight_grad,
        proj_bias_grad,
        ln2_gain_grad,
        ln2_bias_grad,
        in_sum.value.astype(F32),
        fc1_bias_grad,
        out_sum.value.astype(F32),
        fc2_bias_grad,
        freq_norm.reshape(()),
        rest_norm.reshape(()),
    )


def solution(mesh):
    rows = P(("dp", "tensor"), None, None)
    whole = P()
    hidden_in, hidden_out = P(None, "tensor"), P("tensor", None)
    return jax.shard_map(
        functools.partial(body, Exchange(mesh)),
        mesh=mesh,
        in_specs=(
            (rows, P(("dp", "tensor"), None))
            + (whole,) * 9
            + (hidden_in, P("tensor"), hidden_out, whole, rows)
        ),
        out_specs=(
            (rows, rows) + (whole,) * 9 + (hidden_in, P("tensor"), hidden_out) + (whole,) * 3
        ),
        check_vma=False,
    )
```

```python
import functools

import jax
import jax.numpy as jnp
from jax import lax
from jax.experimental import pallas as pl
from jax.experimental.pallas import tpu as pltpu
from jax.sharding import PartitionSpec as P

GRID = 24
EPSILON = 1e-06
MASKED_SCORE = 1e30
ROOT_HALF = 0.7071067811865476
DENSITY_SCALE = 0.3989422804014327
F32 = jnp.float32
BF16 = jnp.bfloat16
LANES = 128
HEAD = 64
HIDDEN_TILE = 256
EMPHASIS = 20
PARAMS = pltpu.CompilerParams(vmem_limit_bytes=56 << 20)


def dot(left, right, left_dim=1, right_dim=0):
    return lax.dot_general(
        left, right, (((left_dim,), (right_dim,)), ((), ())), preferred_element_type=F32
    )


def normalize(row_data):
    row_mean = jnp.mean(row_data, axis=-1, keepdims=True)
    centred = row_data - row_mean
    inverse = lax.rsqrt(jnp.mean(centred * centred, axis=-1, keepdims=True) + EPSILON)
    return (centred * inverse, inverse)


def norm_back(grad_unit, unit_rows, inverse):
    return inverse * (
        grad_unit
        - jnp.mean(grad_unit, axis=-1, keepdims=True)
        - unit_rows * jnp.mean(grad_unit * unit_rows, axis=-1, keepdims=True)
    )


def swap_halves(tile):
    lane = lax.broadcasted_iota(jnp.int32, (1, LANES), 1)
    first = (lane % HEAD) < HEAD // 2
    return jnp.where(
        first, pltpu.roll(tile, LANES - HEAD // 2, 1), pltpu.roll(tile, HEAD // 2, 1)
    )


def as_row(ref):
    return ref[...].astype(F32).reshape(1, -1)


def column_sum(values):
    return jnp.sum(values, axis=0, keepdims=True)


def stack_rows(members):
    width = members[0].shape[1]
    row = lax.broadcasted_iota(jnp.int32, (8, width), 0)
    total = jnp.zeros((8, width), F32)
    for at, member in enumerate(members):
        total = jnp.where(row == at, member, total)
    return total


def shape(dims, dtype=BF16):
    return jax.ShapeDtypeStruct(dims, dtype)


def fixed(*dims):
    return pl.BlockSpec(dims, lambda *_: (0,) * len(dims))


def cost(flops, moved, steep=0):
    return pl.CostEstimate(flops=EMPHASIS * flops, bytes_accessed=moved, transcendentals=steep)


def qkv_kernel(
    x_ref, gain_ref, shift_ref, bias_ref, freq_ref, weight_ref,
    normed_ref, qkv_ref, cos_ref, sin_ref, lanes_ref,
):
    tile, width = x_ref.shape
    across_count = tile // GRID

    @pl.when(pl.program_id(1) == 0)
    def _():
        half = HEAD // 2
        for head in range(width // HEAD):
            for at in (head * HEAD, head * HEAD + half):
                lanes_ref[0:2, at : at + half] = freq_ref[head, :, :]
        first = (pl.program_id(0) * across_count).astype(F32)
        padded = -(-across_count // 8) * 8
        across = first + lax.broadcasted_iota(jnp.int32, (padded, width), 0).astype(F32)
        down = lax.broadcasted_iota(jnp.int32, (GRID, width), 0).astype(F32)
        across = across * lanes_ref[0:1, :]
        down = down * lanes_ref[1:2, :]
        cos_a, sin_a, cos_d, sin_d = jnp.cos(across), jnp.sin(across), jnp.cos(down), jnp.sin(down)
        lane = lax.broadcasted_iota(jnp.int32, (1, width), 1)
        sign = jnp.where((lane % HEAD) < HEAD // 2, -1.0, 1.0)
        for at in range(across_count):
            rows = slice(at * GRID, (at + 1) * GRID)
            one_cos, one_sin = cos_a[at : at + 1], sin_a[at : at + 1]
            cos_ref[rows, :] = one_cos * cos_d - one_sin * sin_d
            sin_ref[rows, :] = (one_sin * cos_d + one_cos * sin_d) * sign

    unit, _ = normalize(x_ref[...].astype(F32))
    normed = (unit * as_row(gain_ref) + as_row(shift_ref)).astype(BF16)
    normed_ref[...] = normed
    bias = as_row(bias_ref)
    for part in range(3):
        cols = slice(part * width, (part + 1) * width)
        packed = dot(normed, weight_ref[:, cols]) + bias[:, cols]
        for at in range(0, width, LANES):
            piece = packed[:, at : at + LANES]
            if part < 2:
                cosine, sine = cos_ref[:, at : at + LANES], sin_ref[:, at : at + LANES]
                piece = piece * cosine + swap_halves(piece) * sine
            if part == 0:
                piece = piece * (HEAD**-0.5)
            qkv_ref[:, part * width + at : part * width + at + LANES] = piece.astype(BF16)


def project_qkv(rows, gain, shift, bias, frequencies, weight, slots):
    row_count, width = rows.shape
    halves = 2
    tile = slots // halves
    row_block = lambda cols: pl.BlockSpec((tile, cols), lambda h, n: (n * halves + h, 0))
    table = pl.BlockSpec((tile, width), lambda h, n: (h, 0))
    return pl.pallas_call(
        qkv_kernel,
        grid=(halves, row_count // slots),
        in_specs=[
            row_block(width),
            fixed(width),
            fixed(width),
            fixed(3 * width),
            fixed(*frequencies.shape),
            fixed(*weight.shape),
        ],
        out_specs=[row_block(width), row_block(3 * width), table, table],
        out_shape=[
            shape((row_count, width)),
            shape((row_count, 3 * width)),
            shape((slots, width), F32),
            shape((slots, width), F32),
        ],
        scratch_shapes=[pltpu.VMEM((8, width), F32)],
        cost_estimate=cost(6 * row_count * width * width, row_count * width * 14),
        compiler_params=PARAMS,
    )(rows, gain, shift, bias, frequencies, weight)


def attend_kernel(q_ref, k_ref, v_ref, mask_ref, mixed_ref, total_ref):
    low = lax.broadcasted_iota(jnp.int32, (1, LANES), 1) < HEAD
    queries, keys, values = q_ref[...], k_ref[...], v_ref[...]
    zero = jnp.zeros_like(queries)
    kept = mask_ref[pl.ds(pl.program_id(0), 1), :].astype(F32)
    mask = (kept - 1.0) * MASKED_SCORE
    mixed, totals = None, []
    for head in range(2):
        keep = low if head == 0 else ~low
        scores = dot(jnp.where(keep, queries, zero), keys, 1, 1) + mask
        row_max = jnp.max(scores, axis=1, keepdims=True)
        weights = jnp.exp(scores - row_max)
        row_total = jnp.sum(weights, axis=1, keepdims=True)
        low_weights = (weights * (1.0 / row_total)).astype(BF16)
        part = dot(low_weights, jnp.where(keep, values, zero))
        mixed = part if mixed is None else mixed + part
        totals.append(row_max + jnp.log(row_total))
    mixed_ref[...] = mixed.astype(BF16)
    total_ref[...] = jnp.where(low, totals[0], totals[1])


def attend(qkv, keep_mask, slots):
    row_count, width = qkv.shape[0], qkv.shape[1] // 3
    images, pairs = row_count // slots, width // LANES
    block = lambda part: pl.BlockSpec((slots, LANES), lambda i, p: (i, p + part * pairs))
    return pl.pallas_call(
        attend_kernel,
        grid=(images, pairs),
        in_specs=[
            block(0),
            block(1),
            block(2),
            fixed(*keep_mask.shape),
        ],
        out_specs=[block(0), block(0)],
        out_shape=[shape((row_count, width)), shape((row_count, width), F32)],
        cost_estimate=cost(
            16 * row_count * slots * width, row_count * width * 12, row_count * slots * 2 * pairs
        ),
        compiler_params=PARAMS,
    )(qkv, qkv, qkv, keep_mask)


def project_kernel(
    mixed_ref, x_ref, grad_ref, mask_ref, bias_ref, gain_ref, shift_ref, weight_ref,
    resid_ref, normed_ref, low_ref, kept_ref,
):
    row = mask_ref[pl.ds(pl.program_id(0), 1), :].astype(F32)
    kept = jnp.transpose(jnp.broadcast_to(row, (8, row.shape[1])))[:, 0:1]
    resid = x_ref[...].astype(F32) + dot(mixed_ref[...], weight_ref[...]) + as_row(bias_ref)
    unit, _ = normalize(resid)
    resid_ref[...] = resid
    normed_ref[...] = (unit * as_row(gain_ref) + as_row(shift_ref)).astype(BF16)
    low_ref[...] = (kept * grad_ref[...].astype(F32)).astype(BF16)
    kept_ref[...] = kept


def project_out(mixed, rows, out_grad, keep_mask, bias, gain, shift, weight):
    row_count, width = rows.shape
    images, slots = keep_mask.shape
    block = pl.BlockSpec((slots, width), lambda i: (i, 0))
    return pl.pallas_call(
        project_kernel,
        grid=(images,),
        in_specs=[block, block, block, fixed(images, slots)]
        + [fixed(width)] * 3
        + [fixed(*weight.shape)],
        out_specs=[block, block, block, pl.BlockSpec((slots, 1), lambda i: (i, 0))],
        out_shape=[
            shape((row_count, width), F32),
            shape((row_count, width)),
            shape((row_count, width)),
            shape((row_count, 1), F32),
        ],
        cost_estimate=cost(2 * row_count * width * width, row_count * width * 14),
        compiler_params=PARAMS,
    )(mixed, rows, out_grad, keep_mask, bias, gain, shift, weight)


def hidden_kernel(
    normed_ref, grad_ref, in_ref, bias_ref, out_ref,
    active_ref, hidden_ref, weights_ref, bias_grad_ref,
):
    normed, grad = normed_ref[...], grad_ref[...]
    hidden = dot(normed, in_ref[...]) + as_row(bias_ref)
    grad_active = dot(grad, out_ref[...], 1, 1)
    half = 0.5 * (1.0 + lax.erf(hidden * ROOT_HALF))
    active = (hidden * half).astype(BF16)
    slope = half + hidden * jnp.exp(-0.5 * hidden * hidden) * DENSITY_SCALE
    grad_hidden = (grad_active * slope).astype(BF16)
    active_ref[...] = active
    hidden_ref[...] = grad_hidden
    weights_ref[0] = dot(normed, grad_hidden, 0, 0).astype(BF16)
    weights_ref[1] = dot(grad, active, 0, 0).astype(BF16)
    bias_grad_ref[...] = column_sum(grad_hidden.astype(F32))


def hidden_units(normed, grad, weight_in, bias_in, weight_out):
    row_count, width = normed.shape
    units = weight_in.shape[1]
    tile = HIDDEN_TILE
    cols = lambda rows: pl.BlockSpec((rows, tile), lambda i: (0, i))
    rows = pl.BlockSpec((tile, width), lambda i: (i, 0))
    return pl.pallas_call(
        hidden_kernel,
        grid=(units // tile,),
        in_specs=[
            fixed(row_count, width), fixed(row_count, width), cols(width),
            pl.BlockSpec((tile,), lambda i: (i,)), rows
        ],
        out_specs=[
            cols(row_count),
            cols(row_count),
            pl.BlockSpec((2, width, tile), lambda i: (0, 0, i)),
            cols(1),
        ],
        out_shape=[
            shape((row_count, units)),
            shape((row_count, units)),
            shape((2, width, units)),
            shape((1, units), F32),
        ],
        cost_estimate=cost(
            8 * row_count * width * units, row_count * width * 8 + width * units * 8,
            2 * row_count * units,
        ),
        compiler_params=PARAMS,
    )(normed, grad, weight_in, bias_in, weight_out)


def mlp_out_kernel(*refs):
    actives, outs = refs[0:4], refs[4:8]
    resid_ref, kept_ref, bias_ref = refs[8:11]
    block_ref = refs[-1]
    mlp_out = sum(dot(a[...], w[...]) for a, w in zip(actives, outs))
    block_ref[...] = (kept_ref[...] * (resid_ref[...] + mlp_out + as_row(bias_ref))).astype(BF16)


def mlp_back_kernel(*refs):
    hiddens, ins = refs[0:4], refs[4:8]
    proj_ref, resid_ref, low_ref, gain_ref = refs[8:12]
    grad_ref, branch_ref, mixed_ref, sums_ref = refs[12:]
    grad_normed = sum(dot(h[...], w[...], 1, 1) for h, w in zip(hiddens, ins))
    unit, inverse = normalize(resid_ref[...])
    grad_rows = low_ref[...].astype(F32)
    grad = grad_rows + norm_back(grad_normed * as_row(gain_ref), unit, inverse)
    branch = grad.astype(BF16)
    grad_ref[...] = grad
    branch_ref[...] = branch
    mixed_ref[...] = dot(branch, proj_ref[...], 1, 1).astype(BF16)
    sums = stack_rows(
        [
            column_sum(branch.astype(F32)),
            column_sum(grad_normed * unit),
            column_sum(grad_normed),
            column_sum(grad_rows),
        ]
    )

    @pl.when(pl.program_id(0) == 0)
    def _():
        sums_ref[...] = sums

    @pl.when(pl.program_id(0) > 0)
    def _():
        sums_ref[...] += sums


def mlp_result(actives, outs, resid, kept_col, bias, image, slots, earlier):
    row_count, width = resid.shape
    tile = slots // 2
    block = pl.BlockSpec((tile, width), lambda i: (2 * image + i, 0))
    return pl.pallas_call(
        mlp_out_kernel,
        grid=(2,),
        in_specs=[block] * 4
        + [fixed(width, width)] * 4
        + [block, pl.BlockSpec((tile, 1), lambda i: (2 * image + i, 0)), fixed(width)]
        + [pl.BlockSpec(memory_space=pl.ANY)] * len(earlier),
        out_specs=block,
        out_shape=shape((row_count, width)),
        input_output_aliases={11: 0} if earlier else {},
        cost_estimate=cost(8 * slots * width * width, slots * width * 14),
        compiler_params=PARAMS,
    )(*actives, *outs, resid, kept_col, bias, *earlier)


def mlp_back(hiddens, ins, proj_weight, resid, grad_low, gain):
    row_count, width = resid.shape
    tile = row_count // 4
    block = pl.BlockSpec((tile, width), lambda i: (i, 0))
    return pl.pallas_call(
        mlp_back_kernel,
        grid=(4,),
        in_specs=[block] * 4
        + [fixed(width, width)] * 5
        + [block, block, fixed(width)],
        out_specs=[block, block, block, fixed(8, width)],
        out_shape=[
            shape((row_count, width), F32),
            shape((row_count, width)),
            shape((row_count, width)),
            shape((8, width), F32),
        ],
        cost_estimate=cost(10 * row_count * width * width, row_count * width * 22),
        compiler_params=PARAMS,
    )(*hiddens, *ins, proj_weight, resid, grad_low, gain)


def attend_back_kernel(
    q_ref, k_ref, v_ref, mixed_ref, grad_ref, total_ref, kept_ref, cos_ref, sin_ref, *refs
):
    packed_ref, sums_ref = refs[-2:]
    slots = q_ref.shape[0]
    low = lax.broadcasted_iota(jnp.int32, (1, LANES), 1) < HEAD
    q, k, v, grad_mixed = q_ref[...], k_ref[...], v_ref[...], grad_ref[...]
    zero = jnp.zeros_like(q)
    mask = (kept_ref[...] - 1.0) * MASKED_SCORE
    product = jnp.transpose(grad_mixed.astype(F32) * mixed_ref[...].astype(F32))
    totals = jnp.transpose(total_ref[...])
    grad_q = grad_k = grad_v = None
    for head in range(2):
        keep = low if head == 0 else ~low
        q_head = jnp.where(keep, q, zero)
        grad_head = jnp.where(keep, grad_mixed, zero)
        k_head = jnp.where(keep, k, zero)
        total = totals[head * HEAD : head * HEAD + 1]
        inner = column_sum(product[head * HEAD : (head + 1) * HEAD])
        weights = jnp.exp((dot(k, q_head, 1, 1) + mask) - total)
        grad_weights = dot(v, grad_head, 1, 1)
        grad_scores = (weights * (grad_weights - inner)).astype(BF16)
        part_v = dot(weights.astype(BF16), grad_head)
        part_k = dot(grad_scores, q_head)
        part_q = dot(grad_scores, k_head, 0, 0)
        grad_v = part_v if grad_v is None else grad_v + part_v
        grad_k = part_k if grad_k is None else grad_k + part_k
        grad_q = part_q if grad_q is None else grad_q + part_q
    turn = grad_q * swap_halves(q.astype(F32)) + grad_k * swap_halves(k.astype(F32))
    slot = lax.broadcasted_iota(jnp.int32, (slots, 1), 0)
    across = slot // GRID
    down = slot - across * GRID
    cosine, sine = cos_ref[...], sin_ref[...]
    grad_q = grad_q * (HEAD**-0.5)
    grad_q = (grad_q * cosine - swap_halves(grad_q) * sine).astype(BF16)
    grad_k = (grad_k * cosine - swap_halves(grad_k) * sine).astype(BF16)
    packed = jnp.concatenate([grad_q, grad_k, grad_v.astype(BF16)], axis=1)
    packed_ref[...] = packed
    parts = column_sum(packed.astype(F32))
    sums = stack_rows(
        [
            column_sum(turn * across.astype(F32)),
            column_sum(turn * down.astype(F32)),
            parts[:, :LANES],
            parts[:, LANES : 2 * LANES],
            parts[:, 2 * LANES :],
        ]
    )

    @pl.when(pl.program_id(0) == 0)
    def _():
        sums_ref[...] = sums

    @pl.when(pl.program_id(0) > 0)
    def _():
        sums_ref[...] += sums


def attend_back(
    qkv, mixed, grad_mixed, totals, kept_col, cosine, sine, slots, pair, count, at, earlier
):
    row_count, width = mixed.shape
    images, pairs = row_count // slots, width // LANES
    block = lambda part: pl.BlockSpec((slots, LANES), lambda i: (i, pair + part * pairs))
    table = pl.BlockSpec((slots, LANES), lambda i: (0, pair))
    return pl.pallas_call(
        attend_back_kernel,
        grid=(images,),
        in_specs=[
            block(0), block(1), block(2), block(0), block(0), block(0),
            pl.BlockSpec((slots, 1), lambda i: (i, 0)),
            table,
            table,
        ] + [pl.BlockSpec(memory_space=pl.ANY)] * len(earlier),
        out_specs=[pl.BlockSpec((slots, 3 * LANES), lambda i: (i, at)), fixed(8, LANES)],
        out_shape=[shape((row_count, count * 3 * LANES)), shape((8, LANES), F32)],
        input_output_aliases={9: 0} if earlier else {},
        cost_estimate=cost(
            40 * row_count * slots * LANES, row_count * LANES * 30, row_count * slots * 2
        ),
        compiler_params=PARAMS,
    )(qkv, qkv, qkv, mixed, grad_mixed, totals, kept_col, cosine, sine, *earlier)


def finish_kernel(count, *refs):
    packed, (weight_ref, x_ref, grad_ref, gain_ref) = refs[:count], refs[count : count + 4]
    more, (input_ref, sums_ref) = refs[count + 4 : -2], refs[-2:]
    pieces = [p[:, at : at + 3 * LANES] for p in packed for at in range(0, p.shape[1], 3 * LANES)]
    full = jnp.concatenate(
        [p[:, part * LANES : (part + 1) * LANES] for part in range(3) for p in pieces], axis=1
    )
    grad_normed = dot(full, weight_ref[...], 1, 1)
    unit, inverse = normalize(x_ref[...].astype(F32))
    input_ref[...] = (
        grad_ref[...] + norm_back(grad_normed * as_row(gain_ref), unit, inverse)
    ).astype(BF16)
    members = [column_sum(grad_normed * unit), column_sum(grad_normed)]
    step = pl.program_id(0)
    if not more:

        @pl.when(step == 0)
        def _():
            sums_ref[...] = stack_rows(members)

        @pl.when(step > 0)
        def _():
            sums_ref[...] += stack_rows(members)

    else:
        own_ref, joined_ref, hidden_refs, pair_refs, before_ref = (
            more[0], more[1], more[2:6], more[6:-2], more[-2],
        )

        @pl.when(step == 0)
        def _():
            row = lax.broadcasted_iota(jnp.int32, (8, 1), 0)
            top = jnp.zeros((8, input_ref.shape[1]), F32)
            for r, hidden in enumerate(hidden_refs):
                top = jnp.where(row == (own_ref[0] ^ r), hidden[...], top)
            low = jnp.where(row < 4, 0.0, pltpu.roll(joined_ref[...], 4, 0))
            sums_ref[0:8, :] = top + low
            pairs = jnp.concatenate([p[...] for p in pair_refs], axis=1)
            ends = pltpu.roll(before_ref[...] + stack_rows(members), 5, 0)
            sums_ref[8:16, :] = jnp.where(row < 5, pairs, ends)

        @pl.when(step > 0)
        def _():
            sums_ref[8:16, :] += pltpu.roll(stack_rows(members), 5, 0)


def finish(packed, weight, rows, grad_resid, gain, image, slots, more):
    row_count, width = rows.shape
    tile = slots // 2
    block = lambda cols: pl.BlockSpec((tile, cols), lambda i: (2 * image + i, 0))
    more_specs = [fixed(*m.shape) for m in more]
    if more:
        more_specs[0] = pl.BlockSpec(memory_space=pltpu.SMEM)
        more_specs[-1] = pl.BlockSpec(memory_space=pl.ANY)
    count = len(packed)
    sums = 16 if more else 8
    return pl.pallas_call(
        functools.partial(finish_kernel, count),
        grid=(2,),
        in_specs=[block(p.shape[1]) for p in packed]
        + [fixed(*weight.shape), block(width), block(width), fixed(width)]
        + more_specs,
        out_specs=[block(width), fixed(sums, width)],
        out_shape=[shape((row_count, width)), shape((sums, width), F32)],
        input_output_aliases={count + 3 + len(more): 0} if more else {},
        cost_estimate=cost(6 * slots * width * width, slots * width * 14),
        compiler_params=PARAMS,
    )(*packed, weight, rows, grad_resid, gain, *more)


def total(values):
    return jnp.sum(jnp.sum(values * values, axis=0, keepdims=True), axis=1, keepdims=True)


def place(blocks, pair, weight_ref, width):
    square = jnp.zeros((1, 1), F32)
    for block, start in blocks:
        for at in range(start, block.shape[1], 3 * LANES):
            for part in range(3):
                piece = block[:, at + part * LANES : at + (part + 1) * LANES].astype(F32)
                first = part * width + pair * LANES
                weight_ref[:, first : first + LANES] = piece
                square = square + total(piece)
            pair += 1
    return square


def final_early_kernel(first_ref, second_ref, weight_ref, proj_ref, square_ref):
    width = proj_ref.shape[1]
    proj = first_ref[:, :width].astype(F32)
    proj_ref[...] = proj
    square = total(proj) + place([(first_ref, width), (second_ref, 0)], 0, weight_ref, width)

    @pl.when(pl.program_id(0) == 0)
    def _():
        square_ref[...] = square

    @pl.when(pl.program_id(0) > 0)
    def _():
        square_ref[...] += square


def final_early(first, second, width):
    depth = first.shape[0]
    tile = depth // 4
    row_block = lambda cols: pl.BlockSpec((tile, cols), lambda i: (i, 0))
    return pl.pallas_call(
        final_early_kernel,
        grid=(4,),
        in_specs=[row_block(first.shape[1]), row_block(second.shape[1])],
        out_specs=[row_block(3 * width), row_block(width), fixed(1, 1)],
        out_shape=[shape((depth, 3 * width), F32), shape((depth, width), F32), shape((1, 1), F32)],
        cost_estimate=cost(depth * width * 8, depth * width * 20),
        compiler_params=PARAMS,
    )(first, second)


def final_kernel(
    own_ref, side_ref, small_ref, square_ref, mine_ref, other_ref, before_ref, *outputs
):
    (
        weight_out, gain1_ref, shift1_ref, bias_ref, freq_ref, proj_bias_ref,
        gain2_ref, shift2_ref, hidden_ref, out_bias_ref, freq_norm_ref, rest_norm_ref,
        staged, sems,
    ) = outputs
    rows, width = mine_ref.shape[0], small_ref.shape[1]
    pairs = width // LANES
    late = mine_ref.shape[1] // (3 * LANES)
    first, span = (pairs - late) * LANES, late * LANES
    square = square_ref[...]
    mine, other = mine_ref[...].astype(F32), other_ref[...].astype(F32)
    square = square + total(mine) + total(other)
    lower = side_ref[0] == 0
    for top, block in ((0, jnp.where(lower, mine, other)), (rows, jnp.where(lower, other, mine))):
        for pair in range(late):
            at = pair * LANES
            for part in range(3):
                start = (3 * pair + part) * LANES
                staged[part, top : top + rows, at : at + LANES] = block[:, start : start + LANES]
    copies = [
        pltpu.make_async_copy(
            staged.at[part],
            weight_out.at[:, part * width + first : part * width + first + span],
            sems.at[part],
        )
        for part in range(3)
    ]
    for copy in copies:
        copy.start()
    small = small_ref[...]
    hidden_ref[...] = small_ref[pl.ds(own_ref[0], 1), :].reshape(width)
    for at, ref in enumerate((proj_bias_ref, gain2_ref, shift2_ref, out_bias_ref)):
        ref[...] = small[4 + at]
    bias_ref[...] = jnp.concatenate([small[10], small[11], small[12]], axis=0)
    gain1_ref[...] = small[13]
    shift1_ref[...] = small[14]
    freq_square = jnp.zeros((1, 1), F32)
    half = HEAD // 2
    for head in range(width // HEAD):
        at = head * HEAD
        turned = small_ref[8:10, at + half : at + HEAD] - small_ref[8:10, at : at + half]
        freq_ref[head, :, :] = turned
        freq_square = freq_square + total(turned)
    freq_norm_ref[...] = jnp.sqrt(freq_square)
    rest_norm_ref[...] = jnp.sqrt(square + total(small[4:8]) + total(small[10:15]))
    for copy in copies:
        copy.wait()


def final(own, side, small, square, mine, other, freq_shape, weight):
    depth, width = weight.shape[0], small.shape[1]
    late = mine.shape[1] // 3
    vector = (shape((width,), F32), fixed(width))
    outputs = [
        (shape(weight.shape, F32), pl.BlockSpec(memory_space=pl.ANY)),
        vector,
        vector,
        (shape((3 * width,), F32), fixed(3 * width)),
        (shape(freq_shape, F32), fixed(*freq_shape)),
        vector,
        vector,
        vector,
        vector,
        vector,
        (shape((1, 1), F32), fixed(1, 1)),
        (shape((1, 1), F32), fixed(1, 1)),
    ]
    return pl.pallas_call(
        final_kernel,
        grid=(1,),
        in_specs=[
            pl.BlockSpec(memory_space=pltpu.SMEM),
            pl.BlockSpec(memory_space=pltpu.SMEM),
            fixed(*small.shape),
            fixed(1, 1),
            fixed(*mine.shape),
            fixed(*other.shape),
            pl.BlockSpec(memory_space=pl.ANY),
        ],
        out_specs=[spec for _, spec in outputs],
        out_shape=[dims for dims, _ in outputs],
        scratch_shapes=[pltpu.VMEM((3, depth, late), F32), pltpu.SemaphoreType.DMA((3,))],
        input_output_aliases={6: 0},
        cost_estimate=cost(depth * width * 8, depth * width * 8),
        compiler_params=PARAMS,
    )(own, side, small, square, mine, other, weight)


class Exchange:
    def __init__(self, mesh):
        self.sizes = dict(mesh.shape)

    def bits(self, axis):
        return [(axis, 1 << b) for b in range(self.sizes[axis].bit_length() - 1)]

    def swap(self, value, step):
        axis, bit = step
        pairs = [(i, i ^ bit) for i in range(self.sizes[axis])]
        return lax.ppermute(value, axis, pairs)

    def side(self, step):
        axis, bit = step
        return (lax.axis_index(axis) // bit) % 2

    def half(self, value, step, mine, dim):
        size = value.shape[dim] // 2
        side = self.side(step)
        return lax.dynamic_slice_in_dim(value, (side if mine else 1 - side) * size, size, dim)

    def join(self, mine, other, step, dim):
        first = self.side(step) == 0
        return jnp.concatenate(
            [jnp.where(first, mine, other), jnp.where(first, other, mine)], axis=dim
        )


def add(*members):
    return sum(member.astype(F32) for member in members).astype(BF16)


def tie(*members):
    return lax.optimization_barrier(members)


class Chain:
    def __init__(self, net, value, halving, full=(), joins=None, dim=0):
        joins = list(reversed(halving)) if joins is None else joins
        self.net, self.value, self.dim = net, value, dim
        self.todo = [("halve", s) for s in halving] + [("full", s) for s in full]
        self.todo += [("join", s) for s in joins]
        self.flight = self.sent = None

    def start(self):
        if not self.todo or self.flight is not None:
            return
        self.prepare()
        self.flight = self.net.swap(self.sent, self.todo[0][1])

    def last(self):
        self.end()
        return self.value

    def prepare(self):
        if self.sent is None:
            kind, step = self.todo[0]
            self.sent = self.value
            if kind == "halve":
                self.sent = self.net.half(self.value, step, False, self.dim)

    def end(self):
        if self.flight is None:
            return
        kind, step = self.todo.pop(0)
        if kind == "halve":
            self.value = add(self.net.half(self.value, step, True, self.dim), self.flight)
        elif kind == "full":
            total = self.value.astype(F32) + self.flight.astype(F32)
            self.value = total.astype(self.value.dtype)
        else:
            self.value = self.net.join(self.value, self.flight, step, self.dim)
        self.flight = self.sent = None


def drain(*chains, keep=0):
    for chain in chains:
        while len(chain.todo) > keep:
            chain.start()
            chain.end()


def meet(chains, *outputs, hold=()):
    flights = [c.flight for c in chains if c.flight is not None]
    for chain in hold:
        chain.prepare()
    landed, outputs, sents = tie(flights, outputs, [h.sent for h in hold])
    landed = list(landed)
    for chain, sent in zip(hold, sents):
        chain.sent = sent
    for chain in chains:
        if chain.flight is not None:
            chain.flight = landed.pop(0)
            chain.end()
    return outputs


def body(
    net,
    images,
    keep_mask,
    ln1_gain,
    ln1_bias,
    qkv_weight,
    qkv_bias,
    frequencies,
    proj_weight,
    proj_bias,
    ln2_gain,
    ln2_bias,
    fc1_weight,
    fc1_bias,
    fc2_weight,
    fc2_bias,
    out_grad,
):
    image_count, slots, width = images.shape
    row_count = image_count * slots
    inner, outer = net.bits("tensor")
    dp_steps = net.bits("dp")
    near_dp, far_dp = dp_steps[:1], dp_steps[1:]

    ins, outs = {0: fc1_weight}, {0: fc2_weight}
    ins[2], outs[2] = net.swap(fc1_weight, outer), net.swap(fc2_weight, outer)
    ins[1], outs[1] = net.swap(fc1_weight, inner), net.swap(fc2_weight, inner)
    biases = {0: fc1_bias}
    biases[1], biases[2] = net.swap(biases[0], inner), net.swap(biases[0], outer)

    rows = images.reshape(row_count, width)
    by_head = jnp.transpose(frequencies, (1, 0, 2))
    normed_one, qkv, cosine, sine = project_qkv(
        rows, ln1_gain, ln1_bias, qkv_bias, by_head, qkv_weight, slots
    )
    mixed, totals = attend(qkv, keep_mask, slots)
    resid, normed_two, grad_low, kept_col = project_out(
        mixed, rows, out_grad.reshape(row_count, width), keep_mask,
        proj_bias, ln2_gain, ln2_bias, proj_weight,
    )

    actives, hiddens, grads, bias_grads = {}, {}, {}, {}

    def chunk(r, normed, grad):
        actives[r], hiddens[r], grads[r], bias_grads[r] = hidden_units(
            normed, grad, ins[r], biases[r], outs[r]
        )

    normed_two, grad_low, ins[1], outs[1], biases[1] = tie(
        normed_two, grad_low, ins[1], outs[1], biases[1]
    )
    chunk(1, normed_two, grad_low)
    normed_two, grads[1], ins[2], outs[2], biases[2] = tie(
        normed_two, grads[1], ins[2], outs[2], biases[2]
    )
    biases[3] = net.swap(biases[2], inner)
    near = net.swap(grads[1], inner)
    ins[3], outs[3] = net.swap(ins[2], inner), net.swap(outs[2], inner)
    chunk(0, normed_two, grad_low)
    normed_two, grads[0], near, ins[3], outs[3], biases[3] = tie(
        normed_two, grads[0], near, ins[3], outs[3], biases[3]
    )
    near = Chain(net, add(grads[0], near), near_dp, joins=[], dim=1)
    near.start()
    chunk(3, normed_two, grad_low)
    normed_two, grads[3] = tie(normed_two, grads[3])
    far = net.swap(grads[3], inner)
    chunk(2, normed_two, grad_low)
    far, grads[2], hiddens[2] = tie(far, grads[2], hiddens[2])
    far = add(grads[2], far)
    far_in = Chain(net, far[0], near_dp, joins=[])
    far_out = Chain(net, far[1], near_dp, joins=[])
    far_out.start()
    ranks = range(4)
    grad_resid, grad_branch, grad_mixed, joined = mlp_back(
        [hiddens[r] for r in ranks], [ins[r] for r in ranks],
        proj_weight, resid, grad_low, ln2_gain,
    )
    grad_branch, grad_mixed = meet(
        [near, far_out], grad_branch, grad_mixed, hold=[far_in]
    )
    far_in.start()
    cross_out = net.swap(far_out.value, outer)
    proj_grad = dot(mixed, grad_branch, 0, 0).astype(BF16)

    pair_sums = {}

    def back(pair, grad, count=1, at=0, earlier=()):
        packed, pair_sums[pair] = attend_back(
            qkv, mixed, grad, totals, kept_col, cosine, sine, slots, pair, count, at, earlier
        )
        return packed

    def weight_grad(packed):
        return dot(normed_one, packed, 0, 0).astype(BF16)

    def group(value):
        return Chain(net, value, [inner, outer] + near_dp, far_dp)

    def begin(*chains):
        for chain in chains:
            chain.start()

    packed_a = back(0, grad_mixed, 2, 0)
    grad_mixed, cross_out, packed_a, proj_grad = meet(
        [far_in], grad_mixed, cross_out, packed_a, proj_grad
    )
    cross_in = net.swap(far_in.value, outer)
    out_half = add(near.value[1], cross_out)
    packed_a = back(1, grad_mixed, 2, 1, [packed_a])
    grad_mixed, cross_in, *first = tie(grad_mixed, cross_in, proj_grad, weight_grad(packed_a))
    mlp_half = jnp.stack([add(near.value[0], cross_in), out_half])
    mlp_sum = Chain(net, mlp_half, far_dp[:1], far_dp[1:], dim=1)
    group_a = group(jnp.concatenate(first, axis=1))
    begin(mlp_sum, group_a)
    packed_b = back(2, grad_mixed, 2, 0)
    grad_mixed, packed_b = meet([mlp_sum, group_a], grad_mixed, packed_b)
    begin(mlp_sum, group_a)
    packed_b = back(3, grad_mixed, 2, 1, [packed_b])
    grad_mixed, grad_b = meet([group_a], grad_mixed, weight_grad(packed_b))
    group_b = group(grad_b)
    begin(group_a, group_b)
    packed_c = back(4, grad_mixed, 2, 0)
    grad_mixed, packed_c = meet([mlp_sum, group_a, group_b], grad_mixed, packed_c)
    begin(mlp_sum, group_a, group_b)
    packed_c = back(5, grad_mixed, 2, 1, [packed_c])
    packed_c, grad_c = meet([group_a, group_b], packed_c, weight_grad(packed_c))
    group_c = group(grad_c)
    begin(group_a, group_b, group_c)

    packed = [packed_a, packed_b, packed_c]
    own_list = lax.axis_index("tensor").astype(jnp.int32).reshape(1)
    groups = [group_a, group_b, group_c]
    input_grad, half_sums = finish(
        packed, qkv_weight, rows, grad_resid, ln1_gain, 0, slots, ()
    )
    input_grad, half_sums = meet([mlp_sum, group_b, group_c], input_grad, half_sums)
    begin(mlp_sum, group_b, group_c)
    input_grad, small = finish(
        packed, qkv_weight, rows, grad_resid, ln1_gain, 1, slots,
        [own_list, joined, *[bias_grads[r] for r in ranks], *[pair_sums[p] for p in range(6)],
         half_sums, input_grad],
    )
    small, actives[0] = meet(groups, small, actives[0])
    small = Chain(net, small, [], [inner, outer] + dp_steps)
    groups.append(small)
    begin(*groups)
    result = lambda image, earlier: mlp_result(
        [actives[r] for r in ranks], [outs[r] for r in ranks],
        resid, kept_col, fc2_bias, image, slots, earlier,
    )
    drain(mlp_sum)
    mlp_in = Chain(net, mlp_sum.value[0], [], joins=near_dp)
    mlp_out = Chain(net, mlp_sum.value[1], [], joins=near_dp)
    block_out = result(0, ())
    (block_out,) = meet(groups, block_out, hold=[mlp_out])
    begin(mlp_out, *groups)
    block_out = result(1, (block_out,))
    (block_out,) = meet(groups, block_out)
    begin(*groups)
    meet(groups)
    begin(*groups)
    meet([mlp_out, *groups], hold=[mlp_in])
    begin(mlp_in, *groups)
    drain(group_a, group_b)
    early = final_early(group_a.value, group_b.value, width)
    *early, fc2_weight_grad = meet(groups, *early, mlp_out.value.T.astype(F32))
    drain(group_c, keep=1)
    drain(small)
    begin(group_c)
    side = net.side(inner).astype(jnp.int32).reshape(1)
    fc1_weight_grad = mlp_in.last().astype(F32)
    proj_weight_grad = early[1]
    (
        qkv_weight_grad, ln1_gain_grad, ln1_bias_grad, qkv_bias_grad,
        freq_grad, proj_bias_grad, ln2_gain_grad, ln2_bias_grad, fc1_bias_grad, fc2_bias_grad,
        freq_norm, rest_norm,
    ) = final(
        own_list, side, small.value, early[2], group_c.value, group_c.flight,
        by_head.shape, early[0],
    )
    return (
        block_out.reshape(images.shape),
        input_grad.reshape(images.shape),
        ln1_gain_grad,
        ln1_bias_grad,
        qkv_weight_grad,
        qkv_bias_grad,
        jnp.transpose(freq_grad, (1, 0, 2)),
        proj_weight_grad,
        proj_bias_grad,
        ln2_gain_grad,
        ln2_bias_grad,
        fc1_weight_grad,
        fc1_bias_grad,
        fc2_weight_grad,
        fc2_bias_grad,
        freq_norm.reshape(()),
        rest_norm.reshape(()),
    )


def solution(mesh):
    rows = P(("dp", "tensor"), None, None)
    whole = P()
    hidden_in, hidden_out = P(None, "tensor"), P("tensor", None)
    return jax.shard_map(
        functools.partial(body, Exchange(mesh)),
        mesh=mesh,
        in_specs=(
            (rows, P(("dp", "tensor"), None))
            + (whole,) * 9
            + (hidden_in, P("tensor"), hidden_out, whole, rows)
        ),
        out_specs=(
            (rows, rows) + (whole,) * 9 + (hidden_in, P("tensor"), hidden_out) + (whole,) * 3
        ),
        check_vma=False,
    )
```

```python
import functools

import jax
import jax.numpy as jnp
from jax import lax
from jax.experimental import pallas as pl
from jax.experimental.pallas import tpu as pltpu
from jax.sharding import PartitionSpec as P

GRID = 24
EPSILON = 1e-06
MASKED_SCORE = 1e30
ROOT_HALF = 0.7071067811865476
DENSITY_SCALE = 0.3989422804014327
F32 = jnp.float32
BF16 = jnp.bfloat16
LANES = 128
HEAD = 64
HIDDEN_TILE = 256
EMPHASIS = 20
EARLY = pltpu.CompilerParams(vmem_limit_bytes=56 << 20)
CHUNK = pltpu.CompilerParams(vmem_limit_bytes=24 << 20)
PARAMS = pltpu.CompilerParams(vmem_limit_bytes=24 << 20)


def dot(left, right, left_dim=1, right_dim=0):
    return lax.dot_general(
        left, right, (((left_dim,), (right_dim,)), ((), ())), preferred_element_type=F32
    )


def normalize(row_data):
    row_mean = jnp.mean(row_data, axis=-1, keepdims=True)
    centred = row_data - row_mean
    inverse = lax.rsqrt(jnp.mean(centred * centred, axis=-1, keepdims=True) + EPSILON)
    return (centred * inverse, inverse)


def norm_back(grad_unit, unit_rows, inverse):
    return inverse * (
        grad_unit
        - jnp.mean(grad_unit, axis=-1, keepdims=True)
        - unit_rows * jnp.mean(grad_unit * unit_rows, axis=-1, keepdims=True)
    )


def swap_halves(tile):
    lane = lax.broadcasted_iota(jnp.int32, (1, LANES), 1)
    first = (lane % HEAD) < HEAD // 2
    return jnp.where(
        first, pltpu.roll(tile, LANES - HEAD // 2, 1), pltpu.roll(tile, HEAD // 2, 1)
    )


def as_row(ref):
    return ref[...].astype(F32).reshape(1, -1)


def column_sum(values):
    return jnp.sum(values, axis=0, keepdims=True)


def stack_rows(members):
    width = members[0].shape[1]
    row = lax.broadcasted_iota(jnp.int32, (8, width), 0)
    total = jnp.zeros((8, width), F32)
    for at, member in enumerate(members):
        total = jnp.where(row == at, member, total)
    return total


def shape(dims, dtype=BF16):
    return jax.ShapeDtypeStruct(dims, dtype)


def fixed(*dims):
    return pl.BlockSpec(dims, lambda *_: (0,) * len(dims))


def cost(flops, moved, steep=0):
    return pl.CostEstimate(flops=EMPHASIS * flops, bytes_accessed=moved, transcendentals=steep)


def qkv_kernel(
    x_ref, gain_ref, shift_ref, bias_ref, freq_ref, weight_ref,
    normed_ref, qkv_ref, cos_ref, sin_ref, lanes_ref,
):
    tile, width = x_ref.shape
    across_count = tile // GRID

    @pl.when(pl.program_id(1) == 0)
    def _():
        half = HEAD // 2
        for head in range(width // HEAD):
            for at in (head * HEAD, head * HEAD + half):
                lanes_ref[0:2, at : at + half] = freq_ref[head, :, :]
        first = (pl.program_id(0) * across_count).astype(F32)
        padded = -(-across_count // 8) * 8
        across = first + lax.broadcasted_iota(jnp.int32, (padded, width), 0).astype(F32)
        down = lax.broadcasted_iota(jnp.int32, (GRID, width), 0).astype(F32)
        across = across * lanes_ref[0:1, :]
        down = down * lanes_ref[1:2, :]
        cos_a, sin_a, cos_d, sin_d = jnp.cos(across), jnp.sin(across), jnp.cos(down), jnp.sin(down)
        lane = lax.broadcasted_iota(jnp.int32, (1, width), 1)
        sign = jnp.where((lane % HEAD) < HEAD // 2, -1.0, 1.0)
        for at in range(across_count):
            rows = slice(at * GRID, (at + 1) * GRID)
            one_cos, one_sin = cos_a[at : at + 1], sin_a[at : at + 1]
            cos_ref[rows, :] = one_cos * cos_d - one_sin * sin_d
            sin_ref[rows, :] = (one_sin * cos_d + one_cos * sin_d) * sign

    unit, _ = normalize(x_ref[...].astype(F32))
    normed = (unit * as_row(gain_ref) + as_row(shift_ref)).astype(BF16)
    normed_ref[...] = normed
    bias = as_row(bias_ref)
    for part in range(3):
        cols = slice(part * width, (part + 1) * width)
        packed = dot(normed, weight_ref[:, cols]) + bias[:, cols]
        for at in range(0, width, LANES):
            piece = packed[:, at : at + LANES]
            if part < 2:
                cosine, sine = cos_ref[:, at : at + LANES], sin_ref[:, at : at + LANES]
                piece = piece * cosine + swap_halves(piece) * sine
            if part == 0:
                piece = piece * (HEAD**-0.5)
            qkv_ref[:, part * width + at : part * width + at + LANES] = piece.astype(BF16)


def project_qkv(rows, gain, shift, bias, frequencies, weight, slots):
    row_count, width = rows.shape
    halves = 2
    tile = slots // halves
    row_block = lambda cols: pl.BlockSpec((tile, cols), lambda h, n: (n * halves + h, 0))
    table = pl.BlockSpec((tile, width), lambda h, n: (h, 0))
    return pl.pallas_call(
        qkv_kernel,
        grid=(halves, row_count // slots),
        in_specs=[
            row_block(width),
            fixed(width),
            fixed(width),
            fixed(3 * width),
            fixed(*frequencies.shape),
            fixed(*weight.shape),
        ],
        out_specs=[row_block(width), row_block(3 * width), table, table],
        out_shape=[
            shape((row_count, width)),
            shape((row_count, 3 * width)),
            shape((slots, width), F32),
            shape((slots, width), F32),
        ],
        scratch_shapes=[pltpu.VMEM((8, width), F32)],
        cost_estimate=cost(6 * row_count * width * width, row_count * width * 14),
        compiler_params=EARLY,
    )(rows, gain, shift, bias, frequencies, weight)


def attend_kernel(q_ref, k_ref, v_ref, mask_ref, mixed_ref, total_ref):
    low = lax.broadcasted_iota(jnp.int32, (1, LANES), 1) < HEAD
    queries, keys, values = q_ref[...], k_ref[...], v_ref[...]
    zero = jnp.zeros_like(queries)
    kept = mask_ref[pl.ds(pl.program_id(0), 1), :].astype(F32)
    mask = (kept - 1.0) * MASKED_SCORE
    mixed, totals = None, []
    for head in range(2):
        keep = low if head == 0 else ~low
        scores = dot(jnp.where(keep, queries, zero), keys, 1, 1) + mask
        row_max = jnp.max(scores, axis=1, keepdims=True)
        weights = jnp.exp(scores - row_max)
        row_total = jnp.sum(weights, axis=1, keepdims=True)
        low_weights = (weights * (1.0 / row_total)).astype(BF16)
        part = dot(low_weights, jnp.where(keep, values, zero))
        mixed = part if mixed is None else mixed + part
        totals.append(row_max + jnp.log(row_total))
    mixed_ref[...] = mixed.astype(BF16)
    total_ref[...] = jnp.where(low, totals[0], totals[1])


def attend(qkv, keep_mask, slots):
    row_count, width = qkv.shape[0], qkv.shape[1] // 3
    images, pairs = row_count // slots, width // LANES
    block = lambda part: pl.BlockSpec((slots, LANES), lambda i, p: (i, p + part * pairs))
    return pl.pallas_call(
        attend_kernel,
        grid=(images, pairs),
        in_specs=[
            block(0),
            block(1),
            block(2),
            fixed(*keep_mask.shape),
        ],
        out_specs=[block(0), block(0)],
        out_shape=[shape((row_count, width)), shape((row_count, width), F32)],
        cost_estimate=cost(
            16 * row_count * slots * width, row_count * width * 12, row_count * slots * 2 * pairs
        ),
        compiler_params=EARLY,
    )(qkv, qkv, qkv, keep_mask)


def project_kernel(
    mixed_ref, x_ref, grad_ref, mask_ref, bias_ref, gain_ref, shift_ref, weight_ref,
    resid_ref, normed_ref, low_ref, kept_ref,
):
    row = mask_ref[pl.ds(pl.program_id(0), 1), :].astype(F32)
    kept = jnp.transpose(jnp.broadcast_to(row, (8, row.shape[1])))[:, 0:1]
    resid = x_ref[...].astype(F32) + dot(mixed_ref[...], weight_ref[...]) + as_row(bias_ref)
    unit, _ = normalize(resid)
    resid_ref[...] = resid
    normed_ref[...] = (unit * as_row(gain_ref) + as_row(shift_ref)).astype(BF16)
    low_ref[...] = (kept * grad_ref[...].astype(F32)).astype(BF16)
    kept_ref[...] = kept


def project_out(mixed, rows, out_grad, keep_mask, bias, gain, shift, weight):
    row_count, width = rows.shape
    images, slots = keep_mask.shape
    block = pl.BlockSpec((slots, width), lambda i: (i, 0))
    return pl.pallas_call(
        project_kernel,
        grid=(images,),
        in_specs=[block, block, block, fixed(images, slots)]
        + [fixed(width)] * 3
        + [fixed(*weight.shape)],
        out_specs=[block, block, block, pl.BlockSpec((slots, 1), lambda i: (i, 0))],
        out_shape=[
            shape((row_count, width), F32),
            shape((row_count, width)),
            shape((row_count, width)),
            shape((row_count, 1), F32),
        ],
        cost_estimate=cost(2 * row_count * width * width, row_count * width * 14),
        compiler_params=EARLY,
    )(mixed, rows, out_grad, keep_mask, bias, gain, shift, weight)


def hidden_kernel(
    normed_ref, grad_ref, in_ref, bias_ref, out_ref,
    active_ref, hidden_ref, weights_ref, bias_grad_ref,
):
    normed, grad = normed_ref[...], grad_ref[...]
    hidden = dot(normed, in_ref[...]) + as_row(bias_ref)
    grad_active = dot(grad, out_ref[...], 1, 1)
    half = 0.5 * (1.0 + lax.erf(hidden * ROOT_HALF))
    active = (hidden * half).astype(BF16)
    slope = half + hidden * jnp.exp(-0.5 * hidden * hidden) * DENSITY_SCALE
    grad_hidden = (grad_active * slope).astype(BF16)
    active_ref[...] = active
    hidden_ref[...] = grad_hidden
    weights_ref[0] = dot(normed, grad_hidden, 0, 0).astype(BF16)
    weights_ref[1] = dot(grad, active, 0, 0).astype(BF16)
    bias_grad_ref[...] = column_sum(grad_hidden.astype(F32))


def hidden_units(normed, grad, weight_in, bias_in, weight_out):
    row_count, width = normed.shape
    units = weight_in.shape[1]
    tile = HIDDEN_TILE
    cols = lambda rows: pl.BlockSpec((rows, tile), lambda i: (0, i))
    rows = pl.BlockSpec((tile, width), lambda i: (i, 0))
    return pl.pallas_call(
        hidden_kernel,
        grid=(units // tile,),
        in_specs=[
            fixed(row_count, width), fixed(row_count, width), cols(width),
            pl.BlockSpec((tile,), lambda i: (i,)), rows
        ],
        out_specs=[
            cols(row_count),
            cols(row_count),
            pl.BlockSpec((2, width, tile), lambda i: (0, 0, i)),
            cols(1),
        ],
        out_shape=[
            shape((row_count, units)),
            shape((row_count, units)),
            shape((2, width, units)),
            shape((1, units), F32),
        ],
        cost_estimate=cost(
            8 * row_count * width * units, row_count * width * 8 + width * units * 8,
            2 * row_count * units,
        ),
        compiler_params=CHUNK,
    )(normed, grad, weight_in, bias_in, weight_out)


def mlp_out_kernel(*refs):
    actives, outs = refs[0:4], refs[4:8]
    resid_ref, kept_ref, bias_ref = refs[8:11]
    block_ref = refs[-1]
    mlp_out = sum(dot(a[...], w[...]) for a, w in zip(actives, outs))
    block_ref[...] = (kept_ref[...] * (resid_ref[...] + mlp_out + as_row(bias_ref))).astype(BF16)


def mlp_back_kernel(*refs):
    hiddens, ins = refs[0:4], refs[4:8]
    proj_ref, resid_ref, low_ref, gain_ref = refs[8:12]
    grad_ref, branch_ref, mixed_ref, sums_ref = refs[12:]
    grad_normed = sum(dot(h[...], w[...], 1, 1) for h, w in zip(hiddens, ins))
    unit, inverse = normalize(resid_ref[...])
    grad_rows = low_ref[...].astype(F32)
    grad = grad_rows + norm_back(grad_normed * as_row(gain_ref), unit, inverse)
    branch = grad.astype(BF16)
    grad_ref[...] = grad
    branch_ref[...] = branch
    mixed_ref[...] = dot(branch, proj_ref[...], 1, 1).astype(BF16)
    sums = stack_rows(
        [
            column_sum(branch.astype(F32)),
            column_sum(grad_normed * unit),
            column_sum(grad_normed),
            column_sum(grad_rows),
        ]
    )

    @pl.when(pl.program_id(0) == 0)
    def _():
        sums_ref[...] = sums

    @pl.when(pl.program_id(0) > 0)
    def _():
        sums_ref[...] += sums


def mlp_result(actives, outs, resid, kept_col, bias, image, slots, earlier):
    row_count, width = resid.shape
    tile = slots // 2
    block = pl.BlockSpec((tile, width), lambda i: (2 * image + i, 0))
    return pl.pallas_call(
        mlp_out_kernel,
        grid=(2,),
        in_specs=[block] * 4
        + [fixed(width, width)] * 4
        + [block, pl.BlockSpec((tile, 1), lambda i: (2 * image + i, 0)), fixed(width)]
        + [pl.BlockSpec(memory_space=pl.ANY)] * len(earlier),
        out_specs=block,
        out_shape=shape((row_count, width)),
        input_output_aliases={11: 0} if earlier else {},
        cost_estimate=cost(8 * slots * width * width, slots * width * 14),
        compiler_params=PARAMS,
    )(*actives, *outs, resid, kept_col, bias, *earlier)


def mlp_back(hiddens, ins, proj_weight, resid, grad_low, gain):
    row_count, width = resid.shape
    tile = row_count // 4
    block = pl.BlockSpec((tile, width), lambda i: (i, 0))
    return pl.pallas_call(
        mlp_back_kernel,
        grid=(4,),
        in_specs=[block] * 4
        + [fixed(width, width)] * 5
        + [block, block, fixed(width)],
        out_specs=[block, block, block, fixed(8, width)],
        out_shape=[
            shape((row_count, width), F32),
            shape((row_count, width)),
            shape((row_count, width)),
            shape((8, width), F32),
        ],
        cost_estimate=cost(10 * row_count * width * width, row_count * width * 22),
        compiler_params=PARAMS,
    )(*hiddens, *ins, proj_weight, resid, grad_low, gain)


def attend_back_kernel(
    q_ref, k_ref, v_ref, mixed_ref, grad_ref, total_ref, kept_ref, cos_ref, sin_ref, *refs
):
    packed_ref, sums_ref = refs[-2:]
    slots = q_ref.shape[0]
    low = lax.broadcasted_iota(jnp.int32, (1, LANES), 1) < HEAD
    q, k, v, grad_mixed = q_ref[...], k_ref[...], v_ref[...], grad_ref[...]
    zero = jnp.zeros_like(q)
    mask = (kept_ref[...] - 1.0) * MASKED_SCORE
    product = jnp.transpose(grad_mixed.astype(F32) * mixed_ref[...].astype(F32))
    totals = jnp.transpose(total_ref[...])
    grad_q = grad_k = grad_v = None
    for head in range(2):
        keep = low if head == 0 else ~low
        q_head = jnp.where(keep, q, zero)
        grad_head = jnp.where(keep, grad_mixed, zero)
        k_head = jnp.where(keep, k, zero)
        total = totals[head * HEAD : head * HEAD + 1]
        inner = column_sum(product[head * HEAD : (head + 1) * HEAD])
        weights = jnp.exp((dot(k, q_head, 1, 1) + mask) - total)
        grad_weights = dot(v, grad_head, 1, 1)
        grad_scores = (weights * (grad_weights - inner)).astype(BF16)
        part_v = dot(weights.astype(BF16), grad_head)
        part_k = dot(grad_scores, q_head)
        part_q = dot(grad_scores, k_head, 0, 0)
        grad_v = part_v if grad_v is None else grad_v + part_v
        grad_k = part_k if grad_k is None else grad_k + part_k
        grad_q = part_q if grad_q is None else grad_q + part_q
    turn = grad_q * swap_halves(q.astype(F32)) + grad_k * swap_halves(k.astype(F32))
    slot = lax.broadcasted_iota(jnp.int32, (slots, 1), 0)
    across = slot // GRID
    down = slot - across * GRID
    cosine, sine = cos_ref[...], sin_ref[...]
    grad_q = grad_q * (HEAD**-0.5)
    grad_q = (grad_q * cosine - swap_halves(grad_q) * sine).astype(BF16)
    grad_k = (grad_k * cosine - swap_halves(grad_k) * sine).astype(BF16)
    packed = jnp.concatenate([grad_q, grad_k, grad_v.astype(BF16)], axis=1)
    packed_ref[...] = packed
    parts = column_sum(packed.astype(F32))
    sums = stack_rows(
        [
            column_sum(turn * across.astype(F32)),
            column_sum(turn * down.astype(F32)),
            parts[:, :LANES],
            parts[:, LANES : 2 * LANES],
            parts[:, 2 * LANES :],
        ]
    )

    @pl.when(pl.program_id(0) == 0)
    def _():
        sums_ref[...] = sums

    @pl.when(pl.program_id(0) > 0)
    def _():
        sums_ref[...] += sums


def attend_back(
    qkv, mixed, grad_mixed, totals, kept_col, cosine, sine, slots, pair, count, at, earlier
):
    row_count, width = mixed.shape
    images, pairs = row_count // slots, width // LANES
    block = lambda part: pl.BlockSpec((slots, LANES), lambda i: (i, pair + part * pairs))
    table = pl.BlockSpec((slots, LANES), lambda i: (0, pair))
    return pl.pallas_call(
        attend_back_kernel,
        grid=(images,),
        in_specs=[
            block(0), block(1), block(2), block(0), block(0), block(0),
            pl.BlockSpec((slots, 1), lambda i: (i, 0)),
            table,
            table,
        ] + [pl.BlockSpec(memory_space=pl.ANY)] * len(earlier),
        out_specs=[pl.BlockSpec((slots, 3 * LANES), lambda i: (i, at)), fixed(8, LANES)],
        out_shape=[shape((row_count, count * 3 * LANES)), shape((8, LANES), F32)],
        input_output_aliases={9: 0} if earlier else {},
        cost_estimate=cost(
            40 * row_count * slots * LANES, row_count * LANES * 30, row_count * slots * 2
        ),
        compiler_params=PARAMS,
    )(qkv, qkv, qkv, mixed, grad_mixed, totals, kept_col, cosine, sine, *earlier)


def finish_kernel(count, *refs):
    packed, (weight_ref, x_ref, grad_ref, gain_ref) = refs[:count], refs[count : count + 4]
    more, (input_ref, sums_ref) = refs[count + 4 : -2], refs[-2:]
    pieces = [p[:, at : at + 3 * LANES] for p in packed for at in range(0, p.shape[1], 3 * LANES)]
    full = jnp.concatenate(
        [p[:, part * LANES : (part + 1) * LANES] for part in range(3) for p in pieces], axis=1
    )
    grad_normed = dot(full, weight_ref[...], 1, 1)
    unit, inverse = normalize(x_ref[...].astype(F32))
    input_ref[...] = (
        grad_ref[...] + norm_back(grad_normed * as_row(gain_ref), unit, inverse)
    ).astype(BF16)
    members = [column_sum(grad_normed * unit), column_sum(grad_normed)]
    step = pl.program_id(0)
    if not more:

        @pl.when(step == 0)
        def _():
            sums_ref[...] = stack_rows(members)

        @pl.when(step > 0)
        def _():
            sums_ref[...] += stack_rows(members)

    else:
        own_ref, joined_ref, hidden_refs, pair_refs, before_ref = (
            more[0], more[1], more[2:6], more[6:-2], more[-2],
        )

        @pl.when(step == 0)
        def _():
            row = lax.broadcasted_iota(jnp.int32, (8, 1), 0)
            top = jnp.zeros((8, input_ref.shape[1]), F32)
            for r, hidden in enumerate(hidden_refs):
                top = jnp.where(row == (own_ref[0] ^ r), hidden[...], top)
            low = jnp.where(row < 4, 0.0, pltpu.roll(joined_ref[...], 4, 0))
            sums_ref[0:8, :] = top + low
            pairs = jnp.concatenate([p[...] for p in pair_refs], axis=1)
            ends = pltpu.roll(before_ref[...] + stack_rows(members), 5, 0)
            sums_ref[8:16, :] = jnp.where(row < 5, pairs, ends)

        @pl.when(step > 0)
        def _():
            sums_ref[8:16, :] += pltpu.roll(stack_rows(members), 5, 0)


def finish(packed, weight, rows, grad_resid, gain, image, slots, more):
    row_count, width = rows.shape
    tile = slots // 2
    block = lambda cols: pl.BlockSpec((tile, cols), lambda i: (2 * image + i, 0))
    more_specs = [fixed(*m.shape) for m in more]
    if more:
        more_specs[0] = pl.BlockSpec(memory_space=pltpu.SMEM)
        more_specs[-1] = pl.BlockSpec(memory_space=pl.ANY)
    count = len(packed)
    sums = 16 if more else 8
    return pl.pallas_call(
        functools.partial(finish_kernel, count),
        grid=(2,),
        in_specs=[block(p.shape[1]) for p in packed]
        + [fixed(*weight.shape), block(width), block(width), fixed(width)]
        + more_specs,
        out_specs=[block(width), fixed(sums, width)],
        out_shape=[shape((row_count, width)), shape((sums, width), F32)],
        input_output_aliases={count + 3 + len(more): 0} if more else {},
        cost_estimate=cost(6 * slots * width * width, slots * width * 14),
        compiler_params=PARAMS,
    )(*packed, weight, rows, grad_resid, gain, *more)


def total(values):
    return jnp.sum(jnp.sum(values * values, axis=0, keepdims=True), axis=1, keepdims=True)


def place(blocks, pair, weight_ref, width):
    square = jnp.zeros((1, 1), F32)
    for block, start in blocks:
        for at in range(start, block.shape[1], 3 * LANES):
            for part in range(3):
                piece = block[:, at + part * LANES : at + (part + 1) * LANES].astype(F32)
                first = part * width + pair * LANES
                weight_ref[:, first : first + LANES] = piece
                square = square + total(piece)
            pair += 1
    return square


def final_early_kernel(first_ref, second_ref, weight_ref, proj_ref, square_ref):
    width = proj_ref.shape[1]
    proj = first_ref[:, :width].astype(F32)
    proj_ref[...] = proj
    square = total(proj) + place([(first_ref, width), (second_ref, 0)], 0, weight_ref, width)

    @pl.when(pl.program_id(0) == 0)
    def _():
        square_ref[...] = square

    @pl.when(pl.program_id(0) > 0)
    def _():
        square_ref[...] += square


def final_early(first, second, width):
    depth = first.shape[0]
    tile = depth // 4
    row_block = lambda cols: pl.BlockSpec((tile, cols), lambda i: (i, 0))
    return pl.pallas_call(
        final_early_kernel,
        grid=(4,),
        in_specs=[row_block(first.shape[1]), row_block(second.shape[1])],
        out_specs=[row_block(3 * width), row_block(width), fixed(1, 1)],
        out_shape=[shape((depth, 3 * width), F32), shape((depth, width), F32), shape((1, 1), F32)],
        cost_estimate=cost(depth * width * 8, depth * width * 20),
        compiler_params=PARAMS,
    )(first, second)


def final_kernel(
    own_ref, side_ref, small_ref, square_ref, mine_ref, other_ref, before_ref, *outputs
):
    (
        weight_out, gain1_ref, shift1_ref, bias_ref, freq_ref, proj_bias_ref,
        gain2_ref, shift2_ref, hidden_ref, out_bias_ref, freq_norm_ref, rest_norm_ref,
        staged, sems,
    ) = outputs
    rows, width = mine_ref.shape[0], small_ref.shape[1]
    pairs = width // LANES
    late = mine_ref.shape[1] // (3 * LANES)
    first, span = (pairs - late) * LANES, late * LANES
    square = square_ref[...]
    mine, other = mine_ref[...].astype(F32), other_ref[...].astype(F32)
    square = square + total(mine) + total(other)
    lower = side_ref[0] == 0
    for top, block in ((0, jnp.where(lower, mine, other)), (rows, jnp.where(lower, other, mine))):
        for pair in range(late):
            at = pair * LANES
            for part in range(3):
                start = (3 * pair + part) * LANES
                staged[part, top : top + rows, at : at + LANES] = block[:, start : start + LANES]
    copies = [
        pltpu.make_async_copy(
            staged.at[part],
            weight_out.at[:, part * width + first : part * width + first + span],
            sems.at[part],
        )
        for part in range(3)
    ]
    for copy in copies:
        copy.start()
    small = small_ref[...]
    hidden_ref[...] = small_ref[pl.ds(own_ref[0], 1), :].reshape(width)
    for at, ref in enumerate((proj_bias_ref, gain2_ref, shift2_ref, out_bias_ref)):
        ref[...] = small[4 + at]
    bias_ref[...] = jnp.concatenate([small[10], small[11], small[12]], axis=0)
    gain1_ref[...] = small[13]
    shift1_ref[...] = small[14]
    freq_square = jnp.zeros((1, 1), F32)
    half = HEAD // 2
    for head in range(width // HEAD):
        at = head * HEAD
        turned = small_ref[8:10, at + half : at + HEAD] - small_ref[8:10, at : at + half]
        freq_ref[head, :, :] = turned
        freq_square = freq_square + total(turned)
    freq_norm_ref[...] = jnp.sqrt(freq_square)
    rest_norm_ref[...] = jnp.sqrt(square + total(small[4:8]) + total(small[10:15]))
    for copy in copies:
        copy.wait()


def final(own, side, small, square, mine, other, freq_shape, weight):
    depth, width = weight.shape[0], small.shape[1]
    late = mine.shape[1] // 3
    vector = (shape((width,), F32), fixed(width))
    outputs = [
        (shape(weight.shape, F32), pl.BlockSpec(memory_space=pl.ANY)),
        vector,
        vector,
        (shape((3 * width,), F32), fixed(3 * width)),
        (shape(freq_shape, F32), fixed(*freq_shape)),
        vector,
        vector,
        vector,
        vector,
        vector,
        (shape((1, 1), F32), fixed(1, 1)),
        (shape((1, 1), F32), fixed(1, 1)),
    ]
    return pl.pallas_call(
        final_kernel,
        grid=(1,),
        in_specs=[
            pl.BlockSpec(memory_space=pltpu.SMEM),
            pl.BlockSpec(memory_space=pltpu.SMEM),
            fixed(*small.shape),
            fixed(1, 1),
            fixed(*mine.shape),
            fixed(*other.shape),
            pl.BlockSpec(memory_space=pl.ANY),
        ],
        out_specs=[spec for _, spec in outputs],
        out_shape=[dims for dims, _ in outputs],
        scratch_shapes=[pltpu.VMEM((3, depth, late), F32), pltpu.SemaphoreType.DMA((3,))],
        input_output_aliases={6: 0},
        cost_estimate=cost(depth * width * 8, depth * width * 8),
        compiler_params=PARAMS,
    )(own, side, small, square, mine, other, weight)


class Exchange:
    def __init__(self, mesh):
        self.sizes = dict(mesh.shape)

    def bits(self, axis):
        return [(axis, 1 << b) for b in range(self.sizes[axis].bit_length() - 1)]

    def swap(self, value, step):
        axis, bit = step
        pairs = [(i, i ^ bit) for i in range(self.sizes[axis])]
        return lax.ppermute(value, axis, pairs)

    def side(self, step):
        axis, bit = step
        return (lax.axis_index(axis) // bit) % 2

    def half(self, value, step, mine, dim):
        size = value.shape[dim] // 2
        side = self.side(step)
        return lax.dynamic_slice_in_dim(value, (side if mine else 1 - side) * size, size, dim)

    def join(self, mine, other, step, dim):
        first = self.side(step) == 0
        return jnp.concatenate(
            [jnp.where(first, mine, other), jnp.where(first, other, mine)], axis=dim
        )


def add(*members):
    return sum(member.astype(F32) for member in members).astype(BF16)


def tie(*members):
    return lax.optimization_barrier(members)


class Chain:
    def __init__(self, net, value, halving, full=(), joins=None, dim=0):
        joins = list(reversed(halving)) if joins is None else joins
        self.net, self.value, self.dim = net, value, dim
        self.todo = [("halve", s) for s in halving] + [("full", s) for s in full]
        self.todo += [("join", s) for s in joins]
        self.flight = self.sent = None

    def start(self):
        if not self.todo or self.flight is not None:
            return
        self.prepare()
        self.flight = self.net.swap(self.sent, self.todo[0][1])

    def prepare(self):
        if self.sent is None:
            kind, step = self.todo[0]
            self.sent = self.value
            if kind == "halve":
                self.sent = self.net.half(self.value, step, False, self.dim)

    def end(self):
        if self.flight is None:
            return
        kind, step = self.todo.pop(0)
        if kind == "halve":
            self.value = add(self.net.half(self.value, step, True, self.dim), self.flight)
        elif kind == "full":
            total = self.value.astype(F32) + self.flight.astype(F32)
            self.value = total.astype(self.value.dtype)
        else:
            self.value = self.net.join(self.value, self.flight, step, self.dim)
        self.flight = self.sent = None


def drain(*chains, keep=0):
    for chain in chains:
        while len(chain.todo) > keep:
            chain.start()
            chain.end()


def meet(chains, *outputs, hold=()):
    flights = [c.flight for c in chains if c.flight is not None]
    for chain in hold:
        chain.prepare()
    landed, outputs, sents = tie(flights, outputs, [h.sent for h in hold])
    landed = list(landed)
    for chain, sent in zip(hold, sents):
        chain.sent = sent
    for chain in chains:
        if chain.flight is not None:
            chain.flight = landed.pop(0)
            chain.end()
    return outputs


def body(
    net,
    images,
    keep_mask,
    ln1_gain,
    ln1_bias,
    qkv_weight,
    qkv_bias,
    frequencies,
    proj_weight,
    proj_bias,
    ln2_gain,
    ln2_bias,
    fc1_weight,
    fc1_bias,
    fc2_weight,
    fc2_bias,
    out_grad,
):
    image_count, slots, width = images.shape
    row_count = image_count * slots
    inner, outer = net.bits("tensor")
    dp_steps = net.bits("dp")
    near_dp, far_dp = dp_steps[:1], dp_steps[1:]

    ins, outs = {0: fc1_weight}, {0: fc2_weight}
    ins[2], outs[2] = net.swap(fc1_weight, outer), net.swap(fc2_weight, outer)
    ins[1], outs[1] = net.swap(fc1_weight, inner), net.swap(fc2_weight, inner)
    biases = {0: fc1_bias}
    biases[1], biases[2] = net.swap(biases[0], inner), net.swap(biases[0], outer)

    rows = images.reshape(row_count, width)
    by_head = jnp.transpose(frequencies, (1, 0, 2))
    normed_one, qkv, cosine, sine = project_qkv(
        rows, ln1_gain, ln1_bias, qkv_bias, by_head, qkv_weight, slots
    )
    mixed, totals = attend(qkv, keep_mask, slots)
    resid, normed_two, grad_low, kept_col = project_out(
        mixed, rows, out_grad.reshape(row_count, width), keep_mask,
        proj_bias, ln2_gain, ln2_bias, proj_weight,
    )

    actives, hiddens, grads, bias_grads = {}, {}, {}, {}

    def chunk(r, normed, grad):
        actives[r], hiddens[r], grads[r], bias_grads[r] = hidden_units(
            normed, grad, ins[r], biases[r], outs[r]
        )

    normed_two, grad_low, ins[1], outs[1], biases[1] = tie(
        normed_two, grad_low, ins[1], outs[1], biases[1]
    )
    chunk(1, normed_two, grad_low)
    normed_two, grads[1], ins[2], outs[2], biases[2] = tie(
        normed_two, grads[1], ins[2], outs[2], biases[2]
    )
    biases[3] = net.swap(biases[2], inner)
    near = net.swap(grads[1], inner)
    ins[3], outs[3] = net.swap(ins[2], inner), net.swap(outs[2], inner)
    chunk(0, normed_two, grad_low)
    normed_two, grads[0], near, ins[3], outs[3], biases[3] = tie(
        normed_two, grads[0], near, ins[3], outs[3], biases[3]
    )
    near = Chain(net, add(grads[0], near), near_dp, joins=[], dim=1)
    near.start()
    chunk(3, normed_two, grad_low)
    normed_two, grads[3] = tie(normed_two, grads[3])
    far = net.swap(grads[3], inner)
    chunk(2, normed_two, grad_low)
    far, grads[2], hiddens[2] = tie(far, grads[2], hiddens[2])
    far = add(grads[2], far)
    far_in = Chain(net, far[0], near_dp, joins=[])
    far_out = Chain(net, far[1], near_dp, joins=[])
    far_out.start()
    ranks = range(4)
    grad_resid, grad_branch, grad_mixed, joined = mlp_back(
        [hiddens[r] for r in ranks], [ins[r] for r in ranks],
        proj_weight, resid, grad_low, ln2_gain,
    )
    grad_branch, grad_mixed = meet(
        [near, far_out], grad_branch, grad_mixed, hold=[far_in]
    )
    far_in.start()
    cross_out = net.swap(far_out.value, outer)
    proj_grad = dot(mixed, grad_branch, 0, 0).astype(BF16)

    pair_sums = {}

    def back(pair, grad, count=1, at=0, earlier=()):
        packed, pair_sums[pair] = attend_back(
            qkv, mixed, grad, totals, kept_col, cosine, sine, slots, pair, count, at, earlier
        )
        return packed

    def weight_grad(packed):
        return dot(normed_one, packed, 0, 0).astype(BF16)

    def group(value):
        return Chain(net, value, [inner, outer] + near_dp, far_dp)

    def begin(*chains):
        for chain in chains:
            chain.start()

    def gather(value):
        return Chain(net, value, far_dp[:1], far_dp[1:], far_dp[:1] + near_dp)

    packed_a = back(0, grad_mixed, 2, 0)
    grad_mixed, cross_out, packed_a, proj_grad = meet(
        [far_in], grad_mixed, cross_out, packed_a, proj_grad
    )
    cross_in = net.swap(far_in.value, outer)
    mlp_out = gather(add(near.value[1], cross_out))
    begin(mlp_out)
    packed_a = back(1, grad_mixed, 2, 1, [packed_a])
    grad_mixed, cross_in, *first = meet(
        [mlp_out], grad_mixed, cross_in, proj_grad, weight_grad(packed_a)
    )
    mlp_in = gather(add(near.value[0], cross_in))
    group_a = group(jnp.concatenate(first, axis=1))
    begin(mlp_in, mlp_out, group_a)
    packed_b = back(2, grad_mixed, 2, 0)
    grad_mixed, packed_b = meet([mlp_in, mlp_out, group_a], grad_mixed, packed_b)
    begin(mlp_in, mlp_out, group_a)
    packed_b = back(3, grad_mixed, 2, 1, [packed_b])
    grad_mixed, grad_b = meet(
        [mlp_in, mlp_out, group_a], grad_mixed, weight_grad(packed_b)
    )
    group_b = group(grad_b)
    begin(mlp_in, group_a, group_b)
    packed_c = back(4, grad_mixed, 2, 0)
    grad_mixed, packed_c = meet(
        [mlp_in, group_a, group_b], grad_mixed, packed_c, hold=[mlp_out]
    )
    begin(mlp_out, group_a, group_b)
    packed_c = back(5, grad_mixed, 2, 1, [packed_c])
    packed_c, grad_c = meet([group_a, group_b], packed_c, weight_grad(packed_c))
    group_c = group(grad_c)
    begin(group_a, group_b, group_c)

    packed = [packed_a, packed_b, packed_c]
    own_list = lax.axis_index("tensor").astype(jnp.int32).reshape(1)
    groups = [group_a, group_b, group_c]
    input_grad, half_sums = finish(
        packed, qkv_weight, rows, grad_resid, ln1_gain, 0, slots, ()
    )
    input_grad, half_sums = meet(
        [mlp_out, group_b, group_c], input_grad, half_sums, hold=[mlp_in]
    )
    begin(mlp_in, group_b, group_c)
    input_grad, small = finish(
        packed, qkv_weight, rows, grad_resid, ln1_gain, 1, slots,
        [own_list, joined, *[bias_grads[r] for r in ranks], *[pair_sums[p] for p in range(6)],
         half_sums, input_grad],
    )
    small, actives[0] = meet(groups, small, actives[0])
    small = Chain(net, small, [], near_dp + [inner, outer] + far_dp)
    groups.append(small)
    begin(*groups)
    result = lambda image, earlier: mlp_result(
        [actives[r] for r in ranks], [outs[r] for r in ranks],
        resid, kept_col, fc2_bias, image, slots, earlier,
    )
    block_out = result(0, ())
    (block_out,) = meet(groups, block_out)
    begin(*groups)
    block_out = result(1, (block_out,))
    (block_out,) = meet([mlp_in, *groups], block_out)
    begin(*groups)
    meet(groups)
    begin(*groups)
    meet(groups)
    begin(*groups)
    drain(group_a, group_b, mlp_in, mlp_out)
    early = final_early(group_a.value, group_b.value, width)
    *early, fc1_weight_grad, fc2_weight_grad = meet(
        groups, *early, mlp_in.value.astype(F32), mlp_out.value.T.astype(F32)
    )
    drain(group_c, keep=1)
    drain(small)
    begin(group_c)
    side = net.side(inner).astype(jnp.int32).reshape(1)
    proj_weight_grad = early[1]
    (
        qkv_weight_grad, ln1_gain_grad, ln1_bias_grad, qkv_bias_grad,
        freq_grad, proj_bias_grad, ln2_gain_grad, ln2_bias_grad, fc1_bias_grad, fc2_bias_grad,
        freq_norm, rest_norm,
    ) = final(
        own_list, side, small.value, early[2], group_c.value, group_c.flight,
        by_head.shape, early[0],
    )
    return (
        block_out.reshape(images.shape),
        input_grad.reshape(images.shape),
        ln1_gain_grad,
        ln1_bias_grad,
        qkv_weight_grad,
        qkv_bias_grad,
        jnp.transpose(freq_grad, (1, 0, 2)),
        proj_weight_grad,
        proj_bias_grad,
        ln2_gain_grad,
        ln2_bias_grad,
        fc1_weight_grad,
        fc1_bias_grad,
        fc2_weight_grad,
        fc2_bias_grad,
        freq_norm.reshape(()),
        rest_norm.reshape(()),
    )


def solution(mesh):
    rows = P(("dp", "tensor"), None, None)
    whole = P()
    hidden_in, hidden_out = P(None, "tensor"), P("tensor", None)
    return jax.shard_map(
        functools.partial(body, Exchange(mesh)),
        mesh=mesh,
        in_specs=(
            (rows, P(("dp", "tensor"), None))
            + (whole,) * 9
            + (hidden_in, P("tensor"), hidden_out, whole, rows)
        ),
        out_specs=(
            (rows, rows) + (whole,) * 9 + (hidden_in, P("tensor"), hidden_out) + (whole,) * 3
        ),
        check_vma=False,
    )
```

```python
import functools

import jax
import jax.numpy as jnp
from jax import lax
from jax.experimental import pallas as pl
from jax.experimental.pallas import tpu as pltpu
from jax.sharding import PartitionSpec as P

GRID = 24
EPSILON = 1e-06
MASKED_SCORE = 1e30
ROOT_HALF = 0.7071067811865476
DENSITY_SCALE = 0.3989422804014327
F32 = jnp.float32
BF16 = jnp.bfloat16
LANES = 128
HEAD = 64
HIDDEN_TILE = 256
EMPHASIS = 20
EARLY = pltpu.CompilerParams(vmem_limit_bytes=56 << 20)
CHUNK = pltpu.CompilerParams(vmem_limit_bytes=24 << 20)
PARAMS = pltpu.CompilerParams(vmem_limit_bytes=32 << 20)


def dot(left, right, left_dim=1, right_dim=0):
    return lax.dot_general(
        left, right, (((left_dim,), (right_dim,)), ((), ())), preferred_element_type=F32
    )


def normalize(row_data):
    row_mean = jnp.mean(row_data, axis=-1, keepdims=True)
    centred = row_data - row_mean
    inverse = lax.rsqrt(jnp.mean(centred * centred, axis=-1, keepdims=True) + EPSILON)
    return (centred * inverse, inverse)


def norm_back(grad_unit, unit_rows, inverse):
    return inverse * (
        grad_unit
        - jnp.mean(grad_unit, axis=-1, keepdims=True)
        - unit_rows * jnp.mean(grad_unit * unit_rows, axis=-1, keepdims=True)
    )


def swap_halves(tile):
    lane = lax.broadcasted_iota(jnp.int32, (1, LANES), 1)
    first = (lane % HEAD) < HEAD // 2
    return jnp.where(
        first, pltpu.roll(tile, LANES - HEAD // 2, 1), pltpu.roll(tile, HEAD // 2, 1)
    )


def as_row(ref):
    return ref[...].astype(F32).reshape(1, -1)


def column_sum(values):
    return jnp.sum(values, axis=0, keepdims=True)


def stack_rows(members):
    width = members[0].shape[1]
    row = lax.broadcasted_iota(jnp.int32, (8, width), 0)
    total = jnp.zeros((8, width), F32)
    for at, member in enumerate(members):
        total = jnp.where(row == at, member, total)
    return total


def shape(dims, dtype=BF16):
    return jax.ShapeDtypeStruct(dims, dtype)


def fixed(*dims):
    return pl.BlockSpec(dims, lambda *_: (0,) * len(dims))


def cost(flops, moved, steep=0):
    return pl.CostEstimate(flops=EMPHASIS * flops, bytes_accessed=moved, transcendentals=steep)


def qkv_kernel(
    x_ref, gain_ref, shift_ref, bias_ref, freq_ref, weight_ref,
    normed_ref, qkv_ref, cos_ref, sin_ref, lanes_ref,
):
    tile, width = x_ref.shape
    across_count = tile // GRID

    @pl.when(pl.program_id(1) == 0)
    def _():
        half = HEAD // 2
        for head in range(width // HEAD):
            for at in (head * HEAD, head * HEAD + half):
                lanes_ref[0:2, at : at + half] = freq_ref[head, :, :]
        first = (pl.program_id(0) * across_count).astype(F32)
        padded = -(-across_count // 8) * 8
        across = first + lax.broadcasted_iota(jnp.int32, (padded, width), 0).astype(F32)
        down = lax.broadcasted_iota(jnp.int32, (GRID, width), 0).astype(F32)
        across = across * lanes_ref[0:1, :]
        down = down * lanes_ref[1:2, :]
        cos_a, sin_a, cos_d, sin_d = jnp.cos(across), jnp.sin(across), jnp.cos(down), jnp.sin(down)
        lane = lax.broadcasted_iota(jnp.int32, (1, width), 1)
        sign = jnp.where((lane % HEAD) < HEAD // 2, -1.0, 1.0)
        for at in range(across_count):
            rows = slice(at * GRID, (at + 1) * GRID)
            one_cos, one_sin = cos_a[at : at + 1], sin_a[at : at + 1]
            cos_ref[rows, :] = one_cos * cos_d - one_sin * sin_d
            sin_ref[rows, :] = (one_sin * cos_d + one_cos * sin_d) * sign

    unit, _ = normalize(x_ref[...].astype(F32))
    normed = (unit * as_row(gain_ref) + as_row(shift_ref)).astype(BF16)
    normed_ref[...] = normed
    bias = as_row(bias_ref)
    for part in range(3):
        cols = slice(part * width, (part + 1) * width)
        packed = dot(normed, weight_ref[:, cols]) + bias[:, cols]
        for at in range(0, width, LANES):
            piece = packed[:, at : at + LANES]
            if part < 2:
                cosine, sine = cos_ref[:, at : at + LANES], sin_ref[:, at : at + LANES]
                piece = piece * cosine + swap_halves(piece) * sine
            if part == 0:
                piece = piece * (HEAD**-0.5)
            qkv_ref[:, part * width + at : part * width + at + LANES] = piece.astype(BF16)


def project_qkv(rows, gain, shift, bias, frequencies, weight, slots):
    row_count, width = rows.shape
    halves = 2
    tile = slots // halves
    row_block = lambda cols: pl.BlockSpec((tile, cols), lambda h, n: (n * halves + h, 0))
    table = pl.BlockSpec((tile, width), lambda h, n: (h, 0))
    return pl.pallas_call(
        qkv_kernel,
        grid=(halves, row_count // slots),
        in_specs=[
            row_block(width),
            fixed(width),
            fixed(width),
            fixed(3 * width),
            fixed(*frequencies.shape),
            fixed(*weight.shape),
        ],
        out_specs=[row_block(width), row_block(3 * width), table, table],
        out_shape=[
            shape((row_count, width)),
            shape((row_count, 3 * width)),
            shape((slots, width), F32),
            shape((slots, width), F32),
        ],
        scratch_shapes=[pltpu.VMEM((8, width), F32)],
        cost_estimate=cost(6 * row_count * width * width, row_count * width * 14),
        compiler_params=EARLY,
    )(rows, gain, shift, bias, frequencies, weight)


def attend_kernel(q_ref, k_ref, v_ref, mask_ref, mixed_ref, total_ref):
    low = lax.broadcasted_iota(jnp.int32, (1, LANES), 1) < HEAD
    queries, keys, values = q_ref[...], k_ref[...], v_ref[...]
    zero = jnp.zeros_like(queries)
    kept = mask_ref[pl.ds(pl.program_id(0), 1), :].astype(F32)
    mask = (kept - 1.0) * MASKED_SCORE
    mixed, totals = None, []
    for head in range(2):
        keep = low if head == 0 else ~low
        scores = dot(jnp.where(keep, queries, zero), keys, 1, 1) + mask
        row_max = jnp.max(scores, axis=1, keepdims=True)
        weights = jnp.exp(scores - row_max)
        row_total = jnp.sum(weights, axis=1, keepdims=True)
        low_weights = (weights * (1.0 / row_total)).astype(BF16)
        part = dot(low_weights, jnp.where(keep, values, zero))
        mixed = part if mixed is None else mixed + part
        totals.append(row_max + jnp.log(row_total))
    mixed_ref[...] = mixed.astype(BF16)
    total_ref[...] = jnp.where(low, totals[0], totals[1])


def attend(qkv, keep_mask, slots):
    row_count, width = qkv.shape[0], qkv.shape[1] // 3
    images, pairs = row_count // slots, width // LANES
    block = lambda part: pl.BlockSpec((slots, LANES), lambda i, p: (i, p + part * pairs))
    return pl.pallas_call(
        attend_kernel,
        grid=(images, pairs),
        in_specs=[
            block(0),
            block(1),
            block(2),
            fixed(*keep_mask.shape),
        ],
        out_specs=[block(0), block(0)],
        out_shape=[shape((row_count, width)), shape((row_count, width), F32)],
        cost_estimate=cost(
            16 * row_count * slots * width, row_count * width * 12, row_count * slots * 2 * pairs
        ),
        compiler_params=EARLY,
    )(qkv, qkv, qkv, keep_mask)


def project_kernel(
    mixed_ref, x_ref, grad_ref, mask_ref, bias_ref, gain_ref, shift_ref, weight_ref,
    resid_ref, normed_ref, low_ref, kept_ref,
):
    row = mask_ref[pl.ds(pl.program_id(0), 1), :].astype(F32)
    kept = jnp.transpose(jnp.broadcast_to(row, (8, row.shape[1])))[:, 0:1]
    resid = x_ref[...].astype(F32) + dot(mixed_ref[...], weight_ref[...]) + as_row(bias_ref)
    unit, _ = normalize(resid)
    resid_ref[...] = resid
    normed_ref[...] = (unit * as_row(gain_ref) + as_row(shift_ref)).astype(BF16)
    low_ref[...] = (kept * grad_ref[...].astype(F32)).astype(BF16)
    kept_ref[...] = kept


def project_out(mixed, rows, out_grad, keep_mask, bias, gain, shift, weight):
    row_count, width = rows.shape
    images, slots = keep_mask.shape
    block = pl.BlockSpec((slots, width), lambda i: (i, 0))
    return pl.pallas_call(
        project_kernel,
        grid=(images,),
        in_specs=[block, block, block, fixed(images, slots)]
        + [fixed(width)] * 3
        + [fixed(*weight.shape)],
        out_specs=[block, block, block, pl.BlockSpec((slots, 1), lambda i: (i, 0))],
        out_shape=[
            shape((row_count, width), F32),
            shape((row_count, width)),
            shape((row_count, width)),
            shape((row_count, 1), F32),
        ],
        cost_estimate=cost(2 * row_count * width * width, row_count * width * 14),
        compiler_params=EARLY,
    )(mixed, rows, out_grad, keep_mask, bias, gain, shift, weight)


def hidden_kernel(
    normed_ref, grad_ref, in_ref, bias_ref, out_ref,
    active_ref, hidden_ref, weights_ref, bias_grad_ref,
):
    normed, grad = normed_ref[...], grad_ref[...]
    hidden = dot(normed, in_ref[...]) + as_row(bias_ref)
    grad_active = dot(grad, out_ref[...], 1, 1)
    half = 0.5 * (1.0 + lax.erf(hidden * ROOT_HALF))
    active = (hidden * half).astype(BF16)
    slope = half + hidden * jnp.exp(-0.5 * hidden * hidden) * DENSITY_SCALE
    grad_hidden = (grad_active * slope).astype(BF16)
    active_ref[...] = active
    hidden_ref[...] = grad_hidden
    weights_ref[0] = dot(normed, grad_hidden, 0, 0).astype(BF16)
    weights_ref[1] = dot(grad, active, 0, 0).astype(BF16)
    bias_grad_ref[...] = column_sum(grad_hidden.astype(F32))


def hidden_units(normed, grad, weight_in, bias_in, weight_out):
    row_count, width = normed.shape
    units = weight_in.shape[1]
    tile = HIDDEN_TILE
    cols = lambda rows: pl.BlockSpec((rows, tile), lambda i: (0, i))
    rows = pl.BlockSpec((tile, width), lambda i: (i, 0))
    return pl.pallas_call(
        hidden_kernel,
        grid=(units // tile,),
        in_specs=[
            fixed(row_count, width), fixed(row_count, width), cols(width),
            pl.BlockSpec((tile,), lambda i: (i,)), rows
        ],
        out_specs=[
            cols(row_count),
            cols(row_count),
            pl.BlockSpec((2, width, tile), lambda i: (0, 0, i)),
            cols(1),
        ],
        out_shape=[
            shape((row_count, units)),
            shape((row_count, units)),
            shape((2, width, units)),
            shape((1, units), F32),
        ],
        cost_estimate=cost(
            8 * row_count * width * units, row_count * width * 8 + width * units * 8,
            2 * row_count * units,
        ),
        compiler_params=CHUNK,
    )(normed, grad, weight_in, bias_in, weight_out)


def mlp_out_kernel(*refs):
    actives, outs = refs[0:4], refs[4:8]
    resid_ref, kept_ref, bias_ref = refs[8:11]
    block_ref = refs[-1]
    mlp_out = sum(dot(a[...], w[...]) for a, w in zip(actives, outs))
    block_ref[...] = (kept_ref[...] * (resid_ref[...] + mlp_out + as_row(bias_ref))).astype(BF16)


def mlp_back_kernel(*refs):
    hiddens, ins = refs[0:4], refs[4:8]
    proj_ref, resid_ref, low_ref, gain_ref = refs[8:12]
    grad_ref, branch_ref, mixed_ref, sums_ref = refs[12:]
    grad_normed = sum(dot(h[...], w[...], 1, 1) for h, w in zip(hiddens, ins))
    unit, inverse = normalize(resid_ref[...])
    grad_rows = low_ref[...].astype(F32)
    grad = grad_rows + norm_back(grad_normed * as_row(gain_ref), unit, inverse)
    branch = grad.astype(BF16)
    grad_ref[...] = grad
    branch_ref[...] = branch
    mixed_ref[...] = dot(branch, proj_ref[...], 1, 1).astype(BF16)
    sums = stack_rows(
        [
            column_sum(branch.astype(F32)),
            column_sum(grad_normed * unit),
            column_sum(grad_normed),
            column_sum(grad_rows),
        ]
    )

    @pl.when(pl.program_id(0) == 0)
    def _():
        sums_ref[...] = sums

    @pl.when(pl.program_id(0) > 0)
    def _():
        sums_ref[...] += sums


def mlp_result(actives, outs, resid, kept_col, bias, image, slots, earlier):
    row_count, width = resid.shape
    tile = slots // 2
    block = pl.BlockSpec((tile, width), lambda i: (2 * image + i, 0))
    return pl.pallas_call(
        mlp_out_kernel,
        grid=(2,),
        in_specs=[block] * 4
        + [fixed(width, width)] * 4
        + [block, pl.BlockSpec((tile, 1), lambda i: (2 * image + i, 0)), fixed(width)]
        + [pl.BlockSpec(memory_space=pl.ANY)] * len(earlier),
        out_specs=block,
        out_shape=shape((row_count, width)),
        input_output_aliases={11: 0} if earlier else {},
        cost_estimate=cost(8 * slots * width * width, slots * width * 14),
        compiler_params=PARAMS,
    )(*actives, *outs, resid, kept_col, bias, *earlier)


def mlp_back(hiddens, ins, proj_weight, resid, grad_low, gain):
    row_count, width = resid.shape
    tile = row_count // 4
    block = pl.BlockSpec((tile, width), lambda i: (i, 0))
    return pl.pallas_call(
        mlp_back_kernel,
        grid=(4,),
        in_specs=[block] * 4
        + [fixed(width, width)] * 5
        + [block, block, fixed(width)],
        out_specs=[block, block, block, fixed(8, width)],
        out_shape=[
            shape((row_count, width), F32),
            shape((row_count, width)),
            shape((row_count, width)),
            shape((8, width), F32),
        ],
        cost_estimate=cost(10 * row_count * width * width, row_count * width * 22),
        compiler_params=PARAMS,
    )(*hiddens, *ins, proj_weight, resid, grad_low, gain)


def attend_back_kernel(
    q_ref, k_ref, v_ref, mixed_ref, grad_ref, total_ref, kept_ref, cos_ref, sin_ref, *refs
):
    packed_ref, sums_ref = refs[-2:]
    slots = q_ref.shape[0]
    low = lax.broadcasted_iota(jnp.int32, (1, LANES), 1) < HEAD
    q, k, v, grad_mixed = q_ref[...], k_ref[...], v_ref[...], grad_ref[...]
    zero = jnp.zeros_like(q)
    mask = (kept_ref[...] - 1.0) * MASKED_SCORE
    product = jnp.transpose(grad_mixed.astype(F32) * mixed_ref[...].astype(F32))
    totals = jnp.transpose(total_ref[...])
    grad_q = grad_k = grad_v = None
    for head in range(2):
        keep = low if head == 0 else ~low
        q_head = jnp.where(keep, q, zero)
        grad_head = jnp.where(keep, grad_mixed, zero)
        k_head = jnp.where(keep, k, zero)
        total = totals[head * HEAD : head * HEAD + 1]
        inner = column_sum(product[head * HEAD : (head + 1) * HEAD])
        weights = jnp.exp((dot(k, q_head, 1, 1) + mask) - total)
        grad_weights = dot(v, grad_head, 1, 1)
        grad_scores = (weights * (grad_weights - inner)).astype(BF16)
        part_v = dot(weights.astype(BF16), grad_head)
        part_k = dot(grad_scores, q_head)
        part_q = dot(grad_scores, k_head, 0, 0)
        grad_v = part_v if grad_v is None else grad_v + part_v
        grad_k = part_k if grad_k is None else grad_k + part_k
        grad_q = part_q if grad_q is None else grad_q + part_q
    turn = grad_q * swap_halves(q.astype(F32)) + grad_k * swap_halves(k.astype(F32))
    slot = lax.broadcasted_iota(jnp.int32, (slots, 1), 0)
    across = slot // GRID
    down = slot - across * GRID
    cosine, sine = cos_ref[...], sin_ref[...]
    grad_q = grad_q * (HEAD**-0.5)
    grad_q = (grad_q * cosine - swap_halves(grad_q) * sine).astype(BF16)
    grad_k = (grad_k * cosine - swap_halves(grad_k) * sine).astype(BF16)
    packed = jnp.concatenate([grad_q, grad_k, grad_v.astype(BF16)], axis=1)
    packed_ref[...] = packed
    parts = column_sum(packed.astype(F32))
    sums = stack_rows(
        [
            column_sum(turn * across.astype(F32)),
            column_sum(turn * down.astype(F32)),
            parts[:, :LANES],
            parts[:, LANES : 2 * LANES],
            parts[:, 2 * LANES :],
        ]
    )

    @pl.when(pl.program_id(0) == 0)
    def _():
        sums_ref[...] = sums

    @pl.when(pl.program_id(0) > 0)
    def _():
        sums_ref[...] += sums


def attend_back(
    qkv, mixed, grad_mixed, totals, kept_col, cosine, sine, slots, pair, count, at, earlier
):
    row_count, width = mixed.shape
    images, pairs = row_count // slots, width // LANES
    block = lambda part: pl.BlockSpec((slots, LANES), lambda i: (i, pair + part * pairs))
    table = pl.BlockSpec((slots, LANES), lambda i: (0, pair))
    return pl.pallas_call(
        attend_back_kernel,
        grid=(images,),
        in_specs=[
            block(0), block(1), block(2), block(0), block(0), block(0),
            pl.BlockSpec((slots, 1), lambda i: (i, 0)),
            table,
            table,
        ] + [pl.BlockSpec(memory_space=pl.ANY)] * len(earlier),
        out_specs=[pl.BlockSpec((slots, 3 * LANES), lambda i: (i, at)), fixed(8, LANES)],
        out_shape=[shape((row_count, count * 3 * LANES)), shape((8, LANES), F32)],
        input_output_aliases={9: 0} if earlier else {},
        cost_estimate=cost(
            40 * row_count * slots * LANES, row_count * LANES * 30, row_count * slots * 2
        ),
        compiler_params=PARAMS,
    )(qkv, qkv, qkv, mixed, grad_mixed, totals, kept_col, cosine, sine, *earlier)


def finish_kernel(count, *refs):
    packed, (weight_ref, x_ref, grad_ref, gain_ref) = refs[:count], refs[count : count + 4]
    more, (input_ref, sums_ref) = refs[count + 4 : -2], refs[-2:]
    pieces = [p[:, at : at + 3 * LANES] for p in packed for at in range(0, p.shape[1], 3 * LANES)]
    full = jnp.concatenate(
        [p[:, part * LANES : (part + 1) * LANES] for part in range(3) for p in pieces], axis=1
    )
    grad_normed = dot(full, weight_ref[...], 1, 1)
    unit, inverse = normalize(x_ref[...].astype(F32))
    input_ref[...] = (
        grad_ref[...] + norm_back(grad_normed * as_row(gain_ref), unit, inverse)
    ).astype(BF16)
    members = [column_sum(grad_normed * unit), column_sum(grad_normed)]
    step = pl.program_id(0)
    if not more:

        @pl.when(step == 0)
        def _():
            sums_ref[...] = stack_rows(members)

        @pl.when(step > 0)
        def _():
            sums_ref[...] += stack_rows(members)

    else:
        own_ref, joined_ref, hidden_refs, pair_refs, before_ref = (
            more[0], more[1], more[2:6], more[6:-2], more[-2],
        )

        @pl.when(step == 0)
        def _():
            row = lax.broadcasted_iota(jnp.int32, (8, 1), 0)
            top = jnp.zeros((8, input_ref.shape[1]), F32)
            for r, hidden in enumerate(hidden_refs):
                top = jnp.where(row == (own_ref[0] ^ r), hidden[...], top)
            low = jnp.where(row < 4, 0.0, pltpu.roll(joined_ref[...], 4, 0))
            sums_ref[0:8, :] = top + low
            pairs = jnp.concatenate([p[...] for p in pair_refs], axis=1)
            ends = pltpu.roll(before_ref[...] + stack_rows(members), 5, 0)
            sums_ref[8:16, :] = jnp.where(row < 5, pairs, ends)

        @pl.when(step > 0)
        def _():
            sums_ref[8:16, :] += pltpu.roll(stack_rows(members), 5, 0)


def finish(packed, weight, rows, grad_resid, gain, image, slots, more):
    row_count, width = rows.shape
    tile = slots // 2
    block = lambda cols: pl.BlockSpec((tile, cols), lambda i: (2 * image + i, 0))
    more_specs = [fixed(*m.shape) for m in more]
    if more:
        more_specs[0] = pl.BlockSpec(memory_space=pltpu.SMEM)
        more_specs[-1] = pl.BlockSpec(memory_space=pl.ANY)
    count = len(packed)
    sums = 16 if more else 8
    return pl.pallas_call(
        functools.partial(finish_kernel, count),
        grid=(2,),
        in_specs=[block(p.shape[1]) for p in packed]
        + [fixed(*weight.shape), block(width), block(width), fixed(width)]
        + more_specs,
        out_specs=[block(width), fixed(sums, width)],
        out_shape=[shape((row_count, width)), shape((sums, width), F32)],
        input_output_aliases={count + 3 + len(more): 0} if more else {},
        cost_estimate=cost(6 * slots * width * width, slots * width * 14),
        compiler_params=PARAMS,
    )(*packed, weight, rows, grad_resid, gain, *more)


def total(values):
    return jnp.sum(jnp.sum(values * values, axis=0, keepdims=True), axis=1, keepdims=True)


def place(blocks, pair, weight_ref, width):
    square = jnp.zeros((1, 1), F32)
    for block, start in blocks:
        for at in range(start, block.shape[1], 3 * LANES):
            for part in range(3):
                piece = block[:, at + part * LANES : at + (part + 1) * LANES].astype(F32)
                first = part * width + pair * LANES
                weight_ref[:, first : first + LANES] = piece
                square = square + total(piece)
            pair += 1
    return square


def final_early_kernel(
    first_ref, second_ref, in_ref, out_ref, weight_ref, proj_ref, fc1_ref, fc2_ref, square_ref
):
    width = proj_ref.shape[1]
    proj = first_ref[:, :width].astype(F32)
    proj_ref[...] = proj
    fc2_ref[...] = jnp.transpose(out_ref[...].astype(F32))
    square = total(proj) + place([(first_ref, width), (second_ref, 0)], 0, weight_ref, width)

    @pl.when(pl.program_id(0) == 0)
    def _():
        square_ref[...] = square
        quarter = in_ref.shape[0] // 4
        for at, source in enumerate((0, 2, 1, 3)):
            rows = slice(source * quarter, (source + 1) * quarter)
            fc1_ref[at * quarter : (at + 1) * quarter, :] = in_ref[rows, :].astype(F32)

    @pl.when(pl.program_id(0) > 0)
    def _():
        square_ref[...] += square


def final_early(first, second, mlp_in, mlp_out, width):
    depth, units = mlp_in.shape
    tile = depth // 3
    row_block = lambda cols: pl.BlockSpec((tile, cols), lambda i: (i, 0))
    return pl.pallas_call(
        final_early_kernel,
        grid=(3,),
        in_specs=[
            row_block(first.shape[1]),
            row_block(second.shape[1]),
            fixed(depth, units),
            row_block(depth),
        ],
        out_specs=[
            row_block(3 * width),
            row_block(width),
            fixed(depth, units),
            pl.BlockSpec((units, tile), lambda i: (0, i)),
            fixed(1, 1),
        ],
        out_shape=[
            shape((depth, 3 * width), F32),
            shape((depth, width), F32),
            shape((depth, units), F32),
            shape((units, depth), F32),
            shape((1, 1), F32),
        ],
        cost_estimate=cost(depth * width * 8, depth * width * 30),
        compiler_params=PARAMS,
    )(first, second, mlp_in, mlp_out)


def final_kernel(
    own_ref, side_ref, small_ref, square_ref, mine_ref, other_ref, before_ref, *outputs
):
    (
        weight_out, gain1_ref, shift1_ref, bias_ref, freq_ref, proj_bias_ref,
        gain2_ref, shift2_ref, hidden_ref, out_bias_ref, freq_norm_ref, rest_norm_ref,
        staged, sems,
    ) = outputs
    rows, width = mine_ref.shape[0], small_ref.shape[1]
    pairs = width // LANES
    late = mine_ref.shape[1] // (3 * LANES)
    first, span = (pairs - late) * LANES, late * LANES
    square = square_ref[...]
    mine, other = mine_ref[...].astype(F32), other_ref[...].astype(F32)
    square = square + total(mine) + total(other)
    lower = side_ref[0] == 0
    for top, block in ((0, jnp.where(lower, mine, other)), (rows, jnp.where(lower, other, mine))):
        for pair in range(late):
            at = pair * LANES
            for part in range(3):
                start = (3 * pair + part) * LANES
                staged[part, top : top + rows, at : at + LANES] = block[:, start : start + LANES]
    copies = [
        pltpu.make_async_copy(
            staged.at[part],
            weight_out.at[:, part * width + first : part * width + first + span],
            sems.at[part],
        )
        for part in range(3)
    ]
    for copy in copies:
        copy.start()
    small = small_ref[...]
    hidden_ref[...] = small_ref[pl.ds(own_ref[0], 1), :].reshape(width)
    for at, ref in enumerate((proj_bias_ref, gain2_ref, shift2_ref, out_bias_ref)):
        ref[...] = small[4 + at]
    bias_ref[...] = jnp.concatenate([small[10], small[11], small[12]], axis=0)
    gain1_ref[...] = small[13]
    shift1_ref[...] = small[14]
    freq_square = jnp.zeros((1, 1), F32)
    half = HEAD // 2
    for head in range(width // HEAD):
        at = head * HEAD
        turned = small_ref[8:10, at + half : at + HEAD] - small_ref[8:10, at : at + half]
        freq_ref[head, :, :] = turned
        freq_square = freq_square + total(turned)
    freq_norm_ref[...] = jnp.sqrt(freq_square)
    rest_norm_ref[...] = jnp.sqrt(square + total(small[4:8]) + total(small[10:15]))
    for copy in copies:
        copy.wait()


def final(own, side, small, square, mine, other, freq_shape, weight):
    depth, width = weight.shape[0], small.shape[1]
    late = mine.shape[1] // 3
    vector = (shape((width,), F32), fixed(width))
    outputs = [
        (shape(weight.shape, F32), pl.BlockSpec(memory_space=pl.ANY)),
        vector,
        vector,
        (shape((3 * width,), F32), fixed(3 * width)),
        (shape(freq_shape, F32), fixed(*freq_shape)),
        vector,
        vector,
        vector,
        vector,
        vector,
        (shape((1, 1), F32), fixed(1, 1)),
        (shape((1, 1), F32), fixed(1, 1)),
    ]
    return pl.pallas_call(
        final_kernel,
        grid=(1,),
        in_specs=[
            pl.BlockSpec(memory_space=pltpu.SMEM),
            pl.BlockSpec(memory_space=pltpu.SMEM),
            fixed(*small.shape),
            fixed(1, 1),
            fixed(*mine.shape),
            fixed(*other.shape),
            pl.BlockSpec(memory_space=pl.ANY),
        ],
        out_specs=[spec for _, spec in outputs],
        out_shape=[dims for dims, _ in outputs],
        scratch_shapes=[pltpu.VMEM((3, depth, late), F32), pltpu.SemaphoreType.DMA((3,))],
        input_output_aliases={6: 0},
        cost_estimate=cost(depth * width * 8, depth * width * 8),
        compiler_params=PARAMS,
    )(own, side, small, square, mine, other, weight)


class Exchange:
    def __init__(self, mesh):
        self.sizes = dict(mesh.shape)

    def bits(self, axis):
        return [(axis, 1 << b) for b in range(self.sizes[axis].bit_length() - 1)]

    def swap(self, value, step):
        axis, bit = step
        pairs = [(i, i ^ bit) for i in range(self.sizes[axis])]
        return lax.ppermute(value, axis, pairs)

    def side(self, step):
        axis, bit = step
        return (lax.axis_index(axis) // bit) % 2

    def half(self, value, step, mine, dim):
        size = value.shape[dim] // 2
        side = self.side(step)
        return lax.dynamic_slice_in_dim(value, (side if mine else 1 - side) * size, size, dim)

    def join(self, mine, other, step, dim):
        first = self.side(step) == 0
        return jnp.concatenate(
            [jnp.where(first, mine, other), jnp.where(first, other, mine)], axis=dim
        )


def add(*members):
    return sum(member.astype(F32) for member in members).astype(BF16)


def tie(*members):
    return lax.optimization_barrier(members)


class Chain:
    def __init__(self, net, value, halving, full=(), joins=None, dim=0):
        joins = list(reversed(halving)) if joins is None else joins
        self.net, self.value, self.dim = net, value, dim
        self.todo = [("halve", s) for s in halving] + [("full", s) for s in full]
        self.todo += [("join", s) for s in joins]
        self.flight = self.sent = None

    def start(self):
        if not self.todo or self.flight is not None:
            return
        self.prepare()
        self.flight = self.net.swap(self.sent, self.todo[0][1])

    def prepare(self):
        if self.sent is None:
            kind, step = self.todo[0]
            self.sent = self.value
            if kind == "halve":
                self.sent = self.net.half(self.value, step, False, self.dim)

    def end(self):
        if self.flight is None:
            return
        kind, step = self.todo.pop(0)
        if kind == "halve":
            self.value = add(self.net.half(self.value, step, True, self.dim), self.flight)
        elif kind == "full":
            total = self.value.astype(F32) + self.flight.astype(F32)
            self.value = total.astype(self.value.dtype)
        else:
            self.value = self.net.join(self.value, self.flight, step, self.dim)
        self.flight = self.sent = None


def drain(*chains, keep=0):
    for chain in chains:
        while len(chain.todo) > keep:
            chain.start()
            chain.end()


def meet(chains, *outputs, hold=()):
    flights = [c.flight for c in chains if c.flight is not None]
    for chain in hold:
        chain.prepare()
    landed, outputs, sents = tie(flights, outputs, [h.sent for h in hold])
    landed = list(landed)
    for chain, sent in zip(hold, sents):
        chain.sent = sent
    for chain in chains:
        if chain.flight is not None:
            chain.flight = landed.pop(0)
            chain.end()
    return outputs


def body(
    net,
    images,
    keep_mask,
    ln1_gain,
    ln1_bias,
    qkv_weight,
    qkv_bias,
    frequencies,
    proj_weight,
    proj_bias,
    ln2_gain,
    ln2_bias,
    fc1_weight,
    fc1_bias,
    fc2_weight,
    fc2_bias,
    out_grad,
):
    image_count, slots, width = images.shape
    row_count = image_count * slots
    inner, outer = net.bits("tensor")
    dp_steps = net.bits("dp")
    near_dp, far_dp = dp_steps[:1], dp_steps[1:]

    ins, outs = {0: fc1_weight}, {0: fc2_weight}
    ins[2], outs[2] = net.swap(fc1_weight, outer), net.swap(fc2_weight, outer)
    ins[1], outs[1] = net.swap(fc1_weight, inner), net.swap(fc2_weight, inner)
    biases = {0: fc1_bias}
    biases[1], biases[2] = net.swap(biases[0], inner), net.swap(biases[0], outer)

    rows = images.reshape(row_count, width)
    by_head = jnp.transpose(frequencies, (1, 0, 2))
    normed_one, qkv, cosine, sine = project_qkv(
        rows, ln1_gain, ln1_bias, qkv_bias, by_head, qkv_weight, slots
    )
    mixed, totals = attend(qkv, keep_mask, slots)
    resid, normed_two, grad_low, kept_col = project_out(
        mixed, rows, out_grad.reshape(row_count, width), keep_mask,
        proj_bias, ln2_gain, ln2_bias, proj_weight,
    )

    actives, hiddens, grads, bias_grads = {}, {}, {}, {}

    def chunk(r, normed, grad):
        actives[r], hiddens[r], grads[r], bias_grads[r] = hidden_units(
            normed, grad, ins[r], biases[r], outs[r]
        )

    normed_two, grad_low, ins[1], outs[1], biases[1] = tie(
        normed_two, grad_low, ins[1], outs[1], biases[1]
    )
    chunk(1, normed_two, grad_low)
    normed_two, grads[1], ins[2], outs[2], biases[2] = tie(
        normed_two, grads[1], ins[2], outs[2], biases[2]
    )
    biases[3] = net.swap(biases[2], inner)
    near = net.swap(grads[1], inner)
    ins[3], outs[3] = net.swap(ins[2], inner), net.swap(outs[2], inner)
    chunk(0, normed_two, grad_low)
    normed_two, grads[0], near, ins[3], outs[3], biases[3] = tie(
        normed_two, grads[0], near, ins[3], outs[3], biases[3]
    )
    near = add(grads[0], near)
    first_dp, second_dp = near_dp + far_dp[:1], far_dp[:1] + near_dp
    near_in = Chain(net, near[0], second_dp, joins=[])
    near_out = Chain(net, near[1], first_dp, joins=[])
    near_in.start()
    near_out.start()
    chunk(3, normed_two, grad_low)
    normed_two, grads[3] = tie(normed_two, grads[3])
    far = net.swap(grads[3], inner)
    chunk(2, normed_two, grad_low)
    far, grads[2], hiddens[2] = tie(far, grads[2], hiddens[2])
    far = add(grads[2], far)
    far_in = Chain(net, far[0], second_dp, joins=[])
    far_out = Chain(net, far[1], first_dp, joins=[])
    far_in.start()
    far_out.start()
    ranks = range(4)
    grad_resid, grad_branch, grad_mixed, joined = mlp_back(
        [hiddens[r] for r in ranks], [ins[r] for r in ranks],
        proj_weight, resid, grad_low, ln2_gain,
    )
    halves = [near_in, near_out, far_in, far_out]
    grad_branch, grad_mixed = meet(halves, grad_branch, grad_mixed)
    for half in halves:
        half.start()
    proj_grad = dot(mixed, grad_branch, 0, 0).astype(BF16)

    pair_sums = {}

    def back(pair, grad, count=1, at=0, earlier=()):
        packed, pair_sums[pair] = attend_back(
            qkv, mixed, grad, totals, kept_col, cosine, sine, slots, pair, count, at, earlier
        )
        return packed

    def weight_grad(packed):
        return dot(normed_one, packed, 0, 0).astype(BF16)

    def group(value):
        return Chain(net, value, [inner, outer] + near_dp, far_dp)

    def begin(*chains):
        for chain in chains:
            chain.start()

    def gather(near, cross):
        return Chain(net, add(near.value, cross), [], far_dp[1:], far_dp[:1] + near_dp)

    packed_a = back(0, grad_mixed, 2, 0)
    grad_mixed, packed_a, proj_grad = meet(halves, grad_mixed, packed_a, proj_grad)
    cross_in, cross_out = net.swap(far_in.value, outer), net.swap(far_out.value, outer)
    packed_a = back(1, grad_mixed, 2, 1, [packed_a])
    grad_mixed, cross_in, cross_out, *first = tie(
        grad_mixed, cross_in, cross_out, proj_grad, weight_grad(packed_a)
    )
    mlp_in, mlp_out = gather(near_in, cross_in), gather(near_out, cross_out)
    group_a = group(jnp.concatenate(first, axis=1))
    begin(mlp_out, group_a)
    packed_b = back(2, grad_mixed, 2, 0)
    grad_mixed, packed_b = meet([mlp_out, group_a], grad_mixed, packed_b, hold=[mlp_in])
    begin(mlp_in, group_a)
    packed_b = back(3, grad_mixed, 2, 1, [packed_b])
    grad_mixed, grad_b = meet(
        [mlp_in, group_a], grad_mixed, weight_grad(packed_b), hold=[mlp_out]
    )
    group_b = group(grad_b)
    begin(mlp_in, mlp_out, group_a, group_b)
    packed_c = back(4, grad_mixed, 2, 0)
    grad_mixed, packed_c = meet(
        [mlp_in, mlp_out, group_a, group_b], grad_mixed, packed_c
    )
    begin(mlp_out, group_a, group_b)
    packed_c = back(5, grad_mixed, 2, 1, [packed_c])
    packed_c, grad_c = meet([group_a, group_b], packed_c, weight_grad(packed_c))
    group_c = group(grad_c)
    begin(group_a, group_b, group_c)

    packed = [packed_a, packed_b, packed_c]
    own_list = lax.axis_index("tensor").astype(jnp.int32).reshape(1)
    groups = [group_a, group_b, group_c]
    input_grad, half_sums = finish(
        packed, qkv_weight, rows, grad_resid, ln1_gain, 0, slots, ()
    )
    input_grad, half_sums = meet(
        [mlp_out, group_b, group_c], input_grad, half_sums, hold=[mlp_in]
    )
    begin(mlp_in, group_b, group_c)
    input_grad, small = finish(
        packed, qkv_weight, rows, grad_resid, ln1_gain, 1, slots,
        [own_list, joined, *[bias_grads[r] for r in ranks], *[pair_sums[p] for p in range(6)],
         half_sums, input_grad],
    )
    small, actives[0] = meet(groups, small, actives[0])
    small = Chain(net, small, [], near_dp + [inner, outer] + far_dp)
    groups.append(small)
    begin(*groups)
    result = lambda image, earlier: mlp_result(
        [actives[r] for r in ranks], [outs[r] for r in ranks],
        resid, kept_col, fc2_bias, image, slots, earlier,
    )
    block_out = result(0, ())
    (block_out,) = meet(groups, block_out)
    begin(*groups)
    block_out = result(1, (block_out,))
    (block_out,) = meet([mlp_in, *groups], block_out)
    begin(*groups)
    meet(groups)
    begin(*groups)
    meet(groups)
    begin(*groups)
    drain(group_a, group_b, mlp_in, mlp_out)
    early = final_early(group_a.value, group_b.value, mlp_in.value, mlp_out.value, width)
    qkv_begun, proj_weight_grad, fc1_weight_grad, fc2_weight_grad, square = meet(groups, *early)
    drain(group_c, keep=1)
    drain(small)
    begin(group_c)
    side = net.side(inner).astype(jnp.int32).reshape(1)
    (
        qkv_weight_grad, ln1_gain_grad, ln1_bias_grad, qkv_bias_grad,
        freq_grad, proj_bias_grad, ln2_gain_grad, ln2_bias_grad, fc1_bias_grad, fc2_bias_grad,
        freq_norm, rest_norm,
    ) = final(
        own_list, side, small.value, square, group_c.value, group_c.flight,
        by_head.shape, qkv_begun,
    )
    return (
        block_out.reshape(images.shape),
        input_grad.reshape(images.shape),
        ln1_gain_grad,
        ln1_bias_grad,
        qkv_weight_grad,
        qkv_bias_grad,
        jnp.transpose(freq_grad, (1, 0, 2)),
        proj_weight_grad,
        proj_bias_grad,
        ln2_gain_grad,
        ln2_bias_grad,
        fc1_weight_grad,
        fc1_bias_grad,
        fc2_weight_grad,
        fc2_bias_grad,
        freq_norm.reshape(()),
        rest_norm.reshape(()),
    )


def solution(mesh):
    rows = P(("dp", "tensor"), None, None)
    whole = P()
    hidden_in, hidden_out = P(None, "tensor"), P("tensor", None)
    return jax.shard_map(
        functools.partial(body, Exchange(mesh)),
        mesh=mesh,
        in_specs=(
            (rows, P(("dp", "tensor"), None))
            + (whole,) * 9
            + (hidden_in, P("tensor"), hidden_out, whole, rows)
        ),
        out_specs=(
            (rows, rows) + (whole,) * 9 + (hidden_in, P("tensor"), hidden_out) + (whole,) * 3
        ),
        check_vma=False,
    )
```

```python
import functools

import jax
import jax.numpy as jnp
from jax import lax
from jax.experimental import pallas as pl
from jax.experimental.pallas import tpu as pltpu
from jax.sharding import PartitionSpec as P

GRID = 24
EPSILON = 1e-06
MASKED_SCORE = 1e30
ROOT_HALF = 0.7071067811865476
DENSITY_SCALE = 0.3989422804014327
F32 = jnp.float32
BF16 = jnp.bfloat16
LANES = 128
HEAD = 64
HIDDEN_TILE = 256
EMPHASIS = 20
EARLY = pltpu.CompilerParams(vmem_limit_bytes=56 << 20)
CHUNK = pltpu.CompilerParams(vmem_limit_bytes=24 << 20)
PARAMS = pltpu.CompilerParams(vmem_limit_bytes=32 << 20)


def dot(left, right, left_dim=1, right_dim=0):
    return lax.dot_general(
        left, right, (((left_dim,), (right_dim,)), ((), ())), preferred_element_type=F32
    )


def normalize(row_data):
    row_mean = jnp.mean(row_data, axis=-1, keepdims=True)
    centred = row_data - row_mean
    inverse = lax.rsqrt(jnp.mean(centred * centred, axis=-1, keepdims=True) + EPSILON)
    return (centred * inverse, inverse)


def norm_back(grad_unit, unit_rows, inverse):
    return inverse * (
        grad_unit
        - jnp.mean(grad_unit, axis=-1, keepdims=True)
        - unit_rows * jnp.mean(grad_unit * unit_rows, axis=-1, keepdims=True)
    )


def swap_halves(tile):
    lane = lax.broadcasted_iota(jnp.int32, (1, LANES), 1)
    first = (lane % HEAD) < HEAD // 2
    return jnp.where(
        first, pltpu.roll(tile, LANES - HEAD // 2, 1), pltpu.roll(tile, HEAD // 2, 1)
    )


def as_row(ref):
    return ref[...].astype(F32).reshape(1, -1)


def column_sum(values):
    return jnp.sum(values, axis=0, keepdims=True)


def stack_rows(members):
    width = members[0].shape[1]
    row = lax.broadcasted_iota(jnp.int32, (8, width), 0)
    total = jnp.zeros((8, width), F32)
    for at, member in enumerate(members):
        total = jnp.where(row == at, member, total)
    return total


def shape(dims, dtype=BF16):
    return jax.ShapeDtypeStruct(dims, dtype)


def fixed(*dims):
    return pl.BlockSpec(dims, lambda *_: (0,) * len(dims))


def cost(flops, moved, steep=0):
    return pl.CostEstimate(flops=EMPHASIS * flops, bytes_accessed=moved, transcendentals=steep)


def qkv_kernel(
    x_ref, gain_ref, shift_ref, bias_ref, freq_ref, weight_ref,
    normed_ref, qkv_ref, cos_ref, sin_ref, lanes_ref,
):
    tile, width = x_ref.shape
    across_count = tile // GRID

    @pl.when(pl.program_id(1) == 0)
    def _():
        half = HEAD // 2
        for head in range(width // HEAD):
            for at in (head * HEAD, head * HEAD + half):
                lanes_ref[0:2, at : at + half] = freq_ref[head, :, :]
        first = (pl.program_id(0) * across_count).astype(F32)
        padded = -(-across_count // 8) * 8
        across = first + lax.broadcasted_iota(jnp.int32, (padded, width), 0).astype(F32)
        down = lax.broadcasted_iota(jnp.int32, (GRID, width), 0).astype(F32)
        across = across * lanes_ref[0:1, :]
        down = down * lanes_ref[1:2, :]
        cos_a, sin_a, cos_d, sin_d = jnp.cos(across), jnp.sin(across), jnp.cos(down), jnp.sin(down)
        lane = lax.broadcasted_iota(jnp.int32, (1, width), 1)
        sign = jnp.where((lane % HEAD) < HEAD // 2, -1.0, 1.0)
        for at in range(across_count):
            rows = slice(at * GRID, (at + 1) * GRID)
            one_cos, one_sin = cos_a[at : at + 1], sin_a[at : at + 1]
            cos_ref[rows, :] = one_cos * cos_d - one_sin * sin_d
            sin_ref[rows, :] = (one_sin * cos_d + one_cos * sin_d) * sign

    unit, _ = normalize(x_ref[...].astype(F32))
    normed = (unit * as_row(gain_ref) + as_row(shift_ref)).astype(BF16)
    normed_ref[...] = normed
    bias = as_row(bias_ref)
    for part in range(3):
        cols = slice(part * width, (part + 1) * width)
        packed = dot(normed, weight_ref[:, cols]) + bias[:, cols]
        for at in range(0, width, LANES):
            piece = packed[:, at : at + LANES]
            if part < 2:
                cosine, sine = cos_ref[:, at : at + LANES], sin_ref[:, at : at + LANES]
                piece = piece * cosine + swap_halves(piece) * sine
            if part == 0:
                piece = piece * (HEAD**-0.5)
            qkv_ref[:, part * width + at : part * width + at + LANES] = piece.astype(BF16)


def project_qkv(rows, gain, shift, bias, frequencies, weight, slots):
    row_count, width = rows.shape
    halves = 1
    tile = slots // halves
    row_block = lambda cols: pl.BlockSpec((tile, cols), lambda h, n: (n * halves + h, 0))
    table = pl.BlockSpec((tile, width), lambda h, n: (h, 0))
    return pl.pallas_call(
        qkv_kernel,
        grid=(halves, row_count // slots),
        in_specs=[
            row_block(width),
            fixed(width),
            fixed(width),
            fixed(3 * width),
            fixed(*frequencies.shape),
            fixed(*weight.shape),
        ],
        out_specs=[row_block(width), row_block(3 * width), table, table],
        out_shape=[
            shape((row_count, width)),
            shape((row_count, 3 * width)),
            shape((slots, width), F32),
            shape((slots, width), F32),
        ],
        scratch_shapes=[pltpu.VMEM((8, width), F32)],
        cost_estimate=cost(6 * row_count * width * width, row_count * width * 14),
        compiler_params=EARLY,
    )(rows, gain, shift, bias, frequencies, weight)


def attend_kernel(q_ref, k_ref, v_ref, mask_ref, mixed_ref, total_ref):
    low = lax.broadcasted_iota(jnp.int32, (1, LANES), 1) < HEAD
    queries, keys, values = q_ref[...], k_ref[...], v_ref[...]
    zero = jnp.zeros_like(queries)
    mask = (mask_ref[pl.ds(pl.program_id(0), 1), :].astype(F32) - 1.0) * MASKED_SCORE
    mask = jnp.transpose(jnp.broadcast_to(mask, (8, mask.shape[1])))[:, 0:1]
    mixed, totals = None, []
    for head in range(2):
        keep = low if head == 0 else ~low
        scores = dot(keys, jnp.where(keep, queries, zero), 1, 1) + mask
        top = jnp.max(scores, axis=0, keepdims=True)
        weights = jnp.exp(scores - top)
        total = column_sum(weights)
        low_weights = (weights * (1.0 / total)).astype(BF16)
        part = dot(jnp.where(keep, values, zero), low_weights, 0, 0)
        mixed = part if mixed is None else mixed + part
        totals.append(top + jnp.log(total))
    mixed_ref[...] = jnp.transpose(mixed).astype(BF16)
    row = lax.broadcasted_iota(jnp.int32, (8, 1), 0)
    total_ref[0] = jnp.where(row == 0, totals[0], totals[1])


def attend(qkv, keep_mask, slots):
    row_count, width = qkv.shape[0], qkv.shape[1] // 3
    images, pairs = row_count // slots, width // LANES
    block = lambda part: pl.BlockSpec((slots, LANES), lambda i, p: (i, p + part * pairs))
    return pl.pallas_call(
        attend_kernel,
        grid=(images, pairs),
        in_specs=[
            block(0),
            block(1),
            block(2),
            fixed(*keep_mask.shape),
        ],
        out_specs=[block(0), pl.BlockSpec((1, 8, slots), lambda i, p: (i, p, 0))],
        out_shape=[shape((row_count, width)), shape((images, 8 * pairs, slots), F32)],
        cost_estimate=cost(
            16 * row_count * slots * width, row_count * width * 12, row_count * slots * 2 * pairs
        ),
        compiler_params=EARLY,
    )(qkv, qkv, qkv, keep_mask)


def project_kernel(
    mixed_ref, x_ref, grad_ref, mask_ref, bias_ref, gain_ref, shift_ref, weight_ref,
    resid_ref, normed_ref, low_ref, kept_ref,
):
    row = mask_ref[pl.ds(pl.program_id(0), 1), :].astype(F32)
    kept = jnp.transpose(jnp.broadcast_to(row, (8, row.shape[1])))[:, 0:1]
    resid = x_ref[...].astype(F32) + dot(mixed_ref[...], weight_ref[...]) + as_row(bias_ref)
    unit, _ = normalize(resid)
    resid_ref[...] = resid
    normed_ref[...] = (unit * as_row(gain_ref) + as_row(shift_ref)).astype(BF16)
    low_ref[...] = (kept * grad_ref[...].astype(F32)).astype(BF16)
    kept_ref[...] = kept


def project_out(mixed, rows, out_grad, keep_mask, bias, gain, shift, weight):
    row_count, width = rows.shape
    images, slots = keep_mask.shape
    block = pl.BlockSpec((slots, width), lambda i: (i, 0))
    return pl.pallas_call(
        project_kernel,
        grid=(images,),
        in_specs=[block, block, block, fixed(images, slots)]
        + [fixed(width)] * 3
        + [fixed(*weight.shape)],
        out_specs=[block, block, block, pl.BlockSpec((slots, 1), lambda i: (i, 0))],
        out_shape=[
            shape((row_count, width), F32),
            shape((row_count, width)),
            shape((row_count, width)),
            shape((row_count, 1), F32),
        ],
        cost_estimate=cost(2 * row_count * width * width, row_count * width * 14),
        compiler_params=EARLY,
    )(mixed, rows, out_grad, keep_mask, bias, gain, shift, weight)


def hidden_kernel(
    normed_ref, grad_ref, in_ref, bias_ref, out_ref,
    active_ref, hidden_ref, weights_ref, bias_grad_ref,
):
    normed, grad = normed_ref[...], grad_ref[...]
    hidden = dot(normed, in_ref[...]) + as_row(bias_ref)
    grad_active = dot(grad, out_ref[...], 1, 1)
    half = 0.5 * (1.0 + lax.erf(hidden * ROOT_HALF))
    active = (hidden * half).astype(BF16)
    slope = half + hidden * jnp.exp(-0.5 * hidden * hidden) * DENSITY_SCALE
    grad_hidden = (grad_active * slope).astype(BF16)
    active_ref[...] = active
    hidden_ref[...] = grad_hidden
    weights_ref[0] = dot(normed, grad_hidden, 0, 0).astype(BF16)
    weights_ref[1] = dot(grad, active, 0, 0).astype(BF16)
    bias_grad_ref[...] = column_sum(grad_hidden.astype(F32))


def hidden_units(normed, grad, weight_in, bias_in, weight_out):
    row_count, width = normed.shape
    units = weight_in.shape[1]
    tile = HIDDEN_TILE
    cols = lambda rows: pl.BlockSpec((rows, tile), lambda i: (0, i))
    rows = pl.BlockSpec((tile, width), lambda i: (i, 0))
    return pl.pallas_call(
        hidden_kernel,
        grid=(units // tile,),
        in_specs=[
            fixed(row_count, width), fixed(row_count, width), cols(width),
            pl.BlockSpec((tile,), lambda i: (i,)), rows
        ],
        out_specs=[
            cols(row_count),
            cols(row_count),
            pl.BlockSpec((2, width, tile), lambda i: (0, 0, i)),
            cols(1),
        ],
        out_shape=[
            shape((row_count, units)),
            shape((row_count, units)),
            shape((2, width, units)),
            shape((1, units), F32),
        ],
        cost_estimate=cost(
            8 * row_count * width * units, row_count * width * 8 + width * units * 8,
            2 * row_count * units,
        ),
        compiler_params=CHUNK,
    )(normed, grad, weight_in, bias_in, weight_out)


def mlp_out_kernel(*refs):
    actives, outs = refs[0:4], refs[4:8]
    resid_ref, kept_ref, bias_ref = refs[8:11]
    block_ref = refs[-1]
    mlp_out = sum(dot(a[...], w[...]) for a, w in zip(actives, outs))
    block_ref[...] = (kept_ref[...] * (resid_ref[...] + mlp_out + as_row(bias_ref))).astype(BF16)


def mlp_back_kernel(*refs):
    hiddens, ins = refs[0:4], refs[4:8]
    proj_ref, resid_ref, low_ref, gain_ref = refs[8:12]
    grad_ref, branch_ref, mixed_ref, sums_ref = refs[12:]
    grad_normed = sum(dot(h[...], w[...], 1, 1) for h, w in zip(hiddens, ins))
    unit, inverse = normalize(resid_ref[...])
    grad_rows = low_ref[...].astype(F32)
    grad = grad_rows + norm_back(grad_normed * as_row(gain_ref), unit, inverse)
    branch = grad.astype(BF16)
    grad_ref[...] = grad
    branch_ref[...] = branch
    mixed_ref[...] = dot(branch, proj_ref[...], 1, 1).astype(BF16)
    sums = stack_rows(
        [
            column_sum(branch.astype(F32)),
            column_sum(grad_normed * unit),
            column_sum(grad_normed),
            column_sum(grad_rows),
        ]
    )

    @pl.when(pl.program_id(0) == 0)
    def _():
        sums_ref[...] = sums

    @pl.when(pl.program_id(0) > 0)
    def _():
        sums_ref[...] += sums


def mlp_result(actives, outs, resid, kept_col, bias, image, slots, earlier):
    row_count, width = resid.shape
    tile = slots // 2
    block = pl.BlockSpec((tile, width), lambda i: (2 * image + i, 0))
    return pl.pallas_call(
        mlp_out_kernel,
        grid=(2,),
        in_specs=[block] * 4
        + [fixed(width, width)] * 4
        + [block, pl.BlockSpec((tile, 1), lambda i: (2 * image + i, 0)), fixed(width)]
        + [pl.BlockSpec(memory_space=pl.ANY)] * len(earlier),
        out_specs=block,
        out_shape=shape((row_count, width)),
        input_output_aliases={11: 0} if earlier else {},
        cost_estimate=cost(8 * slots * width * width, slots * width * 14),
        compiler_params=PARAMS,
    )(*actives, *outs, resid, kept_col, bias, *earlier)


def mlp_back(hiddens, ins, proj_weight, resid, grad_low, gain):
    row_count, width = resid.shape
    tile = row_count // 2
    block = pl.BlockSpec((tile, width), lambda i: (i, 0))
    return pl.pallas_call(
        mlp_back_kernel,
        grid=(2,),
        in_specs=[block] * 4
        + [fixed(width, width)] * 5
        + [block, block, fixed(width)],
        out_specs=[block, block, block, fixed(8, width)],
        out_shape=[
            shape((row_count, width), F32),
            shape((row_count, width)),
            shape((row_count, width)),
            shape((8, width), F32),
        ],
        cost_estimate=cost(10 * row_count * width * width, row_count * width * 22),
        compiler_params=PARAMS,
    )(*hiddens, *ins, proj_weight, resid, grad_low, gain)


def attend_back_kernel(
    q_ref, k_ref, v_ref, mixed_ref, grad_ref, total_ref, kept_ref, cos_ref, sin_ref, *refs
):
    packed_ref, sums_ref = refs[-2:]
    slots = q_ref.shape[0]
    low = lax.broadcasted_iota(jnp.int32, (1, LANES), 1) < HEAD
    q, k, v, grad_mixed = q_ref[...], k_ref[...], v_ref[...], grad_ref[...]
    zero = jnp.zeros_like(q)
    mask = (kept_ref[...] - 1.0) * MASKED_SCORE
    product = jnp.transpose(grad_mixed.astype(F32) * mixed_ref[...].astype(F32))
    grad_q = grad_k = grad_v = None
    for head in range(2):
        keep = low if head == 0 else ~low
        q_head = jnp.where(keep, q, zero)
        grad_head = jnp.where(keep, grad_mixed, zero)
        k_head = jnp.where(keep, k, zero)
        total = total_ref[0, head : head + 1, :]
        inner = column_sum(product[head * HEAD : (head + 1) * HEAD])
        weights = jnp.exp((dot(k, q_head, 1, 1) + mask) - total)
        grad_weights = dot(v, grad_head, 1, 1)
        grad_scores = (weights * (grad_weights - inner)).astype(BF16)
        part_v = dot(weights.astype(BF16), grad_head)
        part_k = dot(grad_scores, q_head)
        part_q = dot(grad_scores, k_head, 0, 0)
        grad_v = part_v if grad_v is None else grad_v + part_v
        grad_k = part_k if grad_k is None else grad_k + part_k
        grad_q = part_q if grad_q is None else grad_q + part_q
    turn = grad_q * swap_halves(q.astype(F32)) + grad_k * swap_halves(k.astype(F32))
    slot = lax.broadcasted_iota(jnp.int32, (slots, 1), 0)
    across = slot // GRID
    down = slot - across * GRID
    cosine, sine = cos_ref[...], sin_ref[...]
    grad_q = grad_q * (HEAD**-0.5)
    grad_q = (grad_q * cosine - swap_halves(grad_q) * sine).astype(BF16)
    grad_k = (grad_k * cosine - swap_halves(grad_k) * sine).astype(BF16)
    packed = jnp.concatenate([grad_q, grad_k, grad_v.astype(BF16)], axis=1)
    packed_ref[...] = packed
    parts = column_sum(packed.astype(F32))
    sums = stack_rows(
        [
            column_sum(turn * across.astype(F32)),
            column_sum(turn * down.astype(F32)),
            parts[:, :LANES],
            parts[:, LANES : 2 * LANES],
            parts[:, 2 * LANES :],
        ]
    )

    @pl.when(pl.program_id(0) == 0)
    def _():
        sums_ref[...] = sums

    @pl.when(pl.program_id(0) > 0)
    def _():
        sums_ref[...] += sums


def attend_back(
    qkv, mixed, grad_mixed, totals, kept_col, cosine, sine, slots, pair, count, at, earlier
):
    row_count, width = mixed.shape
    images, pairs = row_count // slots, width // LANES
    block = lambda part: pl.BlockSpec((slots, LANES), lambda i: (i, pair + part * pairs))
    table = pl.BlockSpec((slots, LANES), lambda i: (0, pair))
    return pl.pallas_call(
        attend_back_kernel,
        grid=(images,),
        in_specs=[
            block(0), block(1), block(2), block(0), block(0),
            pl.BlockSpec((1, 8, slots), lambda i: (i, pair, 0)),
            pl.BlockSpec((slots, 1), lambda i: (i, 0)),
            table,
            table,
        ] + [pl.BlockSpec(memory_space=pl.ANY)] * len(earlier),
        out_specs=[pl.BlockSpec((slots, 3 * LANES), lambda i: (i, at)), fixed(8, LANES)],
        out_shape=[shape((row_count, count * 3 * LANES)), shape((8, LANES), F32)],
        input_output_aliases={9: 0} if earlier else {},
        cost_estimate=cost(
            40 * row_count * slots * LANES, row_count * LANES * 30, row_count * slots * 2
        ),
        compiler_params=PARAMS,
    )(qkv, qkv, qkv, mixed, grad_mixed, totals, kept_col, cosine, sine, *earlier)


def finish_kernel(count, *refs):
    packed, (weight_ref, x_ref, grad_ref, gain_ref) = refs[:count], refs[count : count + 4]
    more, (input_ref, sums_ref) = refs[count + 4 : -2], refs[-2:]
    pieces = [p[:, at : at + 3 * LANES] for p in packed for at in range(0, p.shape[1], 3 * LANES)]
    full = jnp.concatenate(
        [p[:, part * LANES : (part + 1) * LANES] for part in range(3) for p in pieces], axis=1
    )
    grad_normed = dot(full, weight_ref[...], 1, 1)
    unit, inverse = normalize(x_ref[...].astype(F32))
    input_ref[...] = (
        grad_ref[...] + norm_back(grad_normed * as_row(gain_ref), unit, inverse)
    ).astype(BF16)
    members = [column_sum(grad_normed * unit), column_sum(grad_normed)]
    step = pl.program_id(0)
    if not more:

        @pl.when(step == 0)
        def _():
            sums_ref[...] = stack_rows(members)

        @pl.when(step > 0)
        def _():
            sums_ref[...] += stack_rows(members)

    else:
        own_ref, joined_ref, hidden_refs, pair_refs, before_ref = (
            more[0], more[1], more[2:6], more[6:-2], more[-2],
        )

        @pl.when(step == 0)
        def _():
            row = lax.broadcasted_iota(jnp.int32, (8, 1), 0)
            top = jnp.zeros((8, input_ref.shape[1]), F32)
            for r, hidden in enumerate(hidden_refs):
                top = jnp.where(row == (own_ref[0] ^ r), hidden[...], top)
            low = jnp.where(row < 4, 0.0, pltpu.roll(joined_ref[...], 4, 0))
            sums_ref[0:8, :] = top + low
            pairs = jnp.concatenate([p[...] for p in pair_refs], axis=1)
            ends = pltpu.roll(before_ref[...] + stack_rows(members), 5, 0)
            sums_ref[8:16, :] = jnp.where(row < 5, pairs, ends)

        @pl.when(step > 0)
        def _():
            sums_ref[8:16, :] += pltpu.roll(stack_rows(members), 5, 0)


def finish(packed, weight, rows, grad_resid, gain, image, slots, more):
    row_count, width = rows.shape
    tile = slots // 2
    block = lambda cols: pl.BlockSpec((tile, cols), lambda i: (2 * image + i, 0))
    more_specs = [fixed(*m.shape) for m in more]
    if more:
        more_specs[0] = pl.BlockSpec(memory_space=pltpu.SMEM)
        more_specs[-1] = pl.BlockSpec(memory_space=pl.ANY)
    count = len(packed)
    sums = 16 if more else 8
    return pl.pallas_call(
        functools.partial(finish_kernel, count),
        grid=(2,),
        in_specs=[block(p.shape[1]) for p in packed]
        + [fixed(*weight.shape), block(width), block(width), fixed(width)]
        + more_specs,
        out_specs=[block(width), fixed(sums, width)],
        out_shape=[shape((row_count, width)), shape((sums, width), F32)],
        input_output_aliases={count + 3 + len(more): 0} if more else {},
        cost_estimate=cost(6 * slots * width * width, slots * width * 14),
        compiler_params=PARAMS,
    )(*packed, weight, rows, grad_resid, gain, *more)


def total(values):
    return jnp.sum(jnp.sum(values * values, axis=0, keepdims=True), axis=1, keepdims=True)


def place(blocks, pair, weight_ref, width):
    square = jnp.zeros((1, 1), F32)
    for block, start in blocks:
        for at in range(start, block.shape[1], 3 * LANES):
            for part in range(3):
                piece = block[:, at + part * LANES : at + (part + 1) * LANES].astype(F32)
                first = part * width + pair * LANES
                weight_ref[:, first : first + LANES] = piece
                square = square + total(piece)
            pair += 1
    return square


def final_early_kernel(
    first_ref, second_ref, in_ref, out_ref, weight_ref, proj_ref, fc1_ref, fc2_ref, square_ref
):
    width = proj_ref.shape[1]
    proj = first_ref[:, :width].astype(F32)
    proj_ref[...] = proj
    fc2_ref[...] = jnp.transpose(out_ref[...].astype(F32))
    square = total(proj) + place([(first_ref, width), (second_ref, 0)], 0, weight_ref, width)

    @pl.when(pl.program_id(0) == 0)
    def _():
        square_ref[...] = square
        quarter = in_ref.shape[0] // 4
        for at, source in enumerate((0, 2, 1, 3)):
            rows = slice(source * quarter, (source + 1) * quarter)
            fc1_ref[at * quarter : (at + 1) * quarter, :] = in_ref[rows, :].astype(F32)

    @pl.when(pl.program_id(0) > 0)
    def _():
        square_ref[...] += square


def final_early(first, second, mlp_in, mlp_out, width):
    depth, units = mlp_in.shape
    tile = depth // 3
    row_block = lambda cols: pl.BlockSpec((tile, cols), lambda i: (i, 0))
    return pl.pallas_call(
        final_early_kernel,
        grid=(3,),
        in_specs=[
            row_block(first.shape[1]),
            row_block(second.shape[1]),
            fixed(depth, units),
            row_block(depth),
        ],
        out_specs=[
            row_block(3 * width),
            row_block(width),
            fixed(depth, units),
            pl.BlockSpec((units, tile), lambda i: (0, i)),
            fixed(1, 1),
        ],
        out_shape=[
            shape((depth, 3 * width), F32),
            shape((depth, width), F32),
            shape((depth, units), F32),
            shape((units, depth), F32),
            shape((1, 1), F32),
        ],
        cost_estimate=cost(depth * width * 8, depth * width * 30),
        compiler_params=PARAMS,
    )(first, second, mlp_in, mlp_out)


def final_kernel(
    own_ref, side_ref, small_ref, square_ref, mine_ref, other_ref, before_ref, *outputs
):
    (
        weight_out, gain1_ref, shift1_ref, bias_ref, freq_ref, proj_bias_ref,
        gain2_ref, shift2_ref, hidden_ref, out_bias_ref, freq_norm_ref, rest_norm_ref,
        staged, sems,
    ) = outputs
    rows, width = mine_ref.shape[0], small_ref.shape[1]
    pairs = width // LANES
    late = mine_ref.shape[1] // (3 * LANES)
    first, span = (pairs - late) * LANES, late * LANES
    square = square_ref[...]
    mine, other = mine_ref[...].astype(F32), other_ref[...].astype(F32)
    square = square + total(mine) + total(other)
    lower = side_ref[0] == 0
    for top, block in ((0, jnp.where(lower, mine, other)), (rows, jnp.where(lower, other, mine))):
        for pair in range(late):
            at = pair * LANES
            for part in range(3):
                start = (3 * pair + part) * LANES
                staged[part, top : top + rows, at : at + LANES] = block[:, start : start + LANES]
    copies = [
        pltpu.make_async_copy(
            staged.at[part],
            weight_out.at[:, part * width + first : part * width + first + span],
            sems.at[part],
        )
        for part in range(3)
    ]
    for copy in copies:
        copy.start()
    small = small_ref[...]
    hidden_ref[...] = small_ref[pl.ds(own_ref[0], 1), :].reshape(width)
    for at, ref in enumerate((proj_bias_ref, gain2_ref, shift2_ref, out_bias_ref)):
        ref[...] = small[4 + at]
    bias_ref[...] = jnp.concatenate([small[10], small[11], small[12]], axis=0)
    gain1_ref[...] = small[13]
    shift1_ref[...] = small[14]
    freq_square = jnp.zeros((1, 1), F32)
    half = HEAD // 2
    for head in range(width // HEAD):
        at = head * HEAD
        turned = small_ref[8:10, at + half : at + HEAD] - small_ref[8:10, at : at + half]
        freq_ref[head, :, :] = turned
        freq_square = freq_square + total(turned)
    freq_norm_ref[...] = jnp.sqrt(freq_square)
    rest_norm_ref[...] = jnp.sqrt(square + total(small[4:8]) + total(small[10:15]))
    for copy in copies:
        copy.wait()


def final(own, side, small, square, mine, other, freq_shape, weight):
    depth, width = weight.shape[0], small.shape[1]
    late = mine.shape[1] // 3
    vector = (shape((width,), F32), fixed(width))
    outputs = [
        (shape(weight.shape, F32), pl.BlockSpec(memory_space=pl.ANY)),
        vector,
        vector,
        (shape((3 * width,), F32), fixed(3 * width)),
        (shape(freq_shape, F32), fixed(*freq_shape)),
        vector,
        vector,
        vector,
        vector,
        vector,
        (shape((1, 1), F32), fixed(1, 1)),
        (shape((1, 1), F32), fixed(1, 1)),
    ]
    return pl.pallas_call(
        final_kernel,
        grid=(1,),
        in_specs=[
            pl.BlockSpec(memory_space=pltpu.SMEM),
            pl.BlockSpec(memory_space=pltpu.SMEM),
            fixed(*small.shape),
            fixed(1, 1),
            fixed(*mine.shape),
            fixed(*other.shape),
            pl.BlockSpec(memory_space=pl.ANY),
        ],
        out_specs=[spec for _, spec in outputs],
        out_shape=[dims for dims, _ in outputs],
        scratch_shapes=[pltpu.VMEM((3, depth, late), F32), pltpu.SemaphoreType.DMA((3,))],
        input_output_aliases={6: 0},
        cost_estimate=cost(depth * width * 8, depth * width * 8),
        compiler_params=PARAMS,
    )(own, side, small, square, mine, other, weight)


class Exchange:
    def __init__(self, mesh):
        self.sizes = dict(mesh.shape)

    def bits(self, axis):
        return [(axis, 1 << b) for b in range(self.sizes[axis].bit_length() - 1)]

    def swap(self, value, step):
        axis, bit = step
        pairs = [(i, i ^ bit) for i in range(self.sizes[axis])]
        return lax.ppermute(value, axis, pairs)

    def side(self, step):
        axis, bit = step
        return (lax.axis_index(axis) // bit) % 2

    def half(self, value, step, mine, dim):
        size = value.shape[dim] // 2
        side = self.side(step)
        return lax.dynamic_slice_in_dim(value, (side if mine else 1 - side) * size, size, dim)

    def join(self, mine, other, step, dim):
        first = self.side(step) == 0
        return jnp.concatenate(
            [jnp.where(first, mine, other), jnp.where(first, other, mine)], axis=dim
        )


def add(*members):
    return sum(member.astype(F32) for member in members).astype(BF16)


def tie(*members):
    return lax.optimization_barrier(members)


class Chain:
    def __init__(self, net, value, halving, full=(), joins=None, dim=0):
        joins = list(reversed(halving)) if joins is None else joins
        self.net, self.value, self.dim = net, value, dim
        self.todo = [("halve", s) for s in halving] + [("full", s) for s in full]
        self.todo += [("join", s) for s in joins]
        self.flight = self.sent = None

    def start(self):
        if not self.todo or self.flight is not None:
            return
        self.prepare()
        self.flight = self.net.swap(self.sent, self.todo[0][1])

    def prepare(self):
        if self.sent is None:
            kind, step = self.todo[0]
            self.sent = self.value
            if kind == "halve":
                self.sent = self.net.half(self.value, step, False, self.dim)

    def end(self):
        if self.flight is None:
            return
        kind, step = self.todo.pop(0)
        if kind == "halve":
            self.value = add(self.net.half(self.value, step, True, self.dim), self.flight)
        elif kind == "full":
            total = self.value.astype(F32) + self.flight.astype(F32)
            self.value = total.astype(self.value.dtype)
        else:
            self.value = self.net.join(self.value, self.flight, step, self.dim)
        self.flight = self.sent = None


def drain(*chains, keep=0):
    for chain in chains:
        while len(chain.todo) > keep:
            chain.start()
            chain.end()


def meet(chains, *outputs, hold=()):
    flights = [c.flight for c in chains if c.flight is not None]
    for chain in hold:
        chain.prepare()
    landed, outputs, sents = tie(flights, outputs, [h.sent for h in hold])
    landed = list(landed)
    for chain, sent in zip(hold, sents):
        chain.sent = sent
    for chain in chains:
        if chain.flight is not None:
            chain.flight = landed.pop(0)
            chain.end()
    return outputs


def body(
    net,
    images,
    keep_mask,
    ln1_gain,
    ln1_bias,
    qkv_weight,
    qkv_bias,
    frequencies,
    proj_weight,
    proj_bias,
    ln2_gain,
    ln2_bias,
    fc1_weight,
    fc1_bias,
    fc2_weight,
    fc2_bias,
    out_grad,
):
    image_count, slots, width = images.shape
    row_count = image_count * slots
    inner, outer = net.bits("tensor")
    dp_steps = net.bits("dp")
    near_dp, far_dp = dp_steps[:1], dp_steps[1:]

    ins, outs = {0: fc1_weight}, {0: fc2_weight}
    ins[2], outs[2] = net.swap(fc1_weight, outer), net.swap(fc2_weight, outer)
    ins[1], outs[1] = net.swap(fc1_weight, inner), net.swap(fc2_weight, inner)
    biases = {0: fc1_bias}
    biases[1], biases[2] = net.swap(biases[0], inner), net.swap(biases[0], outer)

    rows = images.reshape(row_count, width)
    by_head = jnp.transpose(frequencies, (1, 0, 2))
    normed_one, qkv, cosine, sine = project_qkv(
        rows, ln1_gain, ln1_bias, qkv_bias, by_head, qkv_weight, slots
    )
    mixed, totals = attend(qkv, keep_mask, slots)
    resid, normed_two, grad_low, kept_col = project_out(
        mixed, rows, out_grad.reshape(row_count, width), keep_mask,
        proj_bias, ln2_gain, ln2_bias, proj_weight,
    )

    actives, hiddens, grads, bias_grads = {}, {}, {}, {}

    def chunk(r, normed, grad):
        actives[r], hiddens[r], grads[r], bias_grads[r] = hidden_units(
            normed, grad, ins[r], biases[r], outs[r]
        )

    normed_two, grad_low, ins[1], outs[1], biases[1] = tie(
        normed_two, grad_low, ins[1], outs[1], biases[1]
    )
    chunk(1, normed_two, grad_low)
    normed_two, grads[1], ins[2], outs[2], biases[2] = tie(
        normed_two, grads[1], ins[2], outs[2], biases[2]
    )
    biases[3] = net.swap(biases[2], inner)
    near = net.swap(grads[1], inner)
    ins[3], outs[3] = net.swap(ins[2], inner), net.swap(outs[2], inner)
    chunk(0, normed_two, grad_low)
    normed_two, grads[0], near, ins[3], outs[3], biases[3] = tie(
        normed_two, grads[0], near, ins[3], outs[3], biases[3]
    )
    near = add(grads[0], near)
    near_in = Chain(net, near[0], far_dp[:1], joins=[])
    near_out = Chain(net, near[1], near_dp, joins=[])
    near_in.start()
    near_out.start()
    chunk(3, normed_two, grad_low)
    normed_two, grads[3] = tie(normed_two, grads[3])
    far = net.swap(grads[3], inner)
    chunk(2, normed_two, grad_low)
    far, grads[2], hiddens[2] = tie(far, grads[2], hiddens[2])
    far = add(grads[2], far)
    far_in = Chain(net, far[0], far_dp[:1], joins=[])
    far_out = Chain(net, far[1], near_dp, joins=[])
    far_in.start()
    far_out.start()
    ranks = range(4)
    grad_resid, grad_branch, grad_mixed, joined = mlp_back(
        [hiddens[r] for r in ranks], [ins[r] for r in ranks],
        proj_weight, resid, grad_low, ln2_gain,
    )
    halves = [near_in, near_out, far_in, far_out]
    grad_branch, grad_mixed = meet(halves, grad_branch, grad_mixed)
    pair_in = Chain(net, jnp.stack([near_in.value, far_in.value]), near_dp, joins=[], dim=1)
    pair_out = Chain(net, jnp.stack([near_out.value, far_out.value]), far_dp[:1], joins=[], dim=1)
    pair_in.start()
    pair_out.start()
    proj_grad = dot(mixed, grad_branch, 0, 0).astype(BF16)

    pair_sums = {}

    def back(pair, grad, count=1, at=0, earlier=()):
        packed, pair_sums[pair] = attend_back(
            qkv, mixed, grad, totals, kept_col, cosine, sine, slots, pair, count, at, earlier
        )
        return packed

    def weight_grad(packed):
        return dot(normed_one, packed, 0, 0).astype(BF16)

    def group(value):
        return Chain(net, value, [inner, outer] + near_dp, far_dp)

    def begin(*chains):
        for chain in chains:
            chain.start()

    def gather(pair, cross):
        return Chain(net, add(pair.value[0], cross), [], far_dp[1:], far_dp[:1] + near_dp)

    packed_a = back(0, grad_mixed, 2, 0)
    grad_mixed, packed_a, proj_grad = meet(
        [pair_in, pair_out], grad_mixed, packed_a, proj_grad
    )
    cross_in, cross_out = net.swap(pair_in.value[1], outer), net.swap(pair_out.value[1], outer)
    packed_a = back(1, grad_mixed, 2, 1, [packed_a])
    grad_mixed, cross_in, cross_out, *first = tie(
        grad_mixed, cross_in, cross_out, proj_grad, weight_grad(packed_a)
    )
    mlp_in, mlp_out = gather(pair_in, cross_in), gather(pair_out, cross_out)
    group_a = group(jnp.concatenate(first, axis=1))
    begin(mlp_out, group_a)
    packed_b = back(2, grad_mixed, 2, 0)
    grad_mixed, packed_b = meet([mlp_out, group_a], grad_mixed, packed_b, hold=[mlp_in])
    begin(mlp_in, group_a)
    packed_b = back(3, grad_mixed, 2, 1, [packed_b])
    grad_mixed, grad_b = meet(
        [mlp_in, group_a], grad_mixed, weight_grad(packed_b), hold=[mlp_out]
    )
    group_b = group(grad_b)
    begin(mlp_in, mlp_out, group_a, group_b)
    packed_c = back(4, grad_mixed, 2, 0)
    grad_mixed, packed_c = meet(
        [mlp_in, mlp_out, group_a, group_b], grad_mixed, packed_c
    )
    begin(mlp_out, group_a, group_b)
    packed_c = back(5, grad_mixed, 2, 1, [packed_c])
    packed_c, grad_c = meet([group_a, group_b], packed_c, weight_grad(packed_c))
    group_c = group(grad_c)
    begin(group_a, group_b, group_c)

    packed = [packed_a, packed_b, packed_c]
    own_list = lax.axis_index("tensor").astype(jnp.int32).reshape(1)
    groups = [group_a, group_b, group_c]
    input_grad, half_sums = finish(
        packed, qkv_weight, rows, grad_resid, ln1_gain, 0, slots, ()
    )
    input_grad, half_sums = meet(
        [mlp_out, group_b, group_c], input_grad, half_sums, hold=[mlp_in]
    )
    begin(mlp_in, group_b, group_c)
    input_grad, small = finish(
        packed, qkv_weight, rows, grad_resid, ln1_gain, 1, slots,
        [own_list, joined, *[bias_grads[r] for r in ranks], *[pair_sums[p] for p in range(6)],
         half_sums, input_grad],
    )
    small, actives[0] = meet(groups, small, actives[0])
    small = Chain(net, small, [], near_dp + [inner, outer] + far_dp)
    groups.append(small)
    begin(*groups)
    result = lambda image, earlier: mlp_result(
        [actives[r] for r in ranks], [outs[r] for r in ranks],
        resid, kept_col, fc2_bias, image, slots, earlier,
    )
    block_out = result(0, ())
    (block_out,) = meet(groups, block_out)
    begin(*groups)
    block_out = result(1, (block_out,))
    (block_out,) = meet([mlp_in, *groups], block_out)
    begin(*groups)
    meet(groups)
    begin(*groups)
    meet(groups)
    begin(*groups)
    drain(group_a, group_b, mlp_in, mlp_out)
    early = final_early(group_a.value, group_b.value, mlp_in.value, mlp_out.value, width)
    qkv_begun, proj_weight_grad, fc1_weight_grad, fc2_weight_grad, square = meet(groups, *early)
    drain(group_c, keep=1)
    drain(small)
    begin(group_c)
    side = net.side(inner).astype(jnp.int32).reshape(1)
    (
        qkv_weight_grad, ln1_gain_grad, ln1_bias_grad, qkv_bias_grad,
        freq_grad, proj_bias_grad, ln2_gain_grad, ln2_bias_grad, fc1_bias_grad, fc2_bias_grad,
        freq_norm, rest_norm,
    ) = final(
        own_list, side, small.value, square, group_c.value, group_c.flight,
        by_head.shape, qkv_begun,
    )
    return (
        block_out.reshape(images.shape),
        input_grad.reshape(images.shape),
        ln1_gain_grad,
        ln1_bias_grad,
        qkv_weight_grad,
        qkv_bias_grad,
        jnp.transpose(freq_grad, (1, 0, 2)),
        proj_weight_grad,
        proj_bias_grad,
        ln2_gain_grad,
        ln2_bias_grad,
        fc1_weight_grad,
        fc1_bias_grad,
        fc2_weight_grad,
        fc2_bias_grad,
        freq_norm.reshape(()),
        rest_norm.reshape(()),
    )


def solution(mesh):
    rows = P(("dp", "tensor"), None, None)
    whole = P()
    hidden_in, hidden_out = P(None, "tensor"), P("tensor", None)
    return jax.shard_map(
        functools.partial(body, Exchange(mesh)),
        mesh=mesh,
        in_specs=(
            (rows, P(("dp", "tensor"), None))
            + (whole,) * 9
            + (hidden_in, P("tensor"), hidden_out, whole, rows)
        ),
        out_specs=(
            (rows, rows) + (whole,) * 9 + (hidden_in, P("tensor"), hidden_out) + (whole,) * 3
        ),
        check_vma=False,
    )
```

```python
import functools

import jax
import jax.numpy as jnp
from jax import lax
from jax.experimental import pallas as pl
from jax.experimental.pallas import tpu as pltpu
from jax.sharding import PartitionSpec as P

GRID = 24
EPSILON = 1e-06
MASKED_SCORE = 1e30
ROOT_HALF = 0.7071067811865476
DENSITY_SCALE = 0.3989422804014327
F32 = jnp.float32
BF16 = jnp.bfloat16
LANES = 128
HEAD = 64
HIDDEN_TILE = 256
EMPHASIS = 20
EARLY = pltpu.CompilerParams(vmem_limit_bytes=56 << 20)
CHUNK = pltpu.CompilerParams(vmem_limit_bytes=24 << 20)
PARAMS = pltpu.CompilerParams(vmem_limit_bytes=32 << 20)


def dot(left, right, left_dim=1, right_dim=0):
    return lax.dot_general(
        left, right, (((left_dim,), (right_dim,)), ((), ())), preferred_element_type=F32
    )


def normalize(row_data):
    row_mean = jnp.mean(row_data, axis=-1, keepdims=True)
    centred = row_data - row_mean
    inverse = lax.rsqrt(jnp.mean(centred * centred, axis=-1, keepdims=True) + EPSILON)
    return (centred * inverse, inverse)


def norm_back(grad_unit, unit_rows, inverse):
    return inverse * (
        grad_unit
        - jnp.mean(grad_unit, axis=-1, keepdims=True)
        - unit_rows * jnp.mean(grad_unit * unit_rows, axis=-1, keepdims=True)
    )


def swap_halves(tile):
    lane = lax.broadcasted_iota(jnp.int32, (1, LANES), 1)
    first = (lane % HEAD) < HEAD // 2
    return jnp.where(
        first, pltpu.roll(tile, LANES - HEAD // 2, 1), pltpu.roll(tile, HEAD // 2, 1)
    )


def as_row(ref):
    return ref[...].astype(F32).reshape(1, -1)


def column_sum(values):
    return jnp.sum(values, axis=0, keepdims=True)


def stack_rows(members):
    width = members[0].shape[1]
    row = lax.broadcasted_iota(jnp.int32, (8, width), 0)
    total = jnp.zeros((8, width), F32)
    for at, member in enumerate(members):
        total = jnp.where(row == at, member, total)
    return total


def shape(dims, dtype=BF16):
    return jax.ShapeDtypeStruct(dims, dtype)


def fixed(*dims):
    return pl.BlockSpec(dims, lambda *_: (0,) * len(dims))


def cost(flops, moved, steep=0):
    return pl.CostEstimate(flops=EMPHASIS * flops, bytes_accessed=moved, transcendentals=steep)


def qkv_kernel(
    x_ref, gain_ref, shift_ref, bias_ref, freq_ref, weight_ref,
    normed_ref, qkv_ref, cos_ref, sin_ref, lanes_ref,
):
    tile, width = x_ref.shape
    across_count = tile // GRID

    @pl.when(pl.program_id(1) == 0)
    def _():
        half = HEAD // 2
        for head in range(width // HEAD):
            for at in (head * HEAD, head * HEAD + half):
                lanes_ref[0:2, at : at + half] = freq_ref[head, :, :]
        first = (pl.program_id(0) * across_count).astype(F32)
        padded = -(-across_count // 8) * 8
        across = first + lax.broadcasted_iota(jnp.int32, (padded, width), 0).astype(F32)
        down = lax.broadcasted_iota(jnp.int32, (GRID, width), 0).astype(F32)
        across = across * lanes_ref[0:1, :]
        down = down * lanes_ref[1:2, :]
        cos_a, sin_a, cos_d, sin_d = jnp.cos(across), jnp.sin(across), jnp.cos(down), jnp.sin(down)
        lane = lax.broadcasted_iota(jnp.int32, (1, width), 1)
        sign = jnp.where((lane % HEAD) < HEAD // 2, -1.0, 1.0)
        for at in range(across_count):
            rows = slice(at * GRID, (at + 1) * GRID)
            one_cos, one_sin = cos_a[at : at + 1], sin_a[at : at + 1]
            cos_ref[rows, :] = one_cos * cos_d - one_sin * sin_d
            sin_ref[rows, :] = (one_sin * cos_d + one_cos * sin_d) * sign

    unit, _ = normalize(x_ref[...].astype(F32))
    normed = (unit * as_row(gain_ref) + as_row(shift_ref)).astype(BF16)
    normed_ref[...] = normed
    bias = as_row(bias_ref)
    for part in range(3):
        cols = slice(part * width, (part + 1) * width)
        packed = dot(normed, weight_ref[:, cols]) + bias[:, cols]
        for at in range(0, width, LANES):
            piece = packed[:, at : at + LANES]
            if part < 2:
                cosine, sine = cos_ref[:, at : at + LANES], sin_ref[:, at : at + LANES]
                piece = piece * cosine + swap_halves(piece) * sine
            if part == 0:
                piece = piece * (HEAD**-0.5)
            qkv_ref[:, part * width + at : part * width + at + LANES] = piece.astype(BF16)


def project_qkv(rows, gain, shift, bias, frequencies, weight, slots):
    row_count, width = rows.shape
    halves = 1
    tile = slots // halves
    row_block = lambda cols: pl.BlockSpec((tile, cols), lambda h, n: (n * halves + h, 0))
    table = pl.BlockSpec((tile, width), lambda h, n: (h, 0))
    return pl.pallas_call(
        qkv_kernel,
        grid=(halves, row_count // slots),
        in_specs=[
            row_block(width),
            fixed(width),
            fixed(width),
            fixed(3 * width),
            fixed(*frequencies.shape),
            fixed(*weight.shape),
        ],
        out_specs=[row_block(width), row_block(3 * width), table, table],
        out_shape=[
            shape((row_count, width)),
            shape((row_count, 3 * width)),
            shape((slots, width), F32),
            shape((slots, width), F32),
        ],
        scratch_shapes=[pltpu.VMEM((8, width), F32)],
        cost_estimate=cost(6 * row_count * width * width, row_count * width * 14),
        compiler_params=EARLY,
    )(rows, gain, shift, bias, frequencies, weight)


def attend_kernel(q_ref, k_ref, v_ref, mask_ref, mixed_ref, total_ref):
    low = lax.broadcasted_iota(jnp.int32, (1, LANES), 1) < HEAD
    queries, keys, values = q_ref[...], k_ref[...], v_ref[...]
    zero = jnp.zeros_like(queries)
    mask = (mask_ref[pl.ds(pl.program_id(0), 1), :].astype(F32) - 1.0) * MASKED_SCORE
    mask = jnp.transpose(jnp.broadcast_to(mask, (8, mask.shape[1])))[:, 0:1]
    mixed, totals = None, []
    for head in range(2):
        keep = low if head == 0 else ~low
        scores = dot(keys, jnp.where(keep, queries, zero), 1, 1) + mask
        top = jnp.max(scores, axis=0, keepdims=True)
        weights = jnp.exp(scores - top)
        total = column_sum(weights)
        low_weights = (weights * (1.0 / total)).astype(BF16)
        part = dot(jnp.where(keep, values, zero), low_weights, 0, 0)
        mixed = part if mixed is None else mixed + part
        totals.append(top + jnp.log(total))
    mixed_ref[...] = jnp.transpose(mixed).astype(BF16)
    row = lax.broadcasted_iota(jnp.int32, (8, 1), 0)
    total_ref[0] = jnp.where(row == 0, totals[0], totals[1])


def attend(qkv, keep_mask, slots):
    row_count, width = qkv.shape[0], qkv.shape[1] // 3
    images, pairs = row_count // slots, width // LANES
    block = lambda part: pl.BlockSpec((slots, LANES), lambda i, p: (i, p + part * pairs))
    return pl.pallas_call(
        attend_kernel,
        grid=(images, pairs),
        in_specs=[
            block(0),
            block(1),
            block(2),
            fixed(*keep_mask.shape),
        ],
        out_specs=[block(0), pl.BlockSpec((1, 8, slots), lambda i, p: (i, p, 0))],
        out_shape=[shape((row_count, width)), shape((images, 8 * pairs, slots), F32)],
        cost_estimate=cost(
            16 * row_count * slots * width, row_count * width * 12, row_count * slots * 2 * pairs
        ),
        compiler_params=EARLY,
    )(qkv, qkv, qkv, keep_mask)


def project_kernel(
    mixed_ref, x_ref, grad_ref, mask_ref, bias_ref, gain_ref, shift_ref, weight_ref,
    resid_ref, normed_ref, low_ref, kept_ref,
):
    row = mask_ref[pl.ds(pl.program_id(0), 1), :].astype(F32)
    kept = jnp.transpose(jnp.broadcast_to(row, (8, row.shape[1])))[:, 0:1]
    resid = x_ref[...].astype(F32) + dot(mixed_ref[...], weight_ref[...]) + as_row(bias_ref)
    unit, _ = normalize(resid)
    resid_ref[...] = resid
    normed_ref[...] = (unit * as_row(gain_ref) + as_row(shift_ref)).astype(BF16)
    low_ref[...] = (kept * grad_ref[...].astype(F32)).astype(BF16)
    kept_ref[...] = kept


def project_out(mixed, rows, out_grad, keep_mask, bias, gain, shift, weight):
    row_count, width = rows.shape
    images, slots = keep_mask.shape
    block = pl.BlockSpec((slots, width), lambda i: (i, 0))
    return pl.pallas_call(
        project_kernel,
        grid=(images,),
        in_specs=[block, block, block, fixed(images, slots)]
        + [fixed(width)] * 3
        + [fixed(*weight.shape)],
        out_specs=[block, block, block, pl.BlockSpec((slots, 1), lambda i: (i, 0))],
        out_shape=[
            shape((row_count, width), F32),
            shape((row_count, width)),
            shape((row_count, width)),
            shape((row_count, 1), F32),
        ],
        cost_estimate=cost(2 * row_count * width * width, row_count * width * 14),
        compiler_params=EARLY,
    )(mixed, rows, out_grad, keep_mask, bias, gain, shift, weight)


def hidden_kernel(
    normed_ref, grad_ref, in_ref, bias_ref, out_ref,
    active_ref, hidden_ref, weights_ref, bias_grad_ref,
):
    normed, grad = normed_ref[...], grad_ref[...]
    hidden = dot(normed, in_ref[...]) + as_row(bias_ref)
    grad_active = dot(grad, out_ref[...], 1, 1)
    half = 0.5 * (1.0 + lax.erf(hidden * ROOT_HALF))
    active = (hidden * half).astype(BF16)
    slope = half + hidden * jnp.exp(-0.5 * hidden * hidden) * DENSITY_SCALE
    grad_hidden = (grad_active * slope).astype(BF16)
    active_ref[...] = active
    hidden_ref[...] = grad_hidden
    weights_ref[0] = dot(normed, grad_hidden, 0, 0).astype(BF16)
    weights_ref[1] = dot(grad, active, 0, 0).astype(BF16)
    bias_grad_ref[...] = column_sum(grad_hidden.astype(F32))


def hidden_units(normed, grad, weight_in, bias_in, weight_out):
    row_count, width = normed.shape
    units = weight_in.shape[1]
    tile = HIDDEN_TILE
    cols = lambda rows: pl.BlockSpec((rows, tile), lambda i: (0, i))
    rows = pl.BlockSpec((tile, width), lambda i: (i, 0))
    return pl.pallas_call(
        hidden_kernel,
        grid=(units // tile,),
        in_specs=[
            fixed(row_count, width), fixed(row_count, width), cols(width),
            pl.BlockSpec((tile,), lambda i: (i,)), rows
        ],
        out_specs=[
            cols(row_count),
            cols(row_count),
            pl.BlockSpec((2, width, tile), lambda i: (0, 0, i)),
            cols(1),
        ],
        out_shape=[
            shape((row_count, units)),
            shape((row_count, units)),
            shape((2, width, units)),
            shape((1, units), F32),
        ],
        cost_estimate=cost(
            8 * row_count * width * units, row_count * width * 8 + width * units * 8,
            2 * row_count * units,
        ),
        compiler_params=CHUNK,
    )(normed, grad, weight_in, bias_in, weight_out)


def mlp_out_kernel(*refs):
    actives, outs = refs[0:4], refs[4:8]
    resid_ref, kept_ref, bias_ref = refs[8:11]
    block_ref = refs[-1]
    mlp_out = sum(dot(a[...], w[...]) for a, w in zip(actives, outs))
    block_ref[...] = (kept_ref[...] * (resid_ref[...] + mlp_out + as_row(bias_ref))).astype(BF16)


def mlp_back_kernel(*refs):
    hiddens, ins = refs[0:4], refs[4:8]
    proj_ref, resid_ref, low_ref, gain_ref = refs[8:12]
    grad_ref, branch_ref, mixed_ref, sums_ref = refs[12:]
    grad_normed = sum(dot(h[...], w[...], 1, 1) for h, w in zip(hiddens, ins))
    unit, inverse = normalize(resid_ref[...])
    grad_rows = low_ref[...].astype(F32)
    grad = grad_rows + norm_back(grad_normed * as_row(gain_ref), unit, inverse)
    branch = grad.astype(BF16)
    grad_ref[...] = grad
    branch_ref[...] = branch
    mixed_ref[...] = dot(branch, proj_ref[...], 1, 1).astype(BF16)
    sums = stack_rows(
        [
            column_sum(branch.astype(F32)),
            column_sum(grad_normed * unit),
            column_sum(grad_normed),
            column_sum(grad_rows),
        ]
    )

    @pl.when(pl.program_id(0) == 0)
    def _():
        sums_ref[...] = sums

    @pl.when(pl.program_id(0) > 0)
    def _():
        sums_ref[...] += sums


def mlp_result(actives, outs, resid, kept_col, bias, image, slots, earlier):
    row_count, width = resid.shape
    tile = slots // 2
    block = pl.BlockSpec((tile, width), lambda i: (2 * image + i, 0))
    return pl.pallas_call(
        mlp_out_kernel,
        grid=(2,),
        in_specs=[block] * 4
        + [fixed(width, width)] * 4
        + [block, pl.BlockSpec((tile, 1), lambda i: (2 * image + i, 0)), fixed(width)]
        + [pl.BlockSpec(memory_space=pl.ANY)] * len(earlier),
        out_specs=block,
        out_shape=shape((row_count, width)),
        input_output_aliases={11: 0} if earlier else {},
        cost_estimate=cost(8 * slots * width * width, slots * width * 14),
        compiler_params=PARAMS,
    )(*actives, *outs, resid, kept_col, bias, *earlier)


def mlp_back(hiddens, ins, proj_weight, resid, grad_low, gain):
    row_count, width = resid.shape
    tile = row_count // 2
    block = pl.BlockSpec((tile, width), lambda i: (i, 0))
    return pl.pallas_call(
        mlp_back_kernel,
        grid=(2,),
        in_specs=[block] * 4
        + [fixed(width, width)] * 5
        + [block, block, fixed(width)],
        out_specs=[block, block, block, fixed(8, width)],
        out_shape=[
            shape((row_count, width), F32),
            shape((row_count, width)),
            shape((row_count, width)),
            shape((8, width), F32),
        ],
        cost_estimate=cost(10 * row_count * width * width, row_count * width * 22),
        compiler_params=PARAMS,
    )(*hiddens, *ins, proj_weight, resid, grad_low, gain)


def attend_back_kernel(
    q_ref, k_ref, v_ref, grad_ref, total_ref, kept_ref, cos_ref, sin_ref, *refs
):
    packed_ref, sums_ref = refs[-2:]
    slots = q_ref.shape[0]
    low = lax.broadcasted_iota(jnp.int32, (1, LANES), 1) < HEAD
    q, k, v, grad_mixed = q_ref[...], k_ref[...], v_ref[...], grad_ref[...]
    zero = jnp.zeros_like(q)
    mask = (kept_ref[...] - 1.0) * MASKED_SCORE
    grad_q = grad_k = grad_v = None
    for head in range(2):
        keep = low if head == 0 else ~low
        q_head = jnp.where(keep, q, zero)
        grad_head = jnp.where(keep, grad_mixed, zero)
        k_head = jnp.where(keep, k, zero)
        total = total_ref[0, head : head + 1, :]
        weights = jnp.exp((dot(k, q_head, 1, 1) + mask) - total)
        grad_weights = dot(v, grad_head, 1, 1)
        inner = column_sum(weights * grad_weights)
        grad_scores = (weights * (grad_weights - inner)).astype(BF16)
        part_v = dot(weights.astype(BF16), grad_head)
        part_k = dot(grad_scores, q_head)
        part_q = dot(grad_scores, k_head, 0, 0)
        grad_v = part_v if grad_v is None else grad_v + part_v
        grad_k = part_k if grad_k is None else grad_k + part_k
        grad_q = part_q if grad_q is None else grad_q + part_q
    turn = grad_q * swap_halves(q.astype(F32)) + grad_k * swap_halves(k.astype(F32))
    slot = lax.broadcasted_iota(jnp.int32, (slots, 1), 0)
    across = slot // GRID
    down = slot - across * GRID
    cosine, sine = cos_ref[...], sin_ref[...]
    grad_q = grad_q * (HEAD**-0.5)
    grad_q = (grad_q * cosine - swap_halves(grad_q) * sine).astype(BF16)
    grad_k = (grad_k * cosine - swap_halves(grad_k) * sine).astype(BF16)
    packed = jnp.concatenate([grad_q, grad_k, grad_v.astype(BF16)], axis=1)
    packed_ref[...] = packed
    parts = column_sum(packed.astype(F32))
    sums = stack_rows(
        [
            column_sum(turn * across.astype(F32)),
            column_sum(turn * down.astype(F32)),
            parts[:, :LANES],
            parts[:, LANES : 2 * LANES],
            parts[:, 2 * LANES :],
        ]
    )

    @pl.when(pl.program_id(0) == 0)
    def _():
        sums_ref[...] = sums

    @pl.when(pl.program_id(0) > 0)
    def _():
        sums_ref[...] += sums


def attend_back(
    qkv, grad_mixed, totals, kept_col, cosine, sine, slots, pair, count, at, earlier
):
    row_count, width = grad_mixed.shape
    images, pairs = row_count // slots, width // LANES
    block = lambda part: pl.BlockSpec((slots, LANES), lambda i: (i, pair + part * pairs))
    table = pl.BlockSpec((slots, LANES), lambda i: (0, pair))
    return pl.pallas_call(
        attend_back_kernel,
        grid=(images,),
        in_specs=[
            block(0), block(1), block(2), block(0),
            pl.BlockSpec((1, 8, slots), lambda i: (i, pair, 0)),
            pl.BlockSpec((slots, 1), lambda i: (i, 0)),
            table,
            table,
        ] + [pl.BlockSpec(memory_space=pl.ANY)] * len(earlier),
        out_specs=[pl.BlockSpec((slots, 3 * LANES), lambda i: (i, at)), fixed(8, LANES)],
        out_shape=[shape((row_count, count * 3 * LANES)), shape((8, LANES), F32)],
        input_output_aliases={8: 0} if earlier else {},
        cost_estimate=cost(
            40 * row_count * slots * LANES, row_count * LANES * 30, row_count * slots * 2
        ),
        compiler_params=PARAMS,
    )(qkv, qkv, qkv, grad_mixed, totals, kept_col, cosine, sine, *earlier)


def finish_kernel(count, *refs):
    packed, (weight_ref, x_ref, grad_ref, gain_ref) = refs[:count], refs[count : count + 4]
    more, (input_ref, sums_ref) = refs[count + 4 : -2], refs[-2:]
    pieces = [p[:, at : at + 3 * LANES] for p in packed for at in range(0, p.shape[1], 3 * LANES)]
    full = jnp.concatenate(
        [p[:, part * LANES : (part + 1) * LANES] for part in range(3) for p in pieces], axis=1
    )
    grad_normed = dot(full, weight_ref[...], 1, 1)
    unit, inverse = normalize(x_ref[...].astype(F32))
    input_ref[...] = (
        grad_ref[...] + norm_back(grad_normed * as_row(gain_ref), unit, inverse)
    ).astype(BF16)
    members = [column_sum(grad_normed * unit), column_sum(grad_normed)]
    step = pl.program_id(0)
    if not more:

        @pl.when(step == 0)
        def _():
            sums_ref[...] = stack_rows(members)

        @pl.when(step > 0)
        def _():
            sums_ref[...] += stack_rows(members)

    else:
        own_ref, joined_ref, hidden_refs, pair_refs, before_ref = (
            more[0], more[1], more[2:6], more[6:-2], more[-2],
        )

        @pl.when(step == 0)
        def _():
            row = lax.broadcasted_iota(jnp.int32, (8, 1), 0)
            top = jnp.zeros((8, input_ref.shape[1]), F32)
            for r, hidden in enumerate(hidden_refs):
                top = jnp.where(row == (own_ref[0] ^ r), hidden[...], top)
            low = jnp.where(row < 4, 0.0, pltpu.roll(joined_ref[...], 4, 0))
            sums_ref[0:8, :] = top + low
            pairs = jnp.concatenate([p[...] for p in pair_refs], axis=1)
            ends = pltpu.roll(before_ref[...] + stack_rows(members), 5, 0)
            sums_ref[8:16, :] = jnp.where(row < 5, pairs, ends)

        @pl.when(step > 0)
        def _():
            sums_ref[8:16, :] += pltpu.roll(stack_rows(members), 5, 0)


def finish(packed, weight, rows, grad_resid, gain, image, slots, more):
    row_count, width = rows.shape
    tile = slots // 2
    block = lambda cols: pl.BlockSpec((tile, cols), lambda i: (2 * image + i, 0))
    more_specs = [fixed(*m.shape) for m in more]
    if more:
        more_specs[0] = pl.BlockSpec(memory_space=pltpu.SMEM)
        more_specs[-1] = pl.BlockSpec(memory_space=pl.ANY)
    count = len(packed)
    sums = 16 if more else 8
    return pl.pallas_call(
        functools.partial(finish_kernel, count),
        grid=(2,),
        in_specs=[block(p.shape[1]) for p in packed]
        + [fixed(*weight.shape), block(width), block(width), fixed(width)]
        + more_specs,
        out_specs=[block(width), fixed(sums, width)],
        out_shape=[shape((row_count, width)), shape((sums, width), F32)],
        input_output_aliases={count + 3 + len(more): 0} if more else {},
        cost_estimate=cost(6 * slots * width * width, slots * width * 14),
        compiler_params=PARAMS,
    )(*packed, weight, rows, grad_resid, gain, *more)


def total(values):
    return jnp.sum(jnp.sum(values * values, axis=0, keepdims=True), axis=1, keepdims=True)


def place(blocks, pair, weight_ref, width):
    square = jnp.zeros((1, 1), F32)
    for block, start in blocks:
        for at in range(start, block.shape[1], 3 * LANES):
            for part in range(3):
                piece = block[:, at + part * LANES : at + (part + 1) * LANES].astype(F32)
                first = part * width + pair * LANES
                weight_ref[:, first : first + LANES] = piece
                square = square + total(piece)
            pair += 1
    return square


def final_early_kernel(
    first_ref, second_ref, in_ref, out_ref, weight_ref, proj_ref, fc1_ref, fc2_ref, square_ref
):
    width = proj_ref.shape[1]
    proj = first_ref[:, :width].astype(F32)
    proj_ref[...] = proj
    fc2_ref[...] = jnp.transpose(out_ref[...].astype(F32))
    square = total(proj) + place([(first_ref, width), (second_ref, 0)], 0, weight_ref, width)

    @pl.when(pl.program_id(0) == 0)
    def _():
        square_ref[...] = square
        quarter = in_ref.shape[0] // 4
        for at, source in enumerate((0, 2, 1, 3)):
            rows = slice(source * quarter, (source + 1) * quarter)
            fc1_ref[at * quarter : (at + 1) * quarter, :] = in_ref[rows, :].astype(F32)

    @pl.when(pl.program_id(0) > 0)
    def _():
        square_ref[...] += square


def final_early(first, second, mlp_in, mlp_out, width):
    depth, units = mlp_in.shape
    tile = depth // 3
    row_block = lambda cols: pl.BlockSpec((tile, cols), lambda i: (i, 0))
    return pl.pallas_call(
        final_early_kernel,
        grid=(3,),
        in_specs=[
            row_block(first.shape[1]),
            row_block(second.shape[1]),
            fixed(depth, units),
            row_block(depth),
        ],
        out_specs=[
            row_block(3 * width),
            row_block(width),
            fixed(depth, units),
            pl.BlockSpec((units, tile), lambda i: (0, i)),
            fixed(1, 1),
        ],
        out_shape=[
            shape((depth, 3 * width), F32),
            shape((depth, width), F32),
            shape((depth, units), F32),
            shape((units, depth), F32),
            shape((1, 1), F32),
        ],
        cost_estimate=cost(depth * width * 8, depth * width * 30),
        compiler_params=PARAMS,
    )(first, second, mlp_in, mlp_out)


def final_kernel(
    own_ref, side_ref, small_ref, square_ref, mine_ref, other_ref, before_ref, *outputs
):
    (
        weight_out, gain1_ref, shift1_ref, bias_ref, freq_ref, proj_bias_ref,
        gain2_ref, shift2_ref, hidden_ref, out_bias_ref, freq_norm_ref, rest_norm_ref,
        staged, sems,
    ) = outputs
    rows, width = mine_ref.shape[0], small_ref.shape[1]
    pairs = width // LANES
    late = mine_ref.shape[1] // (3 * LANES)
    first, span = (pairs - late) * LANES, late * LANES
    square = square_ref[...]
    mine, other = mine_ref[...].astype(F32), other_ref[...].astype(F32)
    square = square + total(mine) + total(other)
    lower = side_ref[0] == 0
    for top, block in ((0, jnp.where(lower, mine, other)), (rows, jnp.where(lower, other, mine))):
        for pair in range(late):
            at = pair * LANES
            for part in range(3):
                start = (3 * pair + part) * LANES
                staged[part, top : top + rows, at : at + LANES] = block[:, start : start + LANES]
    copies = [
        pltpu.make_async_copy(
            staged.at[part],
            weight_out.at[:, part * width + first : part * width + first + span],
            sems.at[part],
        )
        for part in range(3)
    ]
    for copy in copies:
        copy.start()
    small = small_ref[...]
    hidden_ref[...] = small_ref[pl.ds(own_ref[0], 1), :].reshape(width)
    for at, ref in enumerate((proj_bias_ref, gain2_ref, shift2_ref, out_bias_ref)):
        ref[...] = small[4 + at]
    bias_ref[...] = jnp.concatenate([small[10], small[11], small[12]], axis=0)
    gain1_ref[...] = small[13]
    shift1_ref[...] = small[14]
    freq_square = jnp.zeros((1, 1), F32)
    half = HEAD // 2
    for head in range(width // HEAD):
        at = head * HEAD
        turned = small_ref[8:10, at + half : at + HEAD] - small_ref[8:10, at : at + half]
        freq_ref[head, :, :] = turned
        freq_square = freq_square + total(turned)
    freq_norm_ref[...] = jnp.sqrt(freq_square)
    rest_norm_ref[...] = jnp.sqrt(square + total(small[4:8]) + total(small[10:15]))
    for copy in copies:
        copy.wait()


def final(own, side, small, square, mine, other, freq_shape, weight):
    depth, width = weight.shape[0], small.shape[1]
    late = mine.shape[1] // 3
    vector = (shape((width,), F32), fixed(width))
    outputs = [
        (shape(weight.shape, F32), pl.BlockSpec(memory_space=pl.ANY)),
        vector,
        vector,
        (shape((3 * width,), F32), fixed(3 * width)),
        (shape(freq_shape, F32), fixed(*freq_shape)),
        vector,
        vector,
        vector,
        vector,
        vector,
        (shape((1, 1), F32), fixed(1, 1)),
        (shape((1, 1), F32), fixed(1, 1)),
    ]
    return pl.pallas_call(
        final_kernel,
        grid=(1,),
        in_specs=[
            pl.BlockSpec(memory_space=pltpu.SMEM),
            pl.BlockSpec(memory_space=pltpu.SMEM),
            fixed(*small.shape),
            fixed(1, 1),
            fixed(*mine.shape),
            fixed(*other.shape),
            pl.BlockSpec(memory_space=pl.ANY),
        ],
        out_specs=[spec for _, spec in outputs],
        out_shape=[dims for dims, _ in outputs],
        scratch_shapes=[pltpu.VMEM((3, depth, late), F32), pltpu.SemaphoreType.DMA((3,))],
        input_output_aliases={6: 0},
        cost_estimate=cost(depth * width * 8, depth * width * 8),
        compiler_params=PARAMS,
    )(own, side, small, square, mine, other, weight)


class Exchange:
    def __init__(self, mesh):
        self.sizes = dict(mesh.shape)

    def bits(self, axis):
        return [(axis, 1 << b) for b in range(self.sizes[axis].bit_length() - 1)]

    def swap(self, value, step):
        axis, bit = step
        pairs = [(i, i ^ bit) for i in range(self.sizes[axis])]
        return lax.ppermute(value, axis, pairs)

    def side(self, step):
        axis, bit = step
        return (lax.axis_index(axis) // bit) % 2

    def half(self, value, step, mine, dim):
        size = value.shape[dim] // 2
        side = self.side(step)
        return lax.dynamic_slice_in_dim(value, (side if mine else 1 - side) * size, size, dim)

    def join(self, mine, other, step, dim):
        first = self.side(step) == 0
        return jnp.concatenate(
            [jnp.where(first, mine, other), jnp.where(first, other, mine)], axis=dim
        )


def add(*members):
    return sum(member.astype(F32) for member in members).astype(BF16)


def tie(*members):
    return lax.optimization_barrier(members)


class Chain:
    def __init__(self, net, value, halving, full=(), joins=None, dim=0):
        joins = list(reversed(halving)) if joins is None else joins
        self.net, self.value, self.dim = net, value, dim
        self.todo = [("halve", s) for s in halving] + [("full", s) for s in full]
        self.todo += [("join", s) for s in joins]
        self.flight = self.sent = None

    def start(self):
        if not self.todo or self.flight is not None:
            return
        self.prepare()
        self.flight = self.net.swap(self.sent, self.todo[0][1])

    def prepare(self):
        if self.sent is None:
            kind, step = self.todo[0]
            self.sent = self.value
            if kind == "halve":
                self.sent = self.net.half(self.value, step, False, self.dim)

    def end(self):
        if self.flight is None:
            return
        kind, step = self.todo.pop(0)
        if kind == "halve":
            self.value = add(self.net.half(self.value, step, True, self.dim), self.flight)
        elif kind == "full":
            total = self.value.astype(F32) + self.flight.astype(F32)
            self.value = total.astype(self.value.dtype)
        else:
            self.value = self.net.join(self.value, self.flight, step, self.dim)
        self.flight = self.sent = None


def drain(*chains, keep=0):
    for chain in chains:
        while len(chain.todo) > keep:
            chain.start()
            chain.end()


def meet(chains, *outputs, hold=()):
    flights = [c.flight for c in chains if c.flight is not None]
    for chain in hold:
        chain.prepare()
    landed, outputs, sents = tie(flights, outputs, [h.sent for h in hold])
    landed = list(landed)
    for chain, sent in zip(hold, sents):
        chain.sent = sent
    for chain in chains:
        if chain.flight is not None:
            chain.flight = landed.pop(0)
            chain.end()
    return outputs


def body(
    net,
    images,
    keep_mask,
    ln1_gain,
    ln1_bias,
    qkv_weight,
    qkv_bias,
    frequencies,
    proj_weight,
    proj_bias,
    ln2_gain,
    ln2_bias,
    fc1_weight,
    fc1_bias,
    fc2_weight,
    fc2_bias,
    out_grad,
):
    image_count, slots, width = images.shape
    row_count = image_count * slots
    inner, outer = net.bits("tensor")
    dp_steps = net.bits("dp")
    near_dp, far_dp = dp_steps[:1], dp_steps[1:]

    ins, outs = {0: fc1_weight}, {0: fc2_weight}
    ins[2], outs[2] = net.swap(fc1_weight, outer), net.swap(fc2_weight, outer)
    ins[1], outs[1] = net.swap(fc1_weight, inner), net.swap(fc2_weight, inner)
    biases = {0: fc1_bias}
    biases[1], biases[2] = net.swap(biases[0], inner), net.swap(biases[0], outer)

    rows = images.reshape(row_count, width)
    by_head = jnp.transpose(frequencies, (1, 0, 2))
    normed_one, qkv, cosine, sine = project_qkv(
        rows, ln1_gain, ln1_bias, qkv_bias, by_head, qkv_weight, slots
    )
    mixed, totals = attend(qkv, keep_mask, slots)
    resid, normed_two, grad_low, kept_col = project_out(
        mixed, rows, out_grad.reshape(row_count, width), keep_mask,
        proj_bias, ln2_gain, ln2_bias, proj_weight,
    )

    actives, hiddens, grads, bias_grads = {}, {}, {}, {}

    def chunk(r, normed, grad):
        actives[r], hiddens[r], grads[r], bias_grads[r] = hidden_units(
            normed, grad, ins[r], biases[r], outs[r]
        )

    normed_two, grad_low, ins[1], outs[1], biases[1] = tie(
        normed_two, grad_low, ins[1], outs[1], biases[1]
    )
    chunk(1, normed_two, grad_low)
    normed_two, grads[1], ins[2], outs[2], biases[2] = tie(
        normed_two, grads[1], ins[2], outs[2], biases[2]
    )
    biases[3] = net.swap(biases[2], inner)
    near = net.swap(grads[1], inner)
    ins[3], outs[3] = net.swap(ins[2], inner), net.swap(outs[2], inner)
    chunk(0, normed_two, grad_low)
    normed_two, grads[0], near, ins[3], outs[3], biases[3] = tie(
        normed_two, grads[0], near, ins[3], outs[3], biases[3]
    )
    near = add(grads[0], near)
    near_in = Chain(net, near[0], far_dp[:1], joins=[])
    near_out = Chain(net, near[1], near_dp, joins=[])
    near_in.start()
    near_out.start()
    chunk(3, normed_two, grad_low)
    normed_two, grads[3] = tie(normed_two, grads[3])
    far = net.swap(grads[3], inner)
    chunk(2, normed_two, grad_low)
    far, grads[2], hiddens[2] = tie(far, grads[2], hiddens[2])
    far = add(grads[2], far)
    far_in = Chain(net, far[0], far_dp[:1], joins=[])
    far_out = Chain(net, far[1], near_dp, joins=[])
    far_in.start()
    far_out.start()
    ranks = range(4)
    grad_resid, grad_branch, grad_mixed, joined = mlp_back(
        [hiddens[r] for r in ranks], [ins[r] for r in ranks],
        proj_weight, resid, grad_low, ln2_gain,
    )
    halves = [near_in, near_out, far_in, far_out]
    grad_branch, grad_mixed = meet(halves, grad_branch, grad_mixed)
    pair_in = Chain(net, jnp.stack([near_in.value, far_in.value]), near_dp, joins=[], dim=1)
    pair_out = Chain(net, jnp.stack([near_out.value, far_out.value]), far_dp[:1], joins=[], dim=1)
    pair_in.start()
    pair_out.start()
    proj_grad = dot(mixed, grad_branch, 0, 0).astype(BF16)

    pair_sums = {}

    def back(pair, grad, count=1, at=0, earlier=()):
        packed, pair_sums[pair] = attend_back(
            qkv, grad, totals, kept_col, cosine, sine, slots, pair, count, at, earlier
        )
        return packed

    def weight_grad(packed):
        return dot(normed_one, packed, 0, 0).astype(BF16)

    def group(value):
        return Chain(net, value, [inner, outer] + near_dp, far_dp)

    def begin(*chains):
        for chain in chains:
            chain.start()

    def gather(pair, cross):
        return Chain(net, add(pair.value[0], cross), [], far_dp[1:], far_dp[:1] + near_dp)

    packed_a = back(0, grad_mixed, 2, 0)
    grad_mixed, packed_a, proj_grad = meet(
        [pair_in, pair_out], grad_mixed, packed_a, proj_grad
    )
    cross_in, cross_out = net.swap(pair_in.value[1], outer), net.swap(pair_out.value[1], outer)
    packed_a = back(1, grad_mixed, 2, 1, [packed_a])
    grad_mixed, cross_in, cross_out, *first = tie(
        grad_mixed, cross_in, cross_out, proj_grad, weight_grad(packed_a)
    )
    mlp_in, mlp_out = gather(pair_in, cross_in), gather(pair_out, cross_out)
    group_a = group(jnp.concatenate(first, axis=1))
    begin(mlp_out, group_a)
    packed_b = back(2, grad_mixed, 2, 0)
    grad_mixed, packed_b = meet([mlp_out, group_a], grad_mixed, packed_b, hold=[mlp_in])
    begin(mlp_in, group_a)
    packed_b = back(3, grad_mixed, 2, 1, [packed_b])
    grad_mixed, grad_b = meet(
        [mlp_in, group_a], grad_mixed, weight_grad(packed_b), hold=[mlp_out]
    )
    group_b = group(grad_b)
    begin(mlp_in, mlp_out, group_a, group_b)
    packed_c = back(4, grad_mixed, 2, 0)
    grad_mixed, packed_c = meet(
        [mlp_in, mlp_out, group_a, group_b], grad_mixed, packed_c
    )
    begin(mlp_out, group_a, group_b)
    packed_c = back(5, grad_mixed, 2, 1, [packed_c])
    packed_c, grad_c = meet([group_a, group_b], packed_c, weight_grad(packed_c))
    group_c = group(grad_c)
    begin(group_a, group_b, group_c)

    packed = [packed_a, packed_b, packed_c]
    own_list = lax.axis_index("tensor").astype(jnp.int32).reshape(1)
    groups = [group_a, group_b, group_c]
    input_grad, half_sums = finish(
        packed, qkv_weight, rows, grad_resid, ln1_gain, 0, slots, ()
    )
    input_grad, half_sums = meet(
        [mlp_out, group_b, group_c], input_grad, half_sums, hold=[mlp_in]
    )
    begin(mlp_in, group_b, group_c)
    input_grad, small = finish(
        packed, qkv_weight, rows, grad_resid, ln1_gain, 1, slots,
        [own_list, joined, *[bias_grads[r] for r in ranks], *[pair_sums[p] for p in range(6)],
         half_sums, input_grad],
    )
    small, actives[0] = meet(groups, small, actives[0])
    small = Chain(net, small, [], near_dp + [inner, outer] + far_dp)
    groups.append(small)
    begin(*groups)
    result = lambda image, earlier: mlp_result(
        [actives[r] for r in ranks], [outs[r] for r in ranks],
        resid, kept_col, fc2_bias, image, slots, earlier,
    )
    block_out = result(0, ())
    (block_out,) = meet(groups, block_out)
    begin(*groups)
    block_out = result(1, (block_out,))
    (block_out,) = meet([mlp_in, *groups], block_out)
    begin(*groups)
    meet(groups)
    begin(*groups)
    meet(groups)
    begin(*groups)
    drain(group_a, group_b, mlp_in, mlp_out)
    early = final_early(group_a.value, group_b.value, mlp_in.value, mlp_out.value, width)
    qkv_begun, proj_weight_grad, fc1_weight_grad, fc2_weight_grad, square = meet(groups, *early)
    drain(group_c, keep=1)
    drain(small)
    begin(group_c)
    side = net.side(inner).astype(jnp.int32).reshape(1)
    (
        qkv_weight_grad, ln1_gain_grad, ln1_bias_grad, qkv_bias_grad,
        freq_grad, proj_bias_grad, ln2_gain_grad, ln2_bias_grad, fc1_bias_grad, fc2_bias_grad,
        freq_norm, rest_norm,
    ) = final(
        own_list, side, small.value, square, group_c.value, group_c.flight,
        by_head.shape, qkv_begun,
    )
    return (
        block_out.reshape(images.shape),
        input_grad.reshape(images.shape),
        ln1_gain_grad,
        ln1_bias_grad,
        qkv_weight_grad,
        qkv_bias_grad,
        jnp.transpose(freq_grad, (1, 0, 2)),
        proj_weight_grad,
        proj_bias_grad,
        ln2_gain_grad,
        ln2_bias_grad,
        fc1_weight_grad,
        fc1_bias_grad,
        fc2_weight_grad,
        fc2_bias_grad,
        freq_norm.reshape(()),
        rest_norm.reshape(()),
    )


def solution(mesh):
    rows = P(("dp", "tensor"), None, None)
    whole = P()
    hidden_in, hidden_out = P(None, "tensor"), P("tensor", None)
    return jax.shard_map(
        functools.partial(body, Exchange(mesh)),
        mesh=mesh,
        in_specs=(
            (rows, P(("dp", "tensor"), None))
            + (whole,) * 9
            + (hidden_in, P("tensor"), hidden_out, whole, rows)
        ),
        out_specs=(
            (rows, rows) + (whole,) * 9 + (hidden_in, P("tensor"), hidden_out) + (whole,) * 3
        ),
        check_vma=False,
    )
```
